256 devices in a mesh: section: 4 (over y), depth: 64 (over x, z, core).
Axes of the slice: x: 4, y: 4, z: 8, core: 2. Of those that a mesh axis runs over, the one named last changes fastest.
Arguments:
- alignment_input: bfloat16 [4, 2048, 32, 768], P('section', 'depth'), may hold values from -6 to 6
- target_slot: int32 [4, 2048], P('section', 'depth'), may hold values from -1 to 2047, as said below
- device_alignment: int32 [4, 64], P('section'), may hold values from 0 to 31, never falling along the last dimension, each value on 1 to 4 neighbouring positions
- layer_norm_gain: float32 [4, 768], P('section'), may hold values from 0.5 to 1.5
- layer_norm_bias: float32 [4, 768], P('section'), may hold values from -3 to 3
- query_key_value_weight: bfloat16 [4, 768, 2304], P('section'), may hold values from -1.25 to 1.25
- output_weight: bfloat16 [4, 768, 768], P('section'), may hold values from -0.21875 to 0.21875
Outputs:
- handed: bfloat16 [4, 2048, 32, 768], P('section', 'depth')
The draws below stay inside these ranges and needn't reach their ends.
Inputs may be any that keep to these rules, and one draw needn't show every extreme that they name: `target_slot`: within a section no slot is named twice. The input slots of one device map to 16 devices, 2 consecutive slots each, at offsets along depth that are the same for every device of the section; empty slots carry -1. Every device receives at least 2 rows, in every draw some device sends 2 live rows to one device and some device receives 32 rows. `device_alignment`: an alignment's devices are consecutive, at most 4 of them, and every alignment holds at least one device.
All inputs are finite; a program needn't handle non-finite values.
Results may differ from the reference program's by a relative error of at most 0.0065.
Values may be sent and summed in bfloat16 or wider, within the bound.
No kernel may reach another device: no remote copies, remote signals or barrier semaphores. Data moves between devices by JAX's collectives and lax.ppermute only.
A program may use at most 128 MiB of HBM per device.

```python
import math
import jax
import jax.numpy as jnp
import numpy as np
from jax import lax

EMBED_WIDTH = 768
H = 12
DH = 64
ROW_LENGTH = 32
ROW_SLOTS = 32
SPAN = 4
CAP = 2
GROUPS = 32
N_SECTION = 4
N_DEPTH = 64


def draw_target_slot(key, part):
    pair_total = ROW_SLOTS // CAP

    def one_section(section_key):
        offsets = jax.random.permutation(jax.random.fold_in(section_key, 1), N_DEPTH)[:pair_total]
        order_keys = jax.random.split(jax.random.fold_in(section_key, 2), N_DEPTH)
        orders = jax.vmap(lambda order_key: jax.random.permutation(order_key, pair_total))(order_keys)
        places = jax.random.permutation(jax.random.fold_in(section_key, 3), ROW_SLOTS)
        sender = jnp.arange(N_DEPTH, dtype=jnp.int32)[:, None]
        row_index = jnp.arange(ROW_SLOTS, dtype=jnp.int32)
        pair_index = jnp.take(orders, row_index // CAP, axis=1)
        target_dev = (sender + offsets[pair_index]) % N_DEPTH
        slot_index = places[pair_index * CAP + (row_index % CAP)[None, :]]
        coin_toss = jax.random.randint(jax.random.fold_in(section_key, 4), (N_DEPTH, ROW_SLOTS), 0, 8)
        full_dev = jax.random.randint(jax.random.fold_in(section_key, 5), (), 0, N_DEPTH)
        live_slot = (pair_index == 0) | (target_dev == full_dev) | (coin_toss < 7)
        return jnp.where(live_slot, target_dev * ROW_SLOTS + slot_index, -1).reshape(-1)
    section_keys = jax.random.split(jax.random.fold_in(key, 17), N_SECTION)
    return jax.vmap(one_section)(section_keys).astype(jnp.int32)


def draw_query_key_value_weight(key, part):
    shape = (N_SECTION, EMBED_WIDTH, 3 * EMBED_WIDTH)
    scale_in = EMBED_WIDTH ** (-0.5)
    base_draw = jnp.clip(jax.random.normal(jax.random.fold_in(key, 3), shape, jnp.float32), -6.0, 6.0) * scale_in
    base_draw = jnp.clip(base_draw, -1.25, 1.25)
    return base_draw.astype(jnp.bfloat16)


def block_scale(rng, dims, cuts, smallest, top_value):
    level, own = 1.0, jax.random.fold_in(rng, 6)
    for position, shards_of in cuts:
        heights = jnp.exp(jax.random.uniform(jax.random.fold_in(own, position), (shards_of,), jnp.float32, smallest / len(cuts), top_value / len(cuts)))
        level = level * jnp.repeat(heights, dims[position] // shards_of).reshape([-1 if axis == position else 1 for axis in range(len(dims))])
    return level


def length_profile(amount, total, limit, lean):
    portions = [(1 << 20) // math.isqrt(standing ** lean) + 1 for standing in range(2, amount + 1)]
    surplus, given = total - limit - (amount - 1), [1] * (amount - 1)
    while surplus > 0:
        movable = [i for i in range(amount - 1) if given[i] < limit]
        pool, left = sum([portions[i] for i in movable]), surplus
        for i in movable:
            addition = min(limit - given[i], max(1, left * portions[i] // pool), surplus)
            given[i] = given[i] + addition
            surplus = surplus - addition
    return np.array([limit] + given)


def ragged(key, count, total, bound, skew):
    if count == 2:
        one = jax.random.randint(key, (), max(1, total - bound), min(bound, total - 1) + 1)
        return jnp.stack([one, total - one])
    sizes = jnp.asarray(length_profile(count, total, bound, skew), jnp.int32)
    twos = (count - 1) // 2
    donor, taker = sizes[1:1 + 2 * twos:2], sizes[2:2 + 2 * twos:2]
    room = jnp.minimum(donor - 1, bound - taker)
    moved = jax.random.randint(jax.random.fold_in(key, 1), (twos,), 0, 1 << 20) % (room + 1)
    sizes = sizes.at[1:1 + 2 * twos:2].set(donor - moved).at[2:2 + 2 * twos:2].set(taker + moved)
    return sizes[jax.random.permutation(jax.random.fold_in(key, 2), count)]


def scatter_about(key, shape, deviation, reach, cuts=(), held_as=jnp.bfloat16):
    level = block_scale(key, shape, cuts, -0.22, 0.18) if cuts else 1.0
    drawn = jax.random.normal(key, shape, jnp.float32) * deviation * level
    return jnp.minimum(jnp.maximum(drawn, -reach), reach).astype(held_as)


def setup_inputs(seed: int = 0) -> dict:
    keys = jax.random.split(jax.random.key(seed), 8)
    alignment_input = scatter_about(keys[0], (N_SECTION, N_DEPTH * ROW_SLOTS, ROW_LENGTH, EMBED_WIDTH), 1.0, 6.0, ((0, 4), (1, 64)))
    target_slot = draw_target_slot(jax.random.fold_in(keys[7], 71), 0)
    device_alignment = jax.vmap(lambda own: jnp.searchsorted(jnp.cumsum(ragged(own, GROUPS, N_DEPTH, SPAN, 2)), jnp.arange(N_DEPTH), side="right"))(jax.random.split(keys[2], N_SECTION)).reshape((N_SECTION, N_DEPTH)).astype(jnp.int32)
    layer_norm_gain = jnp.clip(1.0 + 0.1 * jax.random.normal(keys[3], (N_SECTION, EMBED_WIDTH), jnp.float32), 0.5, 1.5)
    layer_norm_bias = scatter_about(keys[4], (N_SECTION, EMBED_WIDTH), 0.5, 3.0, ((0, 4),), jnp.float32)
    query_key_value_weight = draw_query_key_value_weight(jax.random.fold_in(keys[7], 71), 0)
    output_weight = scatter_about(keys[6], (N_SECTION, EMBED_WIDTH, EMBED_WIDTH), EMBED_WIDTH ** -0.5, 0.21875, ((0, 4),))
    return {"alignment_input": alignment_input, "target_slot": target_slot, "device_alignment": device_alignment, "layer_norm_gain": layer_norm_gain, "layer_norm_bias": layer_norm_bias, "query_key_value_weight": query_key_value_weight, "output_weight": output_weight}


EPSILON = 1e-05

def normalize(incoming_rows, gain_row, offset):
    widened = incoming_rows.astype(jnp.float32)
    average = lax.optimization_barrier(jnp.mean(widened, axis=-1, keepdims=True))
    centred = widened - average
    spread = lax.optimization_barrier(jnp.mean(centred * centred, axis=-1, keepdims=True))
    return (centred * lax.rsqrt(spread + EPSILON) * gain_row + offset).astype(jnp.bfloat16)

def section_layer_apply(incoming_rows, targets, groups, gain_row, offset, weight_qkv, weight_out):
    total_rows = N_DEPTH * ROW_SLOTS
    placed = jnp.where(targets >= 0, targets, total_rows)
    balanced = jnp.zeros((total_rows, ROW_LENGTH, EMBED_WIDTH), jnp.bfloat16).at[placed].set(incoming_rows, mode='drop')
    live_rows = jnp.zeros((total_rows,), jnp.float32).at[placed].set(1.0, mode='drop')
    shards = balanced.reshape(N_DEPTH, ROW_SLOTS, ROW_LENGTH, EMBED_WIDTH)
    shard_live = live_rows.reshape(N_DEPTH, ROW_SLOTS)

    def first_pass(pair_args):
        block_rows, alive_rows = pair_args
        normed = normalize(block_rows, gain_row, offset)
        packed = jnp.dot(normed.reshape(ROW_SLOTS * ROW_LENGTH, EMBED_WIDTH), weight_qkv, preferred_element_type=jnp.float32).astype(jnp.bfloat16)
        packed = packed.reshape(ROW_SLOTS, ROW_LENGTH, 3, H, DH)
        queries = packed[:, :, 0] * alive_rows.astype(jnp.bfloat16)[:, None, None, None]
        own_tied = jnp.einsum('mihd,mjhd->hij', queries.astype(jnp.float32), packed[:, :, 1].astype(jnp.float32))
        return (own_tied, jnp.sum(alive_rows), packed[:, :, 2])
    partials, counts, values = lax.map(first_pass, (shards, shard_live))
    group_tied = jax.ops.segment_sum(partials, groups, num_segments=GROUPS)
    group_depth = jax.ops.segment_sum(counts, groups, num_segments=GROUPS)
    factor = DH ** (-0.5) / jnp.sqrt(group_depth)
    logits = group_tied * factor[:, None, None, None]
    attention = jax.nn.softmax(logits, axis=-1).astype(jnp.bfloat16)
    shard_attention = attention[groups]

    def second_pass(quad_args):
        block_rows, alive_rows, value_block, weight_block = quad_args
        attended = jnp.einsum('hij,mjhd->mihd', weight_block.astype(jnp.float32), value_block.astype(jnp.float32)).astype(jnp.bfloat16)
        mixed_out = jnp.dot(attended.reshape(ROW_SLOTS * ROW_LENGTH, EMBED_WIDTH), weight_out, preferred_element_type=jnp.float32)
        mixed_out = mixed_out + block_rows.reshape(ROW_SLOTS * ROW_LENGTH, EMBED_WIDTH).astype(jnp.float32)
        mixed_out = mixed_out.reshape(ROW_SLOTS, ROW_LENGTH, EMBED_WIDTH) * alive_rows[:, None, None]
        return mixed_out.astype(jnp.bfloat16)
    layer_out = lax.map(second_pass, (shards, shard_live, values, shard_attention))
    return layer_out.reshape(total_rows, ROW_LENGTH, EMBED_WIDTH)

def reference(alignment_input, target_slot, device_alignment, layer_norm_gain, layer_norm_bias, query_key_value_weight, output_weight):
    section_outputs = []
    for section_index in range(N_SECTION):
        section_outputs.append(section_layer_apply(alignment_input[section_index], target_slot[section_index], device_alignment[section_index], layer_norm_gain[section_index], layer_norm_bias[section_index], query_key_value_weight[section_index], output_weight[section_index]))
    stacked = jnp.stack(section_outputs)
    return jnp.roll(stacked, 1, axis=0)
```

```python
import functools

import jax
import jax.numpy as jnp
from jax import lax
from jax.experimental import pallas as pl
from jax.experimental.pallas import tpu as pltpu
from jax.sharding import PartitionSpec as P

H = 12
DH = 64
SPAN = 4
PAIRS = H // 2
EPSILON = 1e-05
CHUNK_ROWS = 8
INTERPRET = False


def spread_kernel(slot_ref, rows_ref, out_ref, sem):
    count = rows_ref.shape[0]

    def copy_of(i):
        return pltpu.make_async_copy(
            rows_ref.at[i], out_ref.at[jnp.maximum(slot_ref[i], 0)], sem.at[i]
        )

    for i in range(count):

        @pl.when(slot_ref[i] >= 0)
        def _():
            copy_of(i).start()

    for i in range(count):

        @pl.when(slot_ref[i] >= 0)
        def _():
            copy_of(i).wait()


def spread(rows, slots, slot_count):
    return pl.pallas_call(
        spread_kernel,
        out_shape=jax.ShapeDtypeStruct((slot_count,) + rows.shape[1:], rows.dtype),
        in_specs=[
            pl.BlockSpec(memory_space=pltpu.SMEM),
            pl.BlockSpec(memory_space=pl.ANY),
        ],
        out_specs=pl.BlockSpec(memory_space=pl.ANY),
        scratch_shapes=[pltpu.SemaphoreType.DMA((rows.shape[0],))],
        interpret=INTERPRET,
    )(slots, rows)


def lane_mask(shape):
    return lax.broadcasted_iota(jnp.int32, shape, len(shape) - 1) % 128 < DH


def front_kernel(
    source_ref,
    rows_ref,
    gain_ref,
    bias_ref,
    weight_ref,
    balanced_ref,
    values_ref,
    tied_ref,
    tied_low_ref,
    landed,
    acc,
    sem,
):
    row_count = source_ref.shape[0]
    length, width = rows_ref.shape[1:]
    copies = [
        pltpu.make_async_copy(
            rows_ref.at[jnp.maximum(source_ref[m], 0)], landed.at[m], sem.at[m]
        )
        for m in range(row_count)
    ]
    for copy in copies:
        copy.start()
    gain = gain_ref[...]
    bias = bias_ref[...]
    weight = weight_ref[...]
    first = lane_mask((length, 256))
    for start in range(0, row_count, CHUNK_ROWS):
        members = range(start, start + CHUNK_ROWS)
        pieces = []
        for m in members:
            copies[m].wait()
            pieces.append(
                jnp.where(source_ref[m] >= 0, landed[m], jnp.zeros_like(landed[m]))
            )
        block = jnp.concatenate(pieces, axis=0)
        tokens = pl.ds(start * length, CHUNK_ROWS * length)
        balanced_ref[tokens, :] = block
        widened = block.astype(jnp.float32)
        average = jnp.mean(widened, axis=-1, keepdims=True)
        centred = widened - average
        spread_of = jnp.mean(centred * centred, axis=-1, keepdims=True)
        normed = (centred * lax.rsqrt(spread_of + EPSILON) * gain + bias).astype(jnp.bfloat16)
        packed = jnp.dot(normed, weight, preferred_element_type=jnp.float32).astype(jnp.bfloat16)
        values_ref[tokens, :] = packed[:, 2 * width :]
        for pair in range(PAIRS):
            lanes = slice(pair * 128, pair * 128 + 128)
            key_lanes = slice(width + pair * 128, width + pair * 128 + 128)
            total = None
            for r in range(0, CHUNK_ROWS, 2):
                query_parts = []
                key_parts = []
                for k in (r, r + 1):
                    own = slice(k * length, (k + 1) * length)
                    query = packed[own, lanes]
                    query_parts.append(
                        jnp.where(source_ref[start + k] >= 0, query, jnp.zeros_like(query))
                    )
                    key_parts.append(packed[own, key_lanes])
                query = jnp.concatenate(query_parts, axis=1)
                key = jnp.concatenate(key_parts, axis=1)
                zero = jnp.zeros_like(query)
                both = jnp.concatenate(
                    [jnp.where(first, query, zero), jnp.where(first, zero, query)], axis=0
                )
                part = lax.dot_general(
                    both, key, (((1,), (1,)), ((), ())), preferred_element_type=jnp.float32
                )
                total = part if total is None else total + part
            own = pl.ds(pair * 2 * length, 2 * length)
            if start == 0:
                acc[own, :] = total
            else:
                acc[own, :] += total
    quarter = H * length // 4
    tied = jnp.concatenate(
        [acc[pl.ds(q * quarter, quarter), :] for q in range(4)], axis=1
    )
    tied_ref[...] = tied
    tied_low_ref[...] = tied.astype(jnp.bfloat16)


def front(source, rows, gain, bias, weight):
    row_count = source.shape[0]
    length, width = rows.shape[1:]
    tokens = row_count * length
    quarter = H * length // 4
    vmem = pl.BlockSpec(memory_space=pltpu.VMEM)
    return pl.pallas_call(
        front_kernel,
        out_shape=(
            jax.ShapeDtypeStruct((tokens, width), jnp.bfloat16),
            jax.ShapeDtypeStruct((tokens, width), jnp.bfloat16),
            jax.ShapeDtypeStruct((quarter, 4 * length), jnp.float32),
            jax.ShapeDtypeStruct((quarter, 4 * length), jnp.bfloat16),
        ),
        in_specs=[
            pl.BlockSpec(memory_space=pltpu.SMEM),
            pl.BlockSpec(memory_space=pl.ANY),
            vmem,
            vmem,
            vmem,
        ],
        out_specs=(vmem, vmem, vmem, vmem),
        scratch_shapes=[
            pltpu.VMEM((row_count, length, width), jnp.bfloat16),
            pltpu.VMEM((H * length, length), jnp.float32),
            pltpu.SemaphoreType.DMA((row_count,)),
        ],
        compiler_params=pltpu.CompilerParams(vmem_limit_bytes=40 << 20),
        interpret=INTERPRET,
    )(source, rows, gain, bias, weight)


def attention_of(tied, scale, length):
    quarter = tied.shape[0]
    logits = (
        jnp.concatenate([tied[:, q * length : (q + 1) * length] for q in range(4)], axis=0) * scale
    )
    top = jnp.max(logits, axis=-1, keepdims=True)
    raised = jnp.exp(logits - top)
    return (raised / jnp.sum(raised, axis=-1, keepdims=True)).astype(jnp.bfloat16)


def back_kernel(
    source_ref,
    flag_ref,
    balanced_ref,
    values_ref,
    tied_ref,
    n1_ref,
    n2_ref,
    n3_ref,
    n4_ref,
    n5_ref,
    n6_ref,
    weight_ref,
    out_ref,
):
    row_count = source_ref.shape[0]
    length = out_ref.shape[0] // row_count
    width = out_ref.shape[1]
    tied = tied_ref[...]
    for place, ref in enumerate((n1_ref, n2_ref, n3_ref, n4_ref, n5_ref, n6_ref)):
        tied = tied + jnp.where(flag_ref[place] > 0, ref[...].astype(jnp.float32), 0.0)
    attention = attention_of(tied, flag_ref[6], length)
    span = CHUNK_ROWS * length
    wide = jnp.concatenate([attention] * CHUNK_ROWS, axis=1)
    diagonal = (
        lax.broadcasted_iota(jnp.int32, (span, span), 0) // length
        == lax.broadcasted_iota(jnp.int32, (span, span), 1) // length
    )
    first = lane_mask((span, 128))
    mixers = []
    for h in range(H):
        tall = jnp.concatenate([wide[h * length : (h + 1) * length]] * CHUNK_ROWS, axis=0)
        mixers.append(jnp.where(diagonal, tall, jnp.zeros_like(tall)))
    weight = weight_ref[...]
    for start in range(0, row_count, CHUNK_ROWS):
        tokens = pl.ds(start * length, span)
        values = values_ref[tokens, :]
        parts = []
        for pair in range(PAIRS):
            lanes = values[:, pair * 128 : pair * 128 + 128]
            low = jnp.dot(mixers[2 * pair], lanes, preferred_element_type=jnp.float32)
            high = jnp.dot(mixers[2 * pair + 1], lanes, preferred_element_type=jnp.float32)
            parts.append(jnp.where(first, low, high).astype(jnp.bfloat16))
        attended = jnp.concatenate(parts, axis=1)
        mixed = jnp.dot(attended, weight, preferred_element_type=jnp.float32)
        mixed = (mixed + balanced_ref[tokens, :].astype(jnp.float32)).astype(jnp.bfloat16)
        for k in range(CHUNK_ROWS):
            own = mixed[k * length : (k + 1) * length]
            out_ref[pl.ds((start + k) * length, length), :] = jnp.where(
                source_ref[start + k] >= 0, own, jnp.zeros_like(own)
            )


def back(source, flags, balanced, values, tied, neighbours, weight):
    vmem = pl.BlockSpec(memory_space=pltpu.VMEM)
    smem = pl.BlockSpec(memory_space=pltpu.SMEM)
    return pl.pallas_call(
        back_kernel,
        out_shape=jax.ShapeDtypeStruct(balanced.shape, jnp.bfloat16),
        in_specs=[smem, smem] + [vmem] * 10,
        out_specs=vmem,
        compiler_params=pltpu.CompilerParams(vmem_limit_bytes=40 << 20),
        interpret=INTERPRET,
    )(source, flags, balanced, values, tied, *neighbours, weight)


def shifted(value, axis, steps, wrap):
    count = lax.axis_size(axis)
    if wrap:
        route = [(i, (i + steps) % count) for i in range(count)]
    else:
        route = [(i, i + steps) for i in range(count) if 0 <= i + steps < count]
    return lax.ppermute(value, axis, route)


def body(
    alignment_input,
    target_slot,
    device_alignment,
    layer_norm_gain,
    layer_norm_bias,
    query_key_value_weight,
    output_weight,
):
    incoming = alignment_input[0]
    targets = target_slot[0]
    groups = device_alignment[0]
    row_count, length, width = incoming.shape
    peers = lax.axis_size("depth")
    position = lax.axis_index("depth")
    capacity = max(2, (row_count + peers - 1) // peers)
    slots = jnp.where(
        targets >= 0,
        targets // row_count * capacity + jnp.arange(row_count) % capacity,
        -1,
    )
    outgoing = spread(incoming, slots, peers * capacity)
    got = lax.all_to_all(
        outgoing.reshape((peers, capacity, length, width)),
        "depth",
        split_axis=0,
        concat_axis=0,
        tiled=True,
    ).reshape(peers * capacity, length, width)
    everywhere = lax.all_to_all(
        jnp.broadcast_to(targets[None], (peers, row_count)),
        "depth",
        split_axis=0,
        concat_axis=0,
        tiled=True,
    )
    local = everywhere - position * row_count
    mine = jnp.logical_and(local >= 0, local < row_count)
    code = (
        lax.broadcasted_iota(jnp.int32, (peers, row_count), 0) * capacity
        + lax.broadcasted_iota(jnp.int32, (peers, row_count), 1) % capacity
    )
    wanted = jnp.where(mine, local, -1).reshape(1, -1)
    hit = jnp.arange(row_count)[:, None] == wanted
    source = jnp.max(jnp.where(hit, code.reshape(1, -1), -1), axis=1)
    own_group = groups[position]
    low = jnp.sum((groups < own_group).astype(jnp.int32))
    high = low + jnp.sum((groups == own_group).astype(jnp.int32))
    inside = jnp.logical_and(everywhere >= low * row_count, everywhere < high * row_count)
    depth_total = jnp.sum(inside.astype(jnp.float32))
    balanced, values, tied, tied_low = front(
        source, got, layer_norm_gain, layer_norm_bias, query_key_value_weight[0]
    )
    steps = [d for k in range(1, SPAN) for d in (k, -k)]
    neighbours = [shifted(tied_low, "depth", d, False) for d in steps]
    flags = [
        jnp.logical_and(position - d >= low, position - d < high).astype(jnp.float32)
        for d in steps
    ]
    flags = jnp.stack(flags + [DH ** (-0.5) / jnp.sqrt(depth_total)])
    layer_out = back(source, flags, balanced, values, tied, neighbours, output_weight[0])
    return shifted(layer_out.reshape(1, row_count, length, width), "section", 1, True)


def solution(mesh):
    placed = (
        P("section", "depth", None, None),
        P("section", "depth"),
        P("section", None),
        P("section", None),
        P("section", None),
        P("section", None, None),
        P("section", None, None),
    )
    return jax.shard_map(
        body,
        mesh=mesh,
        in_specs=placed,
        out_specs=P("section", "depth", None, None),
        check_vma=False,
    )
```

```python
import jax
import jax.numpy as jnp
from jax import lax
from jax.experimental import pallas as pl
from jax.experimental.pallas import tpu as pltpu
from jax.sharding import PartitionSpec as P


H = 12
DH = 64
SPAN = 4
PAIRS = H // 2
EPSILON = 1e-05
CHUNK_ROWS = 8
INTERPRET = False


def spread_kernel(slot_ref, rows_ref, out_ref, sem):
    count = rows_ref.shape[0]

    def copy_of(i):
        return pltpu.make_async_copy(
            rows_ref.at[i], out_ref.at[jnp.maximum(slot_ref[i], 0)], sem.at[i]
        )

    for i in range(count):

        @pl.when(slot_ref[i] >= 0)
        def _():
            copy_of(i).start()

    for i in range(count):

        @pl.when(slot_ref[i] >= 0)
        def _():
            copy_of(i).wait()


def spread(rows, slots, slot_count):
    return pl.pallas_call(
        spread_kernel,
        out_shape=jax.ShapeDtypeStruct((slot_count,) + rows.shape[1:], rows.dtype),
        in_specs=[
            pl.BlockSpec(memory_space=pltpu.SMEM),
            pl.BlockSpec(memory_space=pltpu.VMEM),
        ],
        out_specs=pl.BlockSpec(memory_space=pl.ANY),
        scratch_shapes=[pltpu.SemaphoreType.DMA((rows.shape[0],))],
        name="spread",
        interpret=INTERPRET,
    )(slots, rows)


def settle_kernel(source_ref, rows_ref, *refs):
    out_ref, landed, in_sem, out_sem = refs[-4:]
    row_count, length = landed.shape[:2]

    def arrival(m):
        return pltpu.make_async_copy(
            rows_ref.at[jnp.maximum(source_ref[m], 0)], landed.at[m], in_sem.at[m]
        )

    def leaving(m):
        return pltpu.make_async_copy(
            landed.at[m], out_ref.at[pl.ds(m * length, length), :], out_sem.at[m]
        )

    for m in range(row_count):
        arrival(m).start()
    for m in range(row_count):
        arrival(m).wait()

        @pl.when(source_ref[m] < 0)
        def _():
            landed[m] = jnp.zeros_like(landed[m])

        leaving(m).start()
    for m in range(row_count):
        leaving(m).wait()


def settle(source, rows, scalars, early):
    row_count = source.shape[0]
    length, width = rows.shape[1:]
    return pl.pallas_call(
        settle_kernel,
        out_shape=jax.ShapeDtypeStruct((row_count * length, width), rows.dtype),
        in_specs=[
            pl.BlockSpec(memory_space=pltpu.SMEM),
            pl.BlockSpec(memory_space=pl.ANY),
        ]
        + [pl.BlockSpec(memory_space=pltpu.SMEM)] * len(scalars)
        + [pl.BlockSpec(memory_space=pl.ANY)] * len(early),
        out_specs=pl.BlockSpec(memory_space=pl.ANY),
        scratch_shapes=[
            pltpu.VMEM((row_count, length, width), rows.dtype),
            pltpu.SemaphoreType.DMA((row_count,)),
            pltpu.SemaphoreType.DMA((row_count,)),
        ],
        name="settle",
        interpret=INTERPRET,
    )(source, rows, *scalars, *early)


def lane_mask(shape):
    return lax.broadcasted_iota(jnp.int32, shape, len(shape) - 1) % 128 < DH


def normalized(block, gain, bias):
    widened = block.astype(jnp.float32)
    average = jnp.mean(widened, axis=-1, keepdims=True)
    centred = widened - average
    spread_of = jnp.mean(centred * centred, axis=-1, keepdims=True)
    return (centred * lax.rsqrt(spread_of + EPSILON) * gain + bias).astype(jnp.bfloat16)


def front_kernel(
    source_ref,
    meta_ref,
    scale_ref,
    rows_ref,
    gain_ref,
    bias_ref,
    weight_ref,
    tied_ref,
    tied_low_ref,
    landed,
    acc,
    sem,
):
    row_count = source_ref.shape[0]
    width = rows_ref.shape[1]
    length = rows_ref.shape[0] // row_count
    span = CHUNK_ROWS * length
    chunks = row_count // CHUNK_ROWS
    copies = [
        pltpu.make_async_copy(rows_ref.at[pl.ds(c * span, span), :], landed.at[c], sem.at[c])
        for c in range(chunks)
    ]
    for copy in copies:
        copy.start()
    gain = gain_ref[...]
    bias = bias_ref[...]
    weight = weight_ref[:, : 2 * width]
    first = lane_mask((length, 256))
    for c in range(chunks):
        copies[c].wait()
        start = c * CHUNK_ROWS
        normed = normalized(landed[c], gain, bias)
        packed = jnp.dot(normed, weight, preferred_element_type=jnp.float32).astype(jnp.bfloat16)
        for pair in range(PAIRS):
            lanes = slice(pair * 128, pair * 128 + 128)
            key_lanes = slice(width + pair * 128, width + pair * 128 + 128)
            total = None
            for r in range(0, CHUNK_ROWS, 2):
                query_parts = []
                key_parts = []
                for k in (r, r + 1):
                    own = slice(k * length, (k + 1) * length)
                    query = packed[own, lanes]
                    query_parts.append(
                        jnp.where(source_ref[start + k] >= 0, query, jnp.zeros_like(query))
                    )
                    key_parts.append(packed[own, key_lanes])
                query = jnp.concatenate(query_parts, axis=1)
                key = jnp.concatenate(key_parts, axis=1)
                zero = jnp.zeros_like(query)
                both = jnp.concatenate(
                    [jnp.where(first, query, zero), jnp.where(first, zero, query)], axis=0
                )
                part = lax.dot_general(
                    both, key, (((1,), (1,)), ((), ())), preferred_element_type=jnp.float32
                )
                total = part if total is None else total + part
            own = pl.ds(pair * 2 * length, 2 * length)
            if c == 0:
                acc[own, :] = total
            else:
                acc[own, :] += total
    quarter = H * length // 4
    tied = jnp.concatenate([acc[pl.ds(q * quarter, quarter), :] for q in range(4)], axis=1)
    tied_ref[...] = tied
    tied_low_ref[...] = tied.astype(jnp.bfloat16)


def front(source, meta, scale, rows, gain, bias, weight):
    row_count = source.shape[0]
    width = rows.shape[1]
    length = rows.shape[0] // row_count
    quarter = H * length // 4
    vmem = pl.BlockSpec(memory_space=pltpu.VMEM)
    smem = pl.BlockSpec(memory_space=pltpu.SMEM)
    return pl.pallas_call(
        front_kernel,
        out_shape=(
            jax.ShapeDtypeStruct((quarter, 4 * length), jnp.float32),
            jax.ShapeDtypeStruct((quarter, 4 * length), jnp.bfloat16),
        ),
        in_specs=[smem, smem, smem, pl.BlockSpec(memory_space=pl.ANY), vmem, vmem, vmem],
        out_specs=(vmem, vmem),
        scratch_shapes=[
            pltpu.VMEM((row_count // CHUNK_ROWS, CHUNK_ROWS * length, width), jnp.bfloat16),
            pltpu.VMEM((H * length, length), jnp.float32),
            pltpu.SemaphoreType.DMA((row_count // CHUNK_ROWS,)),
        ],
        compiler_params=pltpu.CompilerParams(vmem_limit_bytes=40 << 20),
        name="front",
        interpret=INTERPRET,
    )(source, meta, scale, rows, gain, bias, weight)


STEPS = tuple(d for k in range(1, SPAN) for d in (k, -k))


def middle_kernel(source_ref, meta_ref, scale_ref, tied_ref, *refs):
    neighbours, out_ref = refs[:-1], refs[-1]
    length = source_ref.shape[0]
    tied = tied_ref[...]
    position, low, high = meta_ref[0], meta_ref[1], meta_ref[2]
    for d, ref in zip(STEPS, neighbours):
        member = jnp.logical_and(position - d >= low, position - d < high)
        tied = tied + jnp.where(member, ref[...].astype(jnp.float32), 0.0)
    quarter = tied.shape[0]
    scale = scale_ref[0]
    logits = (
        jnp.concatenate([tied[:, q * length : (q + 1) * length] for q in range(4)], axis=0) * scale
    )
    top = jnp.max(logits, axis=-1, keepdims=True)
    raised = jnp.exp(logits - top)
    attention = raised / jnp.sum(raised, axis=-1, keepdims=True)
    out_ref[pl.ds(0, quarter), :] = jnp.concatenate(
        [attention[q * quarter : (q + 1) * quarter] for q in range(4)], axis=1
    ).astype(jnp.bfloat16)
    lane = lax.broadcasted_iota(jnp.int32, (16, 4 * length), 1)
    live = jnp.zeros((16, 4 * length), jnp.float32)
    for m in range(source_ref.shape[0]):
        live = jnp.where(jnp.logical_and(lane == m, source_ref[m] >= 0), 1.0, live)
    out_ref[pl.ds(quarter, 16), :] = live.astype(jnp.bfloat16)


def middle(source, meta, scale, tied, neighbours):
    vmem = pl.BlockSpec(memory_space=pltpu.VMEM)
    smem = pl.BlockSpec(memory_space=pltpu.SMEM)
    return pl.pallas_call(
        middle_kernel,
        out_shape=jax.ShapeDtypeStruct((tied.shape[0] + 16, tied.shape[1]), jnp.bfloat16),
        in_specs=[smem, smem, smem] + [vmem] * (1 + len(neighbours)),
        out_specs=vmem,
        name="middle",
        interpret=INTERPRET,
    )(source, meta, scale, tied, *neighbours)


def back_kernel(
    attention_ref, rows_ref, affine_ref, value_weight_ref, weight_ref, out_ref, landed, ready,
    in_sem, out_sem,
):
    chunks = landed.shape[0]
    span, _ = landed.shape[1:]
    length = span // CHUNK_ROWS
    quarter = H * length // 4
    arrivals = [
        pltpu.make_async_copy(rows_ref.at[pl.ds(c * span, span), :], landed.at[c], in_sem.at[c])
        for c in range(chunks)
    ]
    leavings = [
        pltpu.make_async_copy(ready.at[c], out_ref.at[pl.ds(c * span, span), :], out_sem.at[c])
        for c in range(chunks)
    ]
    for copy in arrivals:
        copy.start()
    packed = attention_ref[pl.ds(0, quarter), :]
    attention = jnp.concatenate(
        [packed[:, q * length : (q + 1) * length] for q in range(4)], axis=0
    )
    live = attention_ref[pl.ds(quarter, 16), :].astype(jnp.float32)
    wide = jnp.concatenate([attention] * CHUNK_ROWS, axis=1)
    diagonal = (
        lax.broadcasted_iota(jnp.int32, (span, span), 0) // length
        == lax.broadcasted_iota(jnp.int32, (span, span), 1) // length
    )
    first = lane_mask((span, 128))
    mixers = []
    for h in range(H):
        tall = jnp.concatenate([wide[h * length : (h + 1) * length]] * CHUNK_ROWS, axis=0)
        mixers.append(jnp.where(diagonal, tall, jnp.zeros_like(tall)))
    gain = affine_ref[0:1, :]
    bias = affine_ref[1:2, :]
    value_weight = value_weight_ref[...]
    weight = weight_ref[...]
    for c in range(chunks):
        arrivals[c].wait()
        block = landed[c]
        values = jnp.dot(
            normalized(block, gain, bias), value_weight, preferred_element_type=jnp.float32
        ).astype(jnp.bfloat16)
        parts = []
        for pair in range(PAIRS):
            lanes = values[:, pair * 128 : pair * 128 + 128]
            low = jnp.dot(mixers[2 * pair], lanes, preferred_element_type=jnp.float32)
            high = jnp.dot(mixers[2 * pair + 1], lanes, preferred_element_type=jnp.float32)
            parts.append(jnp.where(first, low, high).astype(jnp.bfloat16))
        attended = jnp.concatenate(parts, axis=1)
        mixed = jnp.dot(attended, weight, preferred_element_type=jnp.float32)
        mixed = mixed + block.astype(jnp.float32)
        for k in range(CHUNK_ROWS):
            m = c * CHUNK_ROWS + k
            own = mixed[k * length : (k + 1) * length]
            ready[c, pl.ds(k * length, length), :] = (
                own * jnp.broadcast_to(live[0:1, m : m + 1], own.shape)
            ).astype(jnp.bfloat16)
        leavings[c].start()
    for copy in leavings:
        copy.wait()


def back(attention, rows, affine, value_weight, weight, row_count):
    vmem = pl.BlockSpec(memory_space=pltpu.VMEM)
    anywhere = pl.BlockSpec(memory_space=pl.ANY)
    width = rows.shape[1]
    chunks = row_count // CHUNK_ROWS
    span = rows.shape[0] // chunks
    return pl.pallas_call(
        back_kernel,
        out_shape=jax.ShapeDtypeStruct(rows.shape, jnp.bfloat16),
        in_specs=[vmem, anywhere, vmem, vmem, vmem],
        out_specs=anywhere,
        scratch_shapes=[
            pltpu.VMEM((chunks, span, width), jnp.bfloat16),
            pltpu.VMEM((chunks, span, width), jnp.bfloat16),
            pltpu.SemaphoreType.DMA((chunks,)),
            pltpu.SemaphoreType.DMA((chunks,)),
        ],
        compiler_params=pltpu.CompilerParams(vmem_limit_bytes=40 << 20),
        name="back",
        interpret=INTERPRET,
    )(attention, rows, affine, value_weight, weight)


def shifted(value, axis, steps, wrap):
    count = lax.axis_size(axis)
    if wrap:
        route = [(i, (i + steps) % count) for i in range(count)]
    else:
        route = [(i, i + steps) for i in range(count) if 0 <= i + steps < count]
    return lax.ppermute(value, axis, route)


def layer(
    alignment_input,
    target_slot,
    device_alignment,
    layer_norm_gain,
    layer_norm_bias,
    query_key_value_weight,
    output_weight,
):
    incoming = alignment_input[0]
    targets = target_slot[0]
    groups = device_alignment[0]
    row_count, length, width = incoming.shape
    peers = lax.axis_size("depth")
    position = lax.axis_index("depth")
    capacity = max(2, (row_count + peers - 1) // peers)
    slots = jnp.where(
        targets >= 0,
        targets // row_count * capacity + jnp.arange(row_count) % capacity,
        -1,
    )
    outgoing = spread(incoming, slots, peers * capacity)
    got = lax.all_to_all(
        outgoing.reshape((peers, capacity, length, width)),
        "depth",
        split_axis=0,
        concat_axis=0,
        tiled=True,
    ).reshape(peers * capacity, length, width)
    everywhere = targets.reshape(1, row_count)
    while everywhere.shape[0] < peers:
        held = everywhere.shape[0]
        passed = shifted(everywhere[: peers - held], "depth", held, True)
        everywhere = jnp.concatenate([everywhere, passed], axis=0)
    value_weight = shifted(query_key_value_weight[0, :, 2 * width :], "section", 1, True)
    out_weight = shifted(output_weight[0], "section", 1, True)
    affine = shifted(
        jnp.concatenate([layer_norm_gain, layer_norm_bias], axis=0), "section", 1, True
    )
    local = everywhere - position * row_count
    mine = jnp.logical_and(local >= 0, local < row_count)
    sender = (position - lax.broadcasted_iota(jnp.int32, (peers, row_count), 0)) % peers
    code = (
        sender * capacity
        + lax.broadcasted_iota(jnp.int32, (peers, row_count), 1) % capacity
    )
    wanted = jnp.where(mine, local, -1).reshape(1, -1)
    hit = jnp.arange(row_count)[:, None] == wanted
    source = jnp.max(jnp.where(hit, code.reshape(1, -1), -1), axis=1)
    own_group = groups[position]
    low = jnp.sum((groups < own_group).astype(jnp.int32))
    high = low + jnp.sum((groups == own_group).astype(jnp.int32))
    inside = jnp.logical_and(everywhere >= low * row_count, everywhere < high * row_count)
    depth_total = jnp.sum(inside.astype(jnp.float32))
    meta = jnp.stack([position, low, high])
    scale = (DH ** (-0.5) / jnp.sqrt(depth_total)).reshape(1)
    balanced = settle(source, got, (meta, scale), (value_weight, out_weight, affine))
    earlier = shifted(balanced, "section", 1, True)
    tied, tied_low = front(
        source,
        meta,
        scale,
        balanced,
        layer_norm_gain,
        layer_norm_bias,
        query_key_value_weight[0],
    )
    neighbours = [shifted(tied_low, "depth", d, False) for d in STEPS]
    attention = shifted(middle(source, meta, scale, tied, neighbours), "section", 1, True)
    handed = back(attention, earlier, affine, value_weight, out_weight, row_count)
    return handed.reshape(1, row_count, length, width)


def solution(mesh):
    placed = (
        P("section", "depth", None, None),
        P("section", "depth"),
        P("section", None),
        P("section", None),
        P("section", None),
        P("section", None, None),
        P("section", None, None),
    )
    return jax.shard_map(
        layer,
        mesh=mesh,
        in_specs=placed,
        out_specs=P("section", "depth", None, None),
        check_vma=False,
    )
```

```python
import jax
import jax.numpy as jnp
from jax import lax
from jax.experimental import pallas as pl
from jax.experimental.pallas import tpu as pltpu
from jax.sharding import PartitionSpec as P


H = 12
DH = 64
SPAN = 4
PAIRS = H // 2
EPSILON = 1e-05
CHUNK_ROWS = 8
INTERPRET = False


def spread_kernel(slot_ref, rows_ref, out_ref, sem):
    count = rows_ref.shape[0]

    def copy_of(i):
        return pltpu.make_async_copy(
            rows_ref.at[i], out_ref.at[jnp.maximum(slot_ref[i], 0)], sem.at[i]
        )

    for i in range(count):

        @pl.when(slot_ref[i] >= 0)
        def _():
            copy_of(i).start()

    for i in range(count):

        @pl.when(slot_ref[i] >= 0)
        def _():
            copy_of(i).wait()


def spread(rows, slots, slot_count):
    return pl.pallas_call(
        spread_kernel,
        out_shape=jax.ShapeDtypeStruct((slot_count,) + rows.shape[1:], rows.dtype),
        in_specs=[
            pl.BlockSpec(memory_space=pltpu.SMEM),
            pl.BlockSpec(memory_space=pltpu.VMEM),
        ],
        out_specs=pl.BlockSpec(memory_space=pltpu.HBM),
        scratch_shapes=[pltpu.SemaphoreType.DMA((rows.shape[0],))],
        name="spread",
        interpret=INTERPRET,
    )(slots, rows)


def settle_kernel(source_ref, rows_ref, *refs):
    out_ref, landed, in_sem, out_sem = refs[-4:]
    row_count, length = landed.shape[:2]

    def arrival(m):
        return pltpu.make_async_copy(
            rows_ref.at[jnp.maximum(source_ref[m], 0)], landed.at[m], in_sem.at[m]
        )

    def leaving(m):
        return pltpu.make_async_copy(
            landed.at[m], out_ref.at[pl.ds(m * length, length), :], out_sem.at[m]
        )

    for m in range(row_count):
        arrival(m).start()
    for m in range(row_count):
        arrival(m).wait()

        @pl.when(source_ref[m] < 0)
        def _():
            landed[m] = jnp.zeros_like(landed[m])

        leaving(m).start()
    for m in range(row_count):
        leaving(m).wait()


def settle(source, rows, scalars, early):
    row_count = source.shape[0]
    length, width = rows.shape[1:]
    return pl.pallas_call(
        settle_kernel,
        out_shape=jax.ShapeDtypeStruct((row_count * length, width), rows.dtype),
        in_specs=[
            pl.BlockSpec(memory_space=pltpu.SMEM),
            pl.BlockSpec(memory_space=pl.ANY),
        ]
        + [pl.BlockSpec(memory_space=pltpu.SMEM)] * len(scalars)
        + [pl.BlockSpec(memory_space=pl.ANY)] * len(early),
        out_specs=pl.BlockSpec(memory_space=pltpu.HBM),
        scratch_shapes=[
            pltpu.VMEM((row_count, length, width), rows.dtype),
            pltpu.SemaphoreType.DMA((row_count,)),
            pltpu.SemaphoreType.DMA((row_count,)),
        ],
        name="settle",
        interpret=INTERPRET,
    )(source, rows, *scalars, *early)


def lane_mask(shape):
    return lax.broadcasted_iota(jnp.int32, shape, len(shape) - 1) % 128 < DH


def normalized(block, gain, bias):
    widened = block.astype(jnp.float32)
    average = jnp.mean(widened, axis=-1, keepdims=True)
    centred = widened - average
    spread_of = jnp.mean(centred * centred, axis=-1, keepdims=True)
    return (centred * lax.rsqrt(spread_of + EPSILON) * gain + bias).astype(jnp.bfloat16)


def front_kernel(
    source_ref,
    meta_ref,
    scale_ref,
    rows_ref,
    gain_ref,
    bias_ref,
    weight_ref,
    tied_ref,
    tied_low_ref,
    landed,
    acc,
    sem,
):
    row_count = source_ref.shape[0]
    width = rows_ref.shape[1]
    length = rows_ref.shape[0] // row_count
    span = CHUNK_ROWS * length
    chunks = row_count // CHUNK_ROWS
    copies = [
        pltpu.make_async_copy(rows_ref.at[pl.ds(c * span, span), :], landed.at[c], sem.at[c])
        for c in range(chunks)
    ]
    for copy in copies:
        copy.start()
    gain = gain_ref[...]
    bias = bias_ref[...]
    weight = weight_ref[:, : 2 * width]
    first = lane_mask((length, 256))
    for c in range(chunks):
        copies[c].wait()
        start = c * CHUNK_ROWS
        normed = normalized(landed[c], gain, bias)
        packed = jnp.dot(normed, weight, preferred_element_type=jnp.float32).astype(jnp.bfloat16)
        for pair in range(PAIRS):
            lanes = slice(pair * 128, pair * 128 + 128)
            key_lanes = slice(width + pair * 128, width + pair * 128 + 128)
            total = None
            for r in range(0, CHUNK_ROWS, 2):
                query_parts = []
                key_parts = []
                for k in (r, r + 1):
                    own = slice(k * length, (k + 1) * length)
                    query = packed[own, lanes]
                    query_parts.append(
                        jnp.where(source_ref[start + k] >= 0, query, jnp.zeros_like(query))
                    )
                    key_parts.append(packed[own, key_lanes])
                query = jnp.concatenate(query_parts, axis=1)
                key = jnp.concatenate(key_parts, axis=1)
                zero = jnp.zeros_like(query)
                both = jnp.concatenate(
                    [jnp.where(first, query, zero), jnp.where(first, zero, query)], axis=0
                )
                part = lax.dot_general(
                    both, key, (((1,), (1,)), ((), ())), preferred_element_type=jnp.float32
                )
                total = part if total is None else total + part
            own = pl.ds(pair * 2 * length, 2 * length)
            if c == 0:
                acc[own, :] = total
            else:
                acc[own, :] += total
    quarter = H * length // 4
    tied = jnp.concatenate([acc[pl.ds(q * quarter, quarter), :] for q in range(4)], axis=1)
    tied_ref[...] = tied
    tied_low_ref[...] = tied.astype(jnp.bfloat16)


def front(source, meta, scale, rows, gain, bias, weight):
    row_count = source.shape[0]
    width = rows.shape[1]
    length = rows.shape[0] // row_count
    quarter = H * length // 4
    vmem = pl.BlockSpec(memory_space=pltpu.VMEM)
    smem = pl.BlockSpec(memory_space=pltpu.SMEM)
    return pl.pallas_call(
        front_kernel,
        out_shape=(
            jax.ShapeDtypeStruct((quarter, 4 * length), jnp.float32),
            jax.ShapeDtypeStruct((quarter, 4 * length), jnp.bfloat16),
        ),
        in_specs=[smem, smem, smem, pl.BlockSpec(memory_space=pltpu.HBM), vmem, vmem, vmem],
        out_specs=(vmem, vmem),
        scratch_shapes=[
            pltpu.VMEM((row_count // CHUNK_ROWS, CHUNK_ROWS * length, width), jnp.bfloat16),
            pltpu.VMEM((H * length, length), jnp.float32),
            pltpu.SemaphoreType.DMA((row_count // CHUNK_ROWS,)),
        ],
        compiler_params=pltpu.CompilerParams(vmem_limit_bytes=40 << 20),
        name="front",
        interpret=INTERPRET,
    )(source, meta, scale, rows, gain, bias, weight)


STEPS = tuple(d for k in range(1, SPAN) for d in (k, -k))


def middle_kernel(source_ref, meta_ref, scale_ref, tied_ref, *refs):
    neighbours, out_ref = refs[:-1], refs[-1]
    length = source_ref.shape[0]
    tied = tied_ref[...]
    position, low, high = meta_ref[0], meta_ref[1], meta_ref[2]
    for d, ref in zip(STEPS, neighbours):
        member = jnp.logical_and(position - d >= low, position - d < high)
        tied = tied + jnp.where(member, ref[...].astype(jnp.float32), 0.0)
    quarter = tied.shape[0]
    scale = scale_ref[0]
    logits = (
        jnp.concatenate([tied[:, q * length : (q + 1) * length] for q in range(4)], axis=0) * scale
    )
    top = jnp.max(logits, axis=-1, keepdims=True)
    raised = jnp.exp(logits - top)
    attention = raised / jnp.sum(raised, axis=-1, keepdims=True)
    out_ref[pl.ds(0, quarter), :] = jnp.concatenate(
        [attention[q * quarter : (q + 1) * quarter] for q in range(4)], axis=1
    ).astype(jnp.bfloat16)
    lane = lax.broadcasted_iota(jnp.int32, (16, 4 * length), 1)
    live = jnp.zeros((16, 4 * length), jnp.float32)
    for m in range(source_ref.shape[0]):
        live = jnp.where(jnp.logical_and(lane == m, source_ref[m] >= 0), 1.0, live)
    out_ref[pl.ds(quarter, 16), :] = live.astype(jnp.bfloat16)


def middle(source, meta, scale, tied, neighbours):
    vmem = pl.BlockSpec(memory_space=pltpu.VMEM)
    smem = pl.BlockSpec(memory_space=pltpu.SMEM)
    return pl.pallas_call(
        middle_kernel,
        out_shape=jax.ShapeDtypeStruct((tied.shape[0] + 16, tied.shape[1]), jnp.bfloat16),
        in_specs=[smem, smem, smem] + [vmem] * (1 + len(neighbours)),
        out_specs=vmem,
        name="middle",
        interpret=INTERPRET,
    )(source, meta, scale, tied, *neighbours)


def back_kernel(
    attention_ref, rows_ref, affine_ref, value_weight_ref, weight_ref, out_ref, landed, ready,
    in_sem, out_sem,
):
    chunks = landed.shape[0]
    span, _ = landed.shape[1:]
    length = span // CHUNK_ROWS
    quarter = H * length // 4
    arrivals = [
        pltpu.make_async_copy(rows_ref.at[pl.ds(c * span, span), :], landed.at[c], in_sem.at[c])
        for c in range(chunks)
    ]
    leavings = [
        pltpu.make_async_copy(ready.at[c], out_ref.at[pl.ds(c * span, span), :], out_sem.at[c])
        for c in range(chunks)
    ]
    for copy in arrivals:
        copy.start()
    packed = attention_ref[pl.ds(0, quarter), :]
    attention = jnp.concatenate(
        [packed[:, q * length : (q + 1) * length] for q in range(4)], axis=0
    )
    live = attention_ref[pl.ds(quarter, 16), :].astype(jnp.float32)
    wide = jnp.concatenate([attention] * CHUNK_ROWS, axis=1)
    diagonal = (
        lax.broadcasted_iota(jnp.int32, (span, span), 0) // length
        == lax.broadcasted_iota(jnp.int32, (span, span), 1) // length
    )
    first = lane_mask((span, 128))
    mixers = []
    for h in range(H):
        tall = jnp.concatenate([wide[h * length : (h + 1) * length]] * CHUNK_ROWS, axis=0)
        mixers.append(jnp.where(diagonal, tall, jnp.zeros_like(tall)))
    gain = affine_ref[0:1, :]
    bias = affine_ref[1:2, :]
    value_weight = value_weight_ref[...]
    weight = weight_ref[...]
    for c in range(chunks):
        arrivals[c].wait()
        block = landed[c]
        values = jnp.dot(
            normalized(block, gain, bias), value_weight, preferred_element_type=jnp.float32
        ).astype(jnp.bfloat16)
        parts = []
        for pair in range(PAIRS):
            lanes = values[:, pair * 128 : pair * 128 + 128]
            low = jnp.dot(mixers[2 * pair], lanes, preferred_element_type=jnp.float32)
            high = jnp.dot(mixers[2 * pair + 1], lanes, preferred_element_type=jnp.float32)
            parts.append(jnp.where(first, low, high).astype(jnp.bfloat16))
        attended = jnp.concatenate(parts, axis=1)
        mixed = jnp.dot(attended, weight, preferred_element_type=jnp.float32)
        mixed = mixed + block.astype(jnp.float32)
        for k in range(CHUNK_ROWS):
            m = c * CHUNK_ROWS + k
            own = mixed[k * length : (k + 1) * length]
            ready[c, pl.ds(k * length, length), :] = (
                own * jnp.broadcast_to(live[0:1, m : m + 1], own.shape)
            ).astype(jnp.bfloat16)
        leavings[c].start()
    for copy in leavings:
        copy.wait()


def back(attention, rows, affine, value_weight, weight, row_count):
    vmem = pl.BlockSpec(memory_space=pltpu.VMEM)
    anywhere = pl.BlockSpec(memory_space=pltpu.HBM)
    width = rows.shape[1]
    chunks = row_count // CHUNK_ROWS
    span = rows.shape[0] // chunks
    return pl.pallas_call(
        back_kernel,
        out_shape=jax.ShapeDtypeStruct(rows.shape, jnp.bfloat16),
        in_specs=[vmem, anywhere, vmem, vmem, vmem],
        out_specs=anywhere,
        scratch_shapes=[
            pltpu.VMEM((chunks, span, width), jnp.bfloat16),
            pltpu.VMEM((chunks, span, width), jnp.bfloat16),
            pltpu.SemaphoreType.DMA((chunks,)),
            pltpu.SemaphoreType.DMA((chunks,)),
        ],
        compiler_params=pltpu.CompilerParams(vmem_limit_bytes=40 << 20),
        name="back",
        interpret=INTERPRET,
    )(attention, rows, affine, value_weight, weight)


def shifted(value, axis, steps, wrap):
    count = lax.axis_size(axis)
    if wrap:
        route = [(i, (i + steps) % count) for i in range(count)]
    else:
        route = [(i, i + steps) for i in range(count) if 0 <= i + steps < count]
    return lax.ppermute(value, axis, route)


def layer(
    alignment_input,
    target_slot,
    device_alignment,
    layer_norm_gain,
    layer_norm_bias,
    query_key_value_weight,
    output_weight,
):
    incoming = alignment_input[0]
    targets = target_slot[0]
    groups = device_alignment[0]
    row_count, length, width = incoming.shape
    peers = lax.axis_size("depth")
    position = lax.axis_index("depth")
    capacity = max(2, (row_count + peers - 1) // peers)
    slots = jnp.where(
        targets >= 0,
        targets // row_count * capacity + jnp.arange(row_count) % capacity,
        -1,
    )
    outgoing = spread(incoming, slots, peers * capacity)
    got = lax.all_to_all(
        outgoing.reshape((peers, capacity, length, width)),
        "depth",
        split_axis=0,
        concat_axis=0,
        tiled=True,
    ).reshape(peers * capacity, length, width)
    everywhere = lax.all_to_all(
        jnp.broadcast_to(targets[None, None], (peers, 1, row_count)),
        "depth",
        split_axis=0,
        concat_axis=0,
        tiled=True,
    ).reshape(peers, row_count)
    value_weight = shifted(query_key_value_weight[0, :, 2 * width :], "section", 1, True)
    out_weight = shifted(output_weight[0], "section", 1, True)
    affine = shifted(
        jnp.concatenate([layer_norm_gain, layer_norm_bias], axis=0), "section", 1, True
    )
    local = everywhere - position * row_count
    mine = jnp.logical_and(local >= 0, local < row_count)
    sender = lax.broadcasted_iota(jnp.int32, (peers, row_count), 0)
    code = (
        sender * capacity
        + lax.broadcasted_iota(jnp.int32, (peers, row_count), 1) % capacity
    )
    wanted = jnp.where(mine, local, -1).reshape(1, -1)
    hit = jnp.arange(row_count)[:, None] == wanted
    source = jnp.max(jnp.where(hit, code.reshape(1, -1), -1), axis=1)
    own_group = groups[position]
    low = jnp.sum((groups < own_group).astype(jnp.int32))
    high = low + jnp.sum((groups == own_group).astype(jnp.int32))
    inside = jnp.logical_and(everywhere >= low * row_count, everywhere < high * row_count)
    depth_total = jnp.sum(inside.astype(jnp.float32))
    meta = jnp.stack([position, low, high])
    scale = (DH ** (-0.5) / jnp.sqrt(depth_total)).reshape(1)
    balanced = settle(source, got, (meta, scale), (value_weight, out_weight, affine))
    earlier = shifted(balanced, "section", 1, True)
    tied, tied_low = front(
        source,
        meta,
        scale,
        balanced,
        layer_norm_gain,
        layer_norm_bias,
        query_key_value_weight[0],
    )
    neighbours = [shifted(tied_low, "depth", d, False) for d in STEPS]
    attention = shifted(middle(source, meta, scale, tied, neighbours), "section", 1, True)
    handed = back(attention, earlier, affine, value_weight, out_weight, row_count)
    return handed.reshape(1, row_count, length, width)


def solution(mesh):
    placed = (
        P("section", "depth", None, None),
        P("section", "depth"),
        P("section", None),
        P("section", None),
        P("section", None),
        P("section", None, None),
        P("section", None, None),
    )
    return jax.shard_map(
        layer,
        mesh=mesh,
        in_specs=placed,
        out_specs=P("section", "depth", None, None),
        check_vma=False,
    )
```

```python
import functools

import jax
import jax.numpy as jnp
from jax import lax
from jax.experimental import pallas as pl
from jax.experimental.pallas import tpu as pltpu
from jax.sharding import PartitionSpec as P


H = 12
DH = 64
SPAN = 4
PAIRS = H // 2
EPSILON = 1e-05
CHUNK_ROWS = 8
INTERPRET = False


def spread_kernel(slot_ref, rows_ref, out_ref, sem):
    count = rows_ref.shape[0]

    def copy_of(i):
        return pltpu.make_async_copy(
            rows_ref.at[i], out_ref.at[jnp.maximum(slot_ref[i], 0)], sem.at[i]
        )

    for i in range(count):

        @pl.when(slot_ref[i] >= 0)
        def _():
            copy_of(i).start()

    for i in range(count):

        @pl.when(slot_ref[i] >= 0)
        def _():
            copy_of(i).wait()


def spread(rows, slots, slot_count):
    return pl.pallas_call(
        spread_kernel,
        out_shape=jax.ShapeDtypeStruct((slot_count,) + rows.shape[1:], rows.dtype),
        in_specs=[
            pl.BlockSpec(memory_space=pltpu.SMEM),
            pl.BlockSpec(memory_space=pltpu.VMEM),
        ],
        out_specs=pl.BlockSpec(memory_space=pltpu.HBM),
        scratch_shapes=[pltpu.SemaphoreType.DMA((rows.shape[0],))],
        name="spread",
        interpret=INTERPRET,
    )(slots, rows)


def settle_kernel(source_ref, rows_ref, out_ref, landed, in_sem, out_sem):
    row_count, _ = landed.shape[:2]

    def arrival(m):
        return pltpu.make_async_copy(
            rows_ref.at[jnp.maximum(source_ref[m], 0)], landed.at[m], in_sem.at[m]
        )

    def leaving(m):
        return pltpu.make_async_copy(landed.at[m], out_ref.at[m], out_sem.at[m])

    for m in range(row_count):
        arrival(m).start()
    for m in range(row_count):
        arrival(m).wait()

        @pl.when(source_ref[m] < 0)
        def _():
            landed[m] = jnp.zeros_like(landed[m])

        leaving(m).start()
    for m in range(row_count):
        leaving(m).wait()


def settle(source, rows):
    row_count = source.shape[0]
    length, width = rows.shape[1:]
    return pl.pallas_call(
        settle_kernel,
        out_shape=jax.ShapeDtypeStruct((row_count, length, width), rows.dtype),
        in_specs=[
            pl.BlockSpec(memory_space=pltpu.SMEM),
            pl.BlockSpec(memory_space=pl.ANY),
        ],
        out_specs=pl.BlockSpec(memory_space=pltpu.HBM),
        scratch_shapes=[
            pltpu.VMEM((row_count, length, width), rows.dtype),
            pltpu.SemaphoreType.DMA((row_count,)),
            pltpu.SemaphoreType.DMA((row_count,)),
        ],
        name="settle",
        interpret=INTERPRET,
    )(source, rows)


def lane_mask(shape):
    return lax.broadcasted_iota(jnp.int32, shape, len(shape) - 1) % 128 < DH


def normalized(block, gain, bias):
    widened = block.astype(jnp.float32)
    average = jnp.mean(widened, axis=-1, keepdims=True)
    centred = widened - average
    spread_of = jnp.mean(centred * centred, axis=-1, keepdims=True)
    return (centred * lax.rsqrt(spread_of + EPSILON) * gain + bias).astype(jnp.bfloat16)


def front_kernel(
    live_ref,
    rows_ref,
    gain_ref,
    bias_ref,
    weight_ref,
    tied_ref,
    tied_low_ref,
    landed,
    acc,
    sem,
):
    row_count = live_ref.shape[0]
    width = rows_ref.shape[1]
    length = rows_ref.shape[0] // row_count
    span = CHUNK_ROWS * length
    chunks = row_count // CHUNK_ROWS
    copies = [
        pltpu.make_async_copy(rows_ref.at[pl.ds(c * span, span), :], landed.at[c], sem.at[c])
        for c in range(chunks)
    ]
    for copy in copies:
        copy.start()
    gain = gain_ref[...]
    bias = bias_ref[...]
    weight = weight_ref[:, : 2 * width]
    first = lane_mask((length, 256))
    for c in range(chunks):
        copies[c].wait()
        start = c * CHUNK_ROWS
        normed = normalized(landed[c], gain, bias)
        packed = jnp.dot(normed, weight, preferred_element_type=jnp.float32).astype(jnp.bfloat16)
        for pair in range(PAIRS):
            lanes = slice(pair * 128, pair * 128 + 128)
            key_lanes = slice(width + pair * 128, width + pair * 128 + 128)
            total = None
            for r in range(0, CHUNK_ROWS, 2):
                query_parts = []
                key_parts = []
                for k in (r, r + 1):
                    own = slice(k * length, (k + 1) * length)
                    query = packed[own, lanes]
                    query_parts.append(
                        jnp.where(live_ref[start + k] > 0, query, jnp.zeros_like(query))
                    )
                    key_parts.append(packed[own, key_lanes])
                query = jnp.concatenate(query_parts, axis=1)
                key = jnp.concatenate(key_parts, axis=1)
                zero = jnp.zeros_like(query)
                both = jnp.concatenate(
                    [jnp.where(first, query, zero), jnp.where(first, zero, query)], axis=0
                )
                part = lax.dot_general(
                    both, key, (((1,), (1,)), ((), ())), preferred_element_type=jnp.float32
                )
                total = part if total is None else total + part
            own = pl.ds(pair * 2 * length, 2 * length)
            if c == 0:
                acc[own, :] = total
            else:
                acc[own, :] += total
    quarter = H * length // 4
    tied = jnp.concatenate([acc[pl.ds(q * quarter, quarter), :] for q in range(4)], axis=1)
    tied_ref[...] = tied
    tied_low_ref[...] = tied.astype(jnp.bfloat16)


def front(live, rows, gain, bias, weight):
    row_count = live.shape[0]
    width = rows.shape[1]
    length = rows.shape[0] // row_count
    quarter = H * length // 4
    vmem = pl.BlockSpec(memory_space=pltpu.VMEM)
    smem = pl.BlockSpec(memory_space=pltpu.SMEM)
    return pl.pallas_call(
        front_kernel,
        out_shape=(
            jax.ShapeDtypeStruct((quarter, 4 * length), jnp.float32),
            jax.ShapeDtypeStruct((quarter, 4 * length), jnp.bfloat16),
        ),
        in_specs=[smem, pl.BlockSpec(memory_space=pltpu.HBM), vmem, vmem, vmem],
        out_specs=(vmem, vmem),
        scratch_shapes=[
            pltpu.VMEM((row_count // CHUNK_ROWS, CHUNK_ROWS * length, width), jnp.bfloat16),
            pltpu.VMEM((H * length, length), jnp.float32),
            pltpu.SemaphoreType.DMA((row_count // CHUNK_ROWS,)),
        ],
        compiler_params=pltpu.CompilerParams(vmem_limit_bytes=40 << 20),
        name="front",
        interpret=INTERPRET,
    )(live, rows, gain, bias, weight)


STEPS = tuple(d for k in range(1, SPAN) for d in (k, -k))


def middle_kernel(live_ref, meta_ref, tied_ref, *refs):
    neighbours, out_ref = refs[:-1], refs[-1]
    length = tied_ref.shape[1] // 4
    tied = tied_ref[...]
    position, low, high = meta_ref[0], meta_ref[1], meta_ref[2]
    for d, ref in zip(STEPS, neighbours):
        member = jnp.logical_and(position - d >= low, position - d < high)
        tied = tied + jnp.where(member, ref[...].astype(jnp.float32), 0.0)
    quarter = tied.shape[0]
    count = jnp.full((1, length), meta_ref[3], jnp.int32).astype(jnp.float32)
    scale = DH ** (-0.5) / jnp.sqrt(count)
    logits = (
        jnp.concatenate([tied[:, q * length : (q + 1) * length] for q in range(4)], axis=0) * scale
    )
    top = jnp.max(logits, axis=-1, keepdims=True)
    raised = jnp.exp(logits - top)
    attention = raised / jnp.sum(raised, axis=-1, keepdims=True)
    out_ref[pl.ds(0, quarter), :] = jnp.concatenate(
        [attention[q * quarter : (q + 1) * quarter] for q in range(4)], axis=1
    ).astype(jnp.bfloat16)
    lane = lax.broadcasted_iota(jnp.int32, (16, 4 * length), 1)
    live = jnp.zeros((16, 4 * length), jnp.float32)
    for m in range(live_ref.shape[0]):
        live = jnp.where(jnp.logical_and(lane == m, live_ref[m] > 0), 1.0, live)
    out_ref[pl.ds(quarter, 16), :] = live.astype(jnp.bfloat16)


def middle(live, meta, tied, neighbours):
    vmem = pl.BlockSpec(memory_space=pltpu.VMEM)
    smem = pl.BlockSpec(memory_space=pltpu.SMEM)
    return pl.pallas_call(
        middle_kernel,
        out_shape=jax.ShapeDtypeStruct((tied.shape[0] + 16, tied.shape[1]), jnp.bfloat16),
        in_specs=[smem, smem] + [vmem] * (1 + len(neighbours)),
        out_specs=vmem,
        name="middle",
        interpret=INTERPRET,
    )(live, meta, tied, *neighbours)


def back_kernel(
    attention_ref, rows_ref, affine_ref, value_weight_ref, weight_ref, out_ref, landed, ready,
    in_sem, out_sem,
):
    chunks = landed.shape[0]
    span, _ = landed.shape[1:]
    length = span // CHUNK_ROWS
    quarter = H * length // 4
    arrivals = [
        pltpu.make_async_copy(rows_ref.at[pl.ds(c * span, span), :], landed.at[c], in_sem.at[c])
        for c in range(chunks)
    ]
    leavings = [
        pltpu.make_async_copy(ready.at[c], out_ref.at[pl.ds(c * span, span), :], out_sem.at[c])
        for c in range(chunks)
    ]
    for copy in arrivals:
        copy.start()
    packed = attention_ref[pl.ds(0, quarter), :]
    attention = jnp.concatenate(
        [packed[:, q * length : (q + 1) * length] for q in range(4)], axis=0
    )
    live = attention_ref[pl.ds(quarter, 16), :].astype(jnp.float32)
    wide = jnp.concatenate([attention] * CHUNK_ROWS, axis=1)
    diagonal = (
        lax.broadcasted_iota(jnp.int32, (span, span), 0) // length
        == lax.broadcasted_iota(jnp.int32, (span, span), 1) // length
    )
    first = lane_mask((span, 128))
    mixers = []
    for h in range(H):
        tall = jnp.concatenate([wide[h * length : (h + 1) * length]] * CHUNK_ROWS, axis=0)
        mixers.append(jnp.where(diagonal, tall, jnp.zeros_like(tall)))
    gain = affine_ref[0:1, :]
    bias = affine_ref[1:2, :]
    value_weight = value_weight_ref[...]
    weight = weight_ref[...]
    for c in range(chunks):
        arrivals[c].wait()
        block = landed[c]
        values = jnp.dot(
            normalized(block, gain, bias), value_weight, preferred_element_type=jnp.float32
        ).astype(jnp.bfloat16)
        parts = []
        for pair in range(PAIRS):
            lanes = values[:, pair * 128 : pair * 128 + 128]
            low = jnp.dot(mixers[2 * pair], lanes, preferred_element_type=jnp.float32)
            high = jnp.dot(mixers[2 * pair + 1], lanes, preferred_element_type=jnp.float32)
            parts.append(jnp.where(first, low, high).astype(jnp.bfloat16))
        attended = jnp.concatenate(parts, axis=1)
        mixed = jnp.dot(attended, weight, preferred_element_type=jnp.float32)
        mixed = mixed + block.astype(jnp.float32)
        for k in range(CHUNK_ROWS):
            m = c * CHUNK_ROWS + k
            own = mixed[k * length : (k + 1) * length]
            ready[c, pl.ds(k * length, length), :] = (
                own * jnp.broadcast_to(live[0:1, m : m + 1], own.shape)
            ).astype(jnp.bfloat16)
        leavings[c].start()
    for copy in leavings:
        copy.wait()


def back(attention, rows, affine, value_weight, weight, row_count):
    vmem = pl.BlockSpec(memory_space=pltpu.VMEM)
    anywhere = pl.BlockSpec(memory_space=pltpu.HBM)
    width = rows.shape[1]
    chunks = row_count // CHUNK_ROWS
    span = rows.shape[0] // chunks
    return pl.pallas_call(
        back_kernel,
        out_shape=jax.ShapeDtypeStruct(rows.shape, jnp.bfloat16),
        in_specs=[vmem, anywhere, vmem, vmem, vmem],
        out_specs=anywhere,
        scratch_shapes=[
            pltpu.VMEM((chunks, span, width), jnp.bfloat16),
            pltpu.VMEM((chunks, span, width), jnp.bfloat16),
            pltpu.SemaphoreType.DMA((chunks,)),
            pltpu.SemaphoreType.DMA((chunks,)),
        ],
        compiler_params=pltpu.CompilerParams(vmem_limit_bytes=40 << 20),
        name="back",
        interpret=INTERPRET,
    )(attention, rows, affine, value_weight, weight)


def shifted(value, axis, steps, wrap):
    count = lax.axis_size(axis)
    if wrap:
        route = [(i, (i + steps) % count) for i in range(count)]
    else:
        route = [(i, i + steps) for i in range(count) if 0 <= i + steps < count]
    return lax.ppermute(value, axis, route)


ROUTE = ((11, 9, 7, 4), (10, 6), 12)
Z_STAY = 8
RING_Z = 8
RING_X = 4


def plan_kernel(position_ref, groups_ref, targets_ref, table_ref, meta_ref):
    peers, row_count = targets_ref.shape
    pair_count = row_count // 2
    position = position_ref[0]
    shape = (peers, 128)
    down = lax.broadcasted_iota(jnp.int32, shape, 0)
    across = lax.broadcasted_iota(jnp.int32, shape, 1)
    zero = jnp.zeros(shape, jnp.int32)

    def over_lanes(value):
        return jnp.broadcast_to(jnp.sum(value, axis=1, keepdims=True), shape)

    def over_rows(value):
        return jnp.broadcast_to(jnp.sum(value, axis=0, keepdims=True), shape)

    def top_rows(value):
        return jnp.max(value, axis=0, keepdims=True)

    def flag(condition):
        return jnp.where(condition, 1, zero)

    def to_lanes(value):
        return over_rows(jnp.where(down == across, value, zero))

    def to_rows(value):
        return over_lanes(jnp.where(down == across, value, zero))

    targets = jnp.concatenate(
        [targets_ref[...], jnp.full((peers, 128 - row_count), -1, jnp.int32)], axis=1
    )
    device = targets >> 5
    offset = jnp.where(targets >= 0, (device - down) & (peers - 1), -1)
    seen = zero
    for i in range(row_count):
        seen = seen | flag(jnp.broadcast_to(offset[:, i : i + 1], shape) == across)
    present_l = flag(over_rows(seen) > 0)
    present = to_rows(present_l)
    odd = down & 1
    odd_l = across & 1

    def turns(core):
        step = ((down + odd * (1 - 2 * core)) >> 1) & 31
        step_l = ((across + odd_l * (1 - 2 * core)) >> 1) & 31
        u, u_l = step & 7, step_l & 7
        order = u * 64 + down
        order_l = u_l * 64 + across
        moving = present * flag(u > 0)
        moving_l = present_l * flag(u_l > 0)
        rank = over_lanes(moving_l * flag(order_l < order))
        rest = over_lanes((present_l - moving_l) * flag(order_l < order))
        return step >> 3, u, moving, rank, rest

    def split_of(core, route):
        caps, _, _ = route
        _, u, moving, rank, _ = turns(core)
        early = moving * flag(rank < across)
        late = moving - early
        good = flag(across <= pair_count)
        for h in range(1, 6):
            cap = caps[h - 1] if h <= len(caps) else 0
            good = good * flag(over_rows(early * flag(u >= h)) <= cap)
            good = good * flag(over_rows(late * flag(RING_Z - u >= h)) <= cap)
        split = jnp.min(jnp.where(good > 0, across, 127), axis=1, keepdims=True)
        return jnp.broadcast_to(split, shape)

    def lanes_of(core, split, route):
        (z1, z2, z3, z4), (x1, x2), x_stay = route
        high, u, moving, rank, rest = turns(core)
        plus = moving * flag(rank < split)
        minus = moving - plus
        staying = present - moving
        hops = jnp.where(plus > 0, u, RING_Z - u)
        place = jnp.where(plus > 0, split - 1 - rank, rank - split)
        base = jnp.where(
            hops == 1,
            zero,
            jnp.where(hops == 2, z1 + zero, jnp.where(hops == 3, z1 + z2 + zero, z1 + z2 + z3)),
        )
        side = jnp.where(minus > 0, 1, zero)
        z_leave = jnp.where(staying > 0, 2 * z1 + rest, side * z1 + place)
        z_all = z1 + z2 + z3 + z4
        z_land = jnp.where(staying > 0, 2 * z_all + rest, side * z_all + base + place)
        turn = (high + minus) & (RING_X - 1)
        turn = jnp.where(present > 0, turn, -1)
        turn_l = to_lanes(turn)
        level = over_lanes(present_l * flag(turn_l == turn) * flag(across < down))
        count = [over_rows(flag(turn == v)) for v in range(RING_X)]
        ahead = (count[2] + count[3] - count[1] + 1) >> 1
        ahead = jnp.minimum(
            jnp.maximum(ahead, jnp.maximum(count[2] - x2, 0)), jnp.minimum(count[2], x2)
        )
        behind = count[2] - ahead
        good = (
            flag(ahead <= x2)
            * flag(behind <= x2)
            * flag(ahead + count[1] <= x1)
            * flag(behind + count[3] <= x1)
            * flag(count[0] <= x_stay)
            * flag(split <= pair_count)
        )
        double = flag(turn == 2)
        forward = flag(turn == 1) + double * flag(level < ahead)
        spot = jnp.where(
            double > 0,
            jnp.where(level < ahead, level, level - ahead),
            level + jnp.where(turn == 1, ahead, behind),
        )
        back_side = 1 - forward
        x_leave = jnp.where(turn == 0, 2 * x1 + level, back_side * x1 + spot)
        x_land = jnp.where(
            turn == 0, 2 * (x1 + x2) + level, back_side * (x1 + x2) + double * x1 + spot
        )
        gone = -1 + zero
        return (
            jnp.max(good),
            jnp.where(present > 0, z_leave, gone),
            jnp.where(present > 0, z_land, gone),
            jnp.where(present > 0, x_leave, gone),
            jnp.where(present > 0, x_land, gone),
        )

    core = position & 1
    split = split_of(core, ROUTE)
    own_good, z_leave, z_land, x_leave, x_land = lanes_of(core, split, ROUTE)
    other_good = lanes_of(1 - core, split_of(1 - core, ROUTE), ROUTE)[0]

    lane_row = lax.broadcasted_iota(jnp.int32, (1, 128), 1)
    origin = -1 + zero
    for b in range(2):
        sender = position if b == 0 else position ^ 1
        mine = targets_ref[pl.ds(sender, 1), :]
        mine = jnp.concatenate([mine, jnp.full((1, 128 - row_count), -1, jnp.int32)], axis=1)
        away = ((mine >> 5) - sender) & (peers - 1)
        away = jnp.where(mine >= 0, away, -1)
        away = jnp.where((away & 1) == b, away, -1)
        hit = jnp.broadcast_to(away, shape) == down
        code = b * pair_count + (jnp.broadcast_to(lane_row, shape) >> 1)
        found = jnp.max(jnp.where(hit, code, -1), axis=1, keepdims=True)
        origin = jnp.maximum(origin, jnp.broadcast_to(found, shape))

    def gathered(slot_of, value):
        return top_rows(jnp.where(slot_of == across, value, -1))

    local = targets - position * row_count
    here = jnp.logical_and(local >= 0, local < row_count)
    settled_a = jnp.full((1, 128), -1, jnp.int32)
    settled_b = settled_a
    lane_full = across & 1
    for r in range(2):
        slot = jnp.max(
            jnp.where(jnp.logical_and(here, lane_full == r), local, -1), axis=1, keepdims=True
        )
        slot = jnp.broadcast_to(slot, shape)
        slot_l = over_rows(jnp.where(down == across, slot + 1, zero)) - 1
        match = across == ((position - down) & (peers - 1))
        slot_by_offset = over_lanes(jnp.where(match, slot_l + 1, zero)) - 1
        settled_a = jnp.maximum(settled_a, gathered(slot_by_offset, x_land * 2 + r))
        settled_b = jnp.maximum(settled_b, gathered(slot_by_offset, z_land * 2 + r))
    empty = jnp.full((1, 128), -1, jnp.int32)
    table_ref[...] = jnp.concatenate(
        [
            gathered(z_leave, origin),
            gathered(x_leave, origin),
            gathered(x_leave, z_land),
            gathered(z_leave, x_land),
            settled_a,
            settled_b,
            empty,
            empty,
        ],
        axis=0,
    )
    groups = groups_ref[...]
    lane = lax.broadcasted_iota(jnp.int32, groups.shape, 1)
    own_group = jnp.sum(jnp.where(lane == position, groups, 0))
    low = jnp.sum(jnp.where(groups < own_group, 1, 0))
    high = low + jnp.sum(jnp.where(groups == own_group, 1, 0))
    inside = jnp.logical_and(targets >= low * row_count, targets < high * row_count)
    meta_ref[0] = position
    meta_ref[1] = low
    meta_ref[2] = high
    meta_ref[3] = jnp.sum(jnp.where(inside, 1, 0))
    meta_ref[4] = own_good * other_good


def plan(position, groups, targets):
    vmem = pl.BlockSpec(memory_space=pltpu.VMEM)
    smem = pl.BlockSpec(memory_space=pltpu.SMEM)
    return pl.pallas_call(
        plan_kernel,
        out_shape=(
            jax.ShapeDtypeStruct((8, 128), jnp.int32),
            jax.ShapeDtypeStruct((8,), jnp.int32),
        ),
        in_specs=[smem, vmem, vmem],
        out_specs=(vmem, smem),
        name="plan",
        interpret=INTERPRET,
    )(position.reshape(1), groups, targets)


def deal(table_ref, row, pool, outs):
    lane = 0
    for out in outs:

        def step(k, carry, out=out, lane=lane):
            out[k] = pool[jnp.maximum(table_ref[row, lane + k], 0)]
            return carry

        lax.fori_loop(0, out.shape[0], step, 0)
        lane += out.shape[0]


def leave_kernel(table_ref, own_ref, partner_ref, *refs):
    outs, (pool, sem) = refs[:-2], refs[-2:]
    pairs = own_ref.shape[0]
    half = own_ref.shape[2] // 2
    copies = []
    for part in range(2):
        for b, ref in enumerate((own_ref, partner_ref)):
            copies.append(
                pltpu.make_async_copy(
                    ref.at[:, :, pl.ds(part * half, half), :],
                    pool.at[part, pl.ds(b * pairs, pairs)],
                    sem.at[len(copies)],
                )
            )
    for copy in copies:
        copy.start()
    for part in range(2):
        copies[2 * part].wait()
        copies[2 * part + 1].wait()
        deal(table_ref, part, pool.at[part], outs[3 * part : 3 * part + 3])


def leave(table, own, partner, route):
    (z1, _, _, _), (x1, _), x_stay = route
    pairs, two, length, width = own.shape
    vmem = pl.BlockSpec(memory_space=pltpu.VMEM)
    anywhere = pl.BlockSpec(memory_space=pl.ANY)
    sizes = (z1, z1, Z_STAY, x1, x1, x_stay)
    return pl.pallas_call(
        leave_kernel,
        out_shape=tuple(
            jax.ShapeDtypeStruct((n, two, length // 2, width), own.dtype) for n in sizes
        ),
        in_specs=[pl.BlockSpec(memory_space=pltpu.SMEM), anywhere, anywhere],
        out_specs=(vmem,) * len(sizes),
        scratch_shapes=[
            pltpu.VMEM((2, 2 * pairs, two, length // 2, width), own.dtype),
            pltpu.SemaphoreType.DMA((4,)),
        ],
        compiler_params=pltpu.CompilerParams(vmem_limit_bytes=40 << 20),
        name="leave",
        interpret=INTERPRET,
    )(table, own, partner)


def pooled(refs, pool, sem):
    copies = []
    start = 0
    for ref in refs:
        count = ref.shape[0]
        copies.append(
            pltpu.make_async_copy(ref, pool.at[pl.ds(start, count)], sem.at[len(copies)])
        )
        start += count
    return copies


def turn_kernel(row, count, table_ref, *refs):
    sources, outs, (pool, sem) = refs[:count], refs[count:-2], refs[-2:]
    copies = pooled(sources, pool, sem)
    for copy in copies:
        copy.start()
    for copy in copies:
        copy.wait()
    deal(table_ref, row, pool, outs)


def turn_over(table, row, sources, sizes):
    vmem = pl.BlockSpec(memory_space=pltpu.VMEM)
    anywhere = pl.BlockSpec(memory_space=pl.ANY)
    payload = sources[0].shape[1:]
    return pl.pallas_call(
        functools.partial(turn_kernel, row, len(sources)),
        out_shape=tuple(jax.ShapeDtypeStruct((n,) + payload, sources[0].dtype) for n in sizes),
        in_specs=[pl.BlockSpec(memory_space=pltpu.SMEM)] + [anywhere] * len(sources),
        out_specs=(vmem,) * len(sizes),
        scratch_shapes=[
            pltpu.VMEM((sum(s.shape[0] for s in sources),) + payload, sources[0].dtype),
            pltpu.SemaphoreType.DMA((len(sources),)),
        ],
        compiler_params=pltpu.CompilerParams(vmem_limit_bytes=40 << 20),
        name="turn_over",
        interpret=INTERPRET,
    )(table, *sources)


def land_kernel(count_a, count_b, table_ref, *refs):
    sources_a, sources_b = refs[:count_a], refs[count_a : count_a + count_b]
    out_ref, live_ref, pool_a, pool_b, done, sem_a, sem_b, out_sem = refs[count_a + count_b :]
    row_count, length, _ = done.shape
    half = length // 2
    copies = pooled(sources_a, pool_a, sem_a) + pooled(sources_b, pool_b, sem_b)
    for copy in copies:
        copy.start()
    for copy in copies:
        copy.wait()

    def step(m, carry):
        live = table_ref[4, m] >= 0
        live_ref[m] = jnp.where(live, 1, 0)
        for part, pool in ((0, pool_a), (1, pool_b)):
            code = jnp.maximum(table_ref[4 + part, m], 0)
            value = pool[code >> 1, code & 1]
            done[m, pl.ds(part * half, half), :] = jnp.where(live, value, jnp.zeros_like(value))
        return carry

    lax.fori_loop(0, row_count, step, 0)
    copy = pltpu.make_async_copy(done, out_ref, out_sem)
    copy.start()
    copy.wait()


def land(table, sources_a, sources_b, row_count, length):
    anywhere = pl.BlockSpec(memory_space=pl.ANY)
    smem = pl.BlockSpec(memory_space=pltpu.SMEM)
    two, half, width = sources_a[0].shape[1:]
    dtype = sources_a[0].dtype
    return pl.pallas_call(
        functools.partial(land_kernel, len(sources_a), len(sources_b)),
        out_shape=(
            jax.ShapeDtypeStruct((row_count, length, width), dtype),
            jax.ShapeDtypeStruct((row_count,), jnp.int32),
        ),
        in_specs=[smem] + [anywhere] * (len(sources_a) + len(sources_b)),
        out_specs=(pl.BlockSpec(memory_space=pltpu.HBM), smem),
        scratch_shapes=[
            pltpu.VMEM((sum(s.shape[0] for s in sources_a), two, half, width), dtype),
            pltpu.VMEM((sum(s.shape[0] for s in sources_b), two, half, width), dtype),
            pltpu.VMEM((row_count, length, width), dtype),
            pltpu.SemaphoreType.DMA((len(sources_a),)),
            pltpu.SemaphoreType.DMA((len(sources_b),)),
            pltpu.SemaphoreType.DMA,
        ],
        compiler_params=pltpu.CompilerParams(vmem_limit_bytes=40 << 20),
        name="land",
        interpret=INTERPRET,
    )(table, *sources_a, *sources_b)


def chain(forward, backward, caps, step):
    onward, returning = [], []
    for cap in caps:
        forward = shifted(forward[:cap], "depth", step, True)
        backward = shifted(backward[:cap], "depth", -step, True)
        onward.append(forward)
        returning.append(backward)
    return onward + returning


def routed(route, table, own, partner):
    z_caps, x_caps, x_stay = route
    z_sizes = (z_caps[0], z_caps[0], Z_STAY)
    x_sizes = (x_caps[0], x_caps[0], x_stay)
    z_plus, z_minus, z_still, x_plus, x_minus, x_still = leave(table, own, partner, route)
    along_x = chain(x_plus, x_minus, x_caps, 2 * RING_Z)
    along_z = chain(z_plus, z_minus, z_caps, 2)
    later = turn_over(table, 3, along_x + [x_still], z_sizes)
    last_b = chain(later[0], later[1], z_caps, 2)
    turned = turn_over(table, 2, along_z + [z_still], x_sizes)
    last_a = chain(turned[0], turned[1], x_caps, 2 * RING_Z)
    return land(
        table,
        last_a + [turned[2]],
        last_b + [later[2]],
        own.shape[0] * own.shape[1],
        own.shape[2],
    )


def dense(targets, everywhere, own):
    row_count = targets.shape[0]
    _, _, length, width = own.shape
    peers = lax.axis_size("depth")
    position = lax.axis_index("depth")
    capacity = max(2, (row_count + peers - 1) // peers)
    slots = jnp.where(
        targets >= 0,
        targets // row_count * capacity + jnp.arange(row_count) % capacity,
        -1,
    )
    outgoing = spread(own.reshape(row_count, length, width), slots, peers * capacity)
    got = lax.all_to_all(
        outgoing.reshape((peers, capacity, length, width)),
        "depth",
        split_axis=0,
        concat_axis=0,
        tiled=True,
    ).reshape(peers * capacity, length, width)
    local = everywhere - position * row_count
    mine = jnp.logical_and(local >= 0, local < row_count)
    code = (
        lax.broadcasted_iota(jnp.int32, (peers, row_count), 0) * capacity
        + lax.broadcasted_iota(jnp.int32, (peers, row_count), 1) % capacity
    )
    wanted = jnp.where(mine, local, -1).reshape(1, -1)
    hit = jnp.arange(row_count)[:, None] == wanted
    source = jnp.max(jnp.where(hit, code.reshape(1, -1), -1), axis=1)
    return settle(source, got), (source >= 0).astype(jnp.int32)


def layer(
    alignment_input,
    target_slot,
    device_alignment,
    layer_norm_gain,
    layer_norm_bias,
    query_key_value_weight,
    output_weight,
):
    targets = target_slot[0]
    row_count, length, width = alignment_input.shape[1:]
    peers = lax.axis_size("depth")
    position = lax.axis_index("depth")
    own = alignment_input.reshape(row_count // 2, 2, length, width)
    everywhere = lax.all_to_all(
        jnp.broadcast_to(targets[None, None], (peers, 1, row_count)),
        "depth",
        split_axis=0,
        concat_axis=0,
        tiled=True,
    ).reshape(peers, row_count)
    partner = lax.ppermute(own, "depth", [(i, i ^ 1) for i in range(peers)])
    value_weight = shifted(query_key_value_weight[0, :, 2 * width :], "section", 1, True)
    out_weight = shifted(output_weight[0], "section", 1, True)
    affine = shifted(
        jnp.concatenate([layer_norm_gain, layer_norm_bias], axis=0), "section", 1, True
    )
    table, meta = plan(position, device_alignment, everywhere)
    settled, live = lax.switch(
        meta[4],
        [
            lambda t, o, p, a, b: dense(a, b, o),
            lambda t, o, p, a, b: routed(ROUTE, t, o, p),
        ],
        table,
        own,
        partner,
        targets,
        everywhere,
    )
    balanced = settled.reshape(row_count * length, width)
    earlier = shifted(balanced, "section", 1, True)
    tied, tied_low = front(
        live, balanced, layer_norm_gain, layer_norm_bias, query_key_value_weight[0]
    )
    neighbours = [shifted(tied_low, "depth", d, False) for d in STEPS]
    attention = shifted(middle(live, meta, tied, neighbours), "section", 1, True)
    handed = back(attention, earlier, affine, value_weight, out_weight, row_count)
    return handed.reshape(1, row_count, length, width)


def solution(mesh):
    placed = (
        P("section", "depth", None, None),
        P("section", "depth"),
        P("section", None),
        P("section", None),
        P("section", None),
        P("section", None, None),
        P("section", None, None),
    )
    return jax.shard_map(
        layer,
        mesh=mesh,
        in_specs=placed,
        out_specs=P("section", "depth", None, None),
        check_vma=False,
    )
```

```python
import functools

import jax
import jax.numpy as jnp
from jax import lax
from jax.experimental import pallas as pl
from jax.experimental.pallas import tpu as pltpu
from jax.sharding import PartitionSpec as P


H = 12
DH = 64
SPAN = 4
PAIRS = H // 2
EPSILON = 1e-05
CHUNK_ROWS = 8
INTERPRET = False


def spread_kernel(slot_ref, rows_ref, out_ref, sem):
    count = rows_ref.shape[0]

    def copy_of(i):
        return pltpu.make_async_copy(
            rows_ref.at[i], out_ref.at[jnp.maximum(slot_ref[i], 0)], sem.at[i]
        )

    for i in range(count):

        @pl.when(slot_ref[i] >= 0)
        def _():
            copy_of(i).start()

    for i in range(count):

        @pl.when(slot_ref[i] >= 0)
        def _():
            copy_of(i).wait()


def spread(rows, slots, slot_count):
    return pl.pallas_call(
        spread_kernel,
        out_shape=jax.ShapeDtypeStruct((slot_count,) + rows.shape[1:], rows.dtype),
        in_specs=[
            pl.BlockSpec(memory_space=pltpu.SMEM),
            pl.BlockSpec(memory_space=pltpu.VMEM),
        ],
        out_specs=pl.BlockSpec(memory_space=pltpu.HBM),
        scratch_shapes=[pltpu.SemaphoreType.DMA((rows.shape[0],))],
        name="spread",
        interpret=INTERPRET,
    )(slots, rows)


def settle_kernel(source_ref, rows_ref, out_ref, landed, in_sem, out_sem):
    row_count, _ = landed.shape[:2]

    def arrival(m):
        return pltpu.make_async_copy(
            rows_ref.at[jnp.maximum(source_ref[m], 0)], landed.at[m], in_sem.at[m]
        )

    def leaving(m):
        return pltpu.make_async_copy(landed.at[m], out_ref.at[m], out_sem.at[m])

    for m in range(row_count):
        arrival(m).start()
    for m in range(row_count):
        arrival(m).wait()

        @pl.when(source_ref[m] < 0)
        def _():
            landed[m] = jnp.zeros_like(landed[m])

        leaving(m).start()
    for m in range(row_count):
        leaving(m).wait()


def settle(source, rows):
    row_count = source.shape[0]
    length, width = rows.shape[1:]
    return pl.pallas_call(
        settle_kernel,
        out_shape=jax.ShapeDtypeStruct((row_count, length, width), rows.dtype),
        in_specs=[
            pl.BlockSpec(memory_space=pltpu.SMEM),
            pl.BlockSpec(memory_space=pl.ANY),
        ],
        out_specs=pl.BlockSpec(memory_space=pltpu.HBM),
        scratch_shapes=[
            pltpu.VMEM((row_count, length, width), rows.dtype),
            pltpu.SemaphoreType.DMA((row_count,)),
            pltpu.SemaphoreType.DMA((row_count,)),
        ],
        name="settle",
        interpret=INTERPRET,
    )(source, rows)


def lane_mask(shape):
    return lax.broadcasted_iota(jnp.int32, shape, len(shape) - 1) % 128 < DH


def normalized(block, gain, bias):
    widened = block.astype(jnp.float32)
    average = jnp.mean(widened, axis=-1, keepdims=True)
    centred = widened - average
    spread_of = jnp.mean(centred * centred, axis=-1, keepdims=True)
    return (centred * lax.rsqrt(spread_of + EPSILON) * gain + bias).astype(jnp.bfloat16)


def front_kernel(
    live_ref,
    rows_ref,
    gain_ref,
    bias_ref,
    weight_ref,
    tied_ref,
    tied_low_ref,
    landed,
    acc,
    sem,
):
    row_count = live_ref.shape[0]
    width = rows_ref.shape[1]
    length = rows_ref.shape[0] // row_count
    span = CHUNK_ROWS * length
    chunks = row_count // CHUNK_ROWS
    copies = [
        pltpu.make_async_copy(rows_ref.at[pl.ds(c * span, span), :], landed.at[c], sem.at[c])
        for c in range(chunks)
    ]
    for copy in copies:
        copy.start()
    gain = gain_ref[...]
    bias = bias_ref[...]
    weight = weight_ref[:, : 2 * width]
    first = lane_mask((length, 256))
    for c in range(chunks):
        copies[c].wait()
        start = c * CHUNK_ROWS
        normed = normalized(landed[c], gain, bias)
        packed = jnp.dot(normed, weight, preferred_element_type=jnp.float32).astype(jnp.bfloat16)
        for pair in range(PAIRS):
            lanes = slice(pair * 128, pair * 128 + 128)
            key_lanes = slice(width + pair * 128, width + pair * 128 + 128)
            total = None
            for r in range(0, CHUNK_ROWS, 2):
                query_parts = []
                key_parts = []
                for k in (r, r + 1):
                    own = slice(k * length, (k + 1) * length)
                    query = packed[own, lanes]
                    query_parts.append(
                        jnp.where(live_ref[start + k] > 0, query, jnp.zeros_like(query))
                    )
                    key_parts.append(packed[own, key_lanes])
                query = jnp.concatenate(query_parts, axis=1)
                key = jnp.concatenate(key_parts, axis=1)
                zero = jnp.zeros_like(query)
                both = jnp.concatenate(
                    [jnp.where(first, query, zero), jnp.where(first, zero, query)], axis=0
                )
                part = lax.dot_general(
                    both, key, (((1,), (1,)), ((), ())), preferred_element_type=jnp.float32
                )
                total = part if total is None else total + part
            own = pl.ds(pair * 2 * length, 2 * length)
            if c == 0:
                acc[own, :] = total
            else:
                acc[own, :] += total
    quarter = H * length // 4
    tied = jnp.concatenate([acc[pl.ds(q * quarter, quarter), :] for q in range(4)], axis=1)
    tied_ref[...] = tied
    tied_low_ref[...] = tied.astype(jnp.bfloat16)


def front(live, rows, gain, bias, weight):
    row_count = live.shape[0]
    width = rows.shape[1]
    length = rows.shape[0] // row_count
    quarter = H * length // 4
    vmem = pl.BlockSpec(memory_space=pltpu.VMEM)
    smem = pl.BlockSpec(memory_space=pltpu.SMEM)
    return pl.pallas_call(
        front_kernel,
        out_shape=(
            jax.ShapeDtypeStruct((quarter, 4 * length), jnp.float32),
            jax.ShapeDtypeStruct((quarter, 4 * length), jnp.bfloat16),
        ),
        in_specs=[smem, pl.BlockSpec(memory_space=pltpu.HBM), vmem, vmem, vmem],
        out_specs=(vmem, vmem),
        scratch_shapes=[
            pltpu.VMEM((row_count // CHUNK_ROWS, CHUNK_ROWS * length, width), jnp.bfloat16),
            pltpu.VMEM((H * length, length), jnp.float32),
            pltpu.SemaphoreType.DMA((row_count // CHUNK_ROWS,)),
        ],
        compiler_params=pltpu.CompilerParams(vmem_limit_bytes=40 << 20),
        name="front",
        interpret=INTERPRET,
    )(live, rows, gain, bias, weight)


STEPS = tuple(d for k in range(1, SPAN) for d in (k, -k))


def middle_kernel(live_ref, meta_ref, tied_ref, *refs):
    neighbours, out_ref = refs[:-1], refs[-1]
    length = tied_ref.shape[1] // 4
    tied = tied_ref[...]
    position, low, high = meta_ref[0], meta_ref[1], meta_ref[2]
    for d, ref in zip(STEPS, neighbours):
        member = jnp.logical_and(position - d >= low, position - d < high)
        tied = tied + jnp.where(member, ref[...].astype(jnp.float32), 0.0)
    quarter = tied.shape[0]
    count = jnp.full((1, length), meta_ref[3], jnp.int32).astype(jnp.float32)
    scale = DH ** (-0.5) / jnp.sqrt(count)
    logits = (
        jnp.concatenate([tied[:, q * length : (q + 1) * length] for q in range(4)], axis=0) * scale
    )
    top = jnp.max(logits, axis=-1, keepdims=True)
    raised = jnp.exp(logits - top)
    attention = raised / jnp.sum(raised, axis=-1, keepdims=True)
    out_ref[pl.ds(0, quarter), :] = jnp.concatenate(
        [attention[q * quarter : (q + 1) * quarter] for q in range(4)], axis=1
    ).astype(jnp.bfloat16)
    lane = lax.broadcasted_iota(jnp.int32, (16, 4 * length), 1)
    live = jnp.zeros((16, 4 * length), jnp.float32)
    for m in range(live_ref.shape[0]):
        live = jnp.where(jnp.logical_and(lane == m, live_ref[m] > 0), 1.0, live)
    out_ref[pl.ds(quarter, 16), :] = live.astype(jnp.bfloat16)


def middle(live, meta, tied, neighbours):
    vmem = pl.BlockSpec(memory_space=pltpu.VMEM)
    smem = pl.BlockSpec(memory_space=pltpu.SMEM)
    return pl.pallas_call(
        middle_kernel,
        out_shape=jax.ShapeDtypeStruct((tied.shape[0] + 16, tied.shape[1]), jnp.bfloat16),
        in_specs=[smem, smem] + [vmem] * (1 + len(neighbours)),
        out_specs=vmem,
        name="middle",
        interpret=INTERPRET,
    )(live, meta, tied, *neighbours)


def back_kernel(
    attention_ref, rows_ref, affine_ref, value_weight_ref, weight_ref, out_ref, landed, ready,
    in_sem, out_sem,
):
    chunks = landed.shape[0]
    span, _ = landed.shape[1:]
    length = span // CHUNK_ROWS
    quarter = H * length // 4
    arrivals = [
        pltpu.make_async_copy(rows_ref.at[pl.ds(c * span, span), :], landed.at[c], in_sem.at[c])
        for c in range(chunks)
    ]
    leavings = [
        pltpu.make_async_copy(ready.at[c], out_ref.at[pl.ds(c * span, span), :], out_sem.at[c])
        for c in range(chunks)
    ]
    for copy in arrivals:
        copy.start()
    packed = attention_ref[pl.ds(0, quarter), :]
    attention = jnp.concatenate(
        [packed[:, q * length : (q + 1) * length] for q in range(4)], axis=0
    )
    live = attention_ref[pl.ds(quarter, 16), :].astype(jnp.float32)
    wide = jnp.concatenate([attention] * CHUNK_ROWS, axis=1)
    diagonal = (
        lax.broadcasted_iota(jnp.int32, (span, span), 0) // length
        == lax.broadcasted_iota(jnp.int32, (span, span), 1) // length
    )
    first = lane_mask((span, 128))
    mixers = []
    for h in range(H):
        tall = jnp.concatenate([wide[h * length : (h + 1) * length]] * CHUNK_ROWS, axis=0)
        mixers.append(jnp.where(diagonal, tall, jnp.zeros_like(tall)))
    gain = affine_ref[0:1, :]
    bias = affine_ref[1:2, :]
    value_weight = value_weight_ref[...]
    weight = weight_ref[...]
    for c in range(chunks):
        arrivals[c].wait()
        block = landed[c]
        values = jnp.dot(
            normalized(block, gain, bias), value_weight, preferred_element_type=jnp.float32
        ).astype(jnp.bfloat16)
        parts = []
        for pair in range(PAIRS):
            lanes = values[:, pair * 128 : pair * 128 + 128]
            low = jnp.dot(mixers[2 * pair], lanes, preferred_element_type=jnp.float32)
            high = jnp.dot(mixers[2 * pair + 1], lanes, preferred_element_type=jnp.float32)
            parts.append(jnp.where(first, low, high).astype(jnp.bfloat16))
        attended = jnp.concatenate(parts, axis=1)
        mixed = jnp.dot(attended, weight, preferred_element_type=jnp.float32)
        mixed = mixed + block.astype(jnp.float32)
        for k in range(CHUNK_ROWS):
            m = c * CHUNK_ROWS + k
            own = mixed[k * length : (k + 1) * length]
            ready[c, pl.ds(k * length, length), :] = (
                own * jnp.broadcast_to(live[0:1, m : m + 1], own.shape)
            ).astype(jnp.bfloat16)
        leavings[c].start()
    for copy in leavings:
        copy.wait()


def back(attention, rows, affine, value_weight, weight, row_count):
    vmem = pl.BlockSpec(memory_space=pltpu.VMEM)
    anywhere = pl.BlockSpec(memory_space=pltpu.HBM)
    width = rows.shape[1]
    chunks = row_count // CHUNK_ROWS
    span = rows.shape[0] // chunks
    return pl.pallas_call(
        back_kernel,
        out_shape=jax.ShapeDtypeStruct(rows.shape, jnp.bfloat16),
        in_specs=[vmem, anywhere, vmem, vmem, vmem],
        out_specs=anywhere,
        scratch_shapes=[
            pltpu.VMEM((chunks, span, width), jnp.bfloat16),
            pltpu.VMEM((chunks, span, width), jnp.bfloat16),
            pltpu.SemaphoreType.DMA((chunks,)),
            pltpu.SemaphoreType.DMA((chunks,)),
        ],
        compiler_params=pltpu.CompilerParams(vmem_limit_bytes=40 << 20),
        name="back",
        interpret=INTERPRET,
    )(attention, rows, affine, value_weight, weight)


def shifted(value, axis, steps, wrap):
    count = lax.axis_size(axis)
    if wrap:
        route = [(i, (i + steps) % count) for i in range(count)]
    else:
        route = [(i, i + steps) for i in range(count) if 0 <= i + steps < count]
    return lax.ppermute(value, axis, route)


ROUTE = ((11, 9, 6, 4), (10, 5), 12)
Z_STAY = 8
RING_Z = 8
RING_X = 4


def plan_kernel(position_ref, groups_ref, targets_ref, table_ref, meta_ref):
    peers, row_count = targets_ref.shape
    pair_count = row_count // 2
    position = position_ref[0]
    shape = (peers, 128)
    down = lax.broadcasted_iota(jnp.int32, shape, 0)
    across = lax.broadcasted_iota(jnp.int32, shape, 1)
    zero = jnp.zeros(shape, jnp.int32)

    def over_lanes(value):
        return jnp.broadcast_to(jnp.sum(value, axis=1, keepdims=True), shape)

    def over_rows(value):
        return jnp.broadcast_to(jnp.sum(value, axis=0, keepdims=True), shape)

    def top_rows(value):
        return jnp.max(value, axis=0, keepdims=True)

    def flag(condition):
        return jnp.where(condition, 1, zero)

    def to_lanes(value):
        return over_rows(jnp.where(down == across, value, zero))

    def to_rows(value):
        return over_lanes(jnp.where(down == across, value, zero))

    targets = jnp.concatenate(
        [targets_ref[...], jnp.full((peers, 128 - row_count), -1, jnp.int32)], axis=1
    )
    device = targets >> 5
    offset = jnp.where(targets >= 0, (device - down) & (peers - 1), -1)
    seen = zero
    for i in range(row_count):
        seen = seen | flag(jnp.broadcast_to(offset[:, i : i + 1], shape) == across)
    present_l = flag(over_rows(seen) > 0)
    present = to_rows(present_l)
    odd = down & 1
    odd_l = across & 1

    def turns(core):
        step = ((down + odd * (1 - 2 * core)) >> 1) & 31
        step_l = ((across + odd_l * (1 - 2 * core)) >> 1) & 31
        u, u_l = step & 7, step_l & 7
        order = u * 64 + down
        order_l = u_l * 64 + across
        moving = present * flag(u > 0)
        moving_l = present_l * flag(u_l > 0)
        rank = over_lanes(moving_l * flag(order_l < order))
        rest = over_lanes((present_l - moving_l) * flag(order_l < order))
        return step >> 3, u, moving, rank, rest

    def split_of(core):
        caps = ROUTE[0]
        _, u, moving, rank, _ = turns(core)
        early = moving * flag(rank < across)
        late = moving - early
        good = flag(across <= pair_count)
        for h in range(1, 6):
            cap = caps[h - 1] if h <= len(caps) else 0
            good = good * flag(over_rows(early * flag(u >= h)) <= cap)
            good = good * flag(over_rows(late * flag(RING_Z - u >= h)) <= cap)
        split = jnp.min(jnp.where(good > 0, across, 127), axis=1, keepdims=True)
        return jnp.broadcast_to(split, shape)

    def z_lanes(core, split):
        (z1, z2, z3, z4) = ROUTE[0]
        _, u, moving, rank, rest = turns(core)
        plus = moving * flag(rank < split)
        staying = present - moving
        hops = jnp.where(plus > 0, u, RING_Z - u)
        place = jnp.where(plus > 0, split - 1 - rank, rank - split)
        base = jnp.where(
            hops == 1, 0, jnp.where(hops == 2, z1, jnp.where(hops == 3, z1 + z2, z1 + z2 + z3))
        )
        side = moving - plus
        z_all = z1 + z2 + z3 + z4
        z_leave = jnp.where(staying > 0, 2 * z1 + rest, side * z1 + place)
        z_land = jnp.where(staying > 0, 2 * z_all + rest, side * z_all + base + place)
        return jnp.where(present > 0, z_leave, -1), jnp.where(present > 0, z_land, -1)

    def x_counts(core, line):
        high, u, _, _, _ = turns(core)
        turn = (high + flag(line < u)) & (RING_X - 1)
        turn = jnp.where(present > 0, turn, -1)
        count = [over_rows(flag(turn == v)) for v in range(RING_X)]
        x2 = ROUTE[1][1]
        ahead = (count[2] + count[3] - count[1] + 1) >> 1
        ahead = jnp.minimum(
            jnp.maximum(ahead, jnp.maximum(count[2] - x2, 0)), jnp.minimum(count[2], x2)
        )
        return turn, count, ahead

    def fits(core):
        x1, x2 = ROUTE[1]
        _, count, ahead = x_counts(core, across)
        behind = count[2] - ahead
        good = (
            flag(ahead <= x2)
            * flag(behind <= x2)
            * flag(ahead + count[1] <= x1)
            * flag(behind + count[3] <= x1)
            * flag(count[0] <= ROUTE[2])
        )
        return jnp.min(jnp.where(across < RING_Z, good, 1))

    def x_lanes(core, line):
        x1, x2 = ROUTE[1]
        turn, count, ahead = x_counts(core, line)
        turn_l = to_lanes(turn)
        level = over_lanes(present_l * flag(turn_l == turn) * flag(across < down))
        double = flag(turn == 2)
        near = double * flag(level < ahead)
        forward = flag(turn == 1) + near
        spot = jnp.where(
            double > 0,
            level - jnp.where(near > 0, 0, ahead),
            level + jnp.where(turn == 1, ahead, count[2] - ahead),
        )
        side = 1 - forward
        x_leave = jnp.where(turn == 0, 2 * x1 + level, side * x1 + spot)
        x_land = jnp.where(
            turn == 0, 2 * (x1 + x2) + level, side * (x1 + x2) + double * x1 + spot
        )
        return jnp.where(present > 0, x_leave, -1), jnp.where(present > 0, x_land, -1)

    core = position & 1
    split = split_of(core)
    z_leave, z_land = z_lanes(core, split)
    line = (position >> 1) & (RING_Z - 1)
    x_leave_a, x_land_a = x_lanes(core, line)
    x_leave_b, x_land_b = x_lanes(core, RING_Z - 1 - line)
    other_split = split_of(1 - core)
    good = jnp.where(
        jnp.max(jnp.maximum(split, other_split)) <= pair_count, fits(core) * fits(1 - core), 0
    )

    lane_row = lax.broadcasted_iota(jnp.int32, (1, 128), 1)
    origin = -1 + zero
    for b in range(2):
        sender = position if b == 0 else position ^ 1
        mine = targets_ref[pl.ds(sender, 1), :]
        mine = jnp.concatenate([mine, jnp.full((1, 128 - row_count), -1, jnp.int32)], axis=1)
        away = ((mine >> 5) - sender) & (peers - 1)
        away = jnp.where(mine >= 0, away, -1)
        away = jnp.where((away & 1) == b, away, -1)
        hit = jnp.broadcast_to(away, shape) == down
        code = b * pair_count + (jnp.broadcast_to(lane_row, shape) >> 1)
        found = jnp.max(jnp.where(hit, code, -1), axis=1, keepdims=True)
        origin = jnp.maximum(origin, jnp.broadcast_to(found, shape))

    def gathered(slot_of, value):
        return top_rows(jnp.where(slot_of == across, value, -1))

    local = targets - position * row_count
    here = jnp.logical_and(local >= 0, local < row_count)
    settled_a = jnp.full((1, 128), -1, jnp.int32)
    settled_b = settled_a
    lane_full = across & 1
    for r in range(2):
        slot = jnp.max(
            jnp.where(jnp.logical_and(here, lane_full == r), local, -1), axis=1, keepdims=True
        )
        slot = jnp.broadcast_to(slot, shape)
        slot_l = over_rows(jnp.where(down == across, slot + 1, zero)) - 1
        match = across == ((position - down) & (peers - 1))
        slot_by_offset = over_lanes(jnp.where(match, slot_l + 1, zero)) - 1
        settled_a = jnp.maximum(settled_a, gathered(slot_by_offset, x_land_a * 2 + r))
        settled_b = jnp.maximum(settled_b, gathered(slot_by_offset, z_land * 2 + r))
    empty = jnp.full((1, 128), -1, jnp.int32)
    table_ref[...] = jnp.concatenate(
        [
            gathered(z_leave, origin),
            gathered(x_leave_b, origin),
            gathered(x_leave_a, z_land),
            gathered(z_leave, x_land_b),
            settled_a,
            settled_b,
            empty,
            empty,
        ],
        axis=0,
    )
    groups = groups_ref[...]
    lane = lax.broadcasted_iota(jnp.int32, groups.shape, 1)
    own_group = jnp.sum(jnp.where(lane == position, groups, 0))
    low = jnp.sum(jnp.where(groups < own_group, 1, 0))
    high = low + jnp.sum(jnp.where(groups == own_group, 1, 0))
    inside = jnp.logical_and(targets >= low * row_count, targets < high * row_count)
    meta_ref[0] = position
    meta_ref[1] = low
    meta_ref[2] = high
    meta_ref[3] = jnp.sum(jnp.where(inside, 1, 0))
    meta_ref[4] = good


def plan(position, groups, targets):
    vmem = pl.BlockSpec(memory_space=pltpu.VMEM)
    smem = pl.BlockSpec(memory_space=pltpu.SMEM)
    return pl.pallas_call(
        plan_kernel,
        out_shape=(
            jax.ShapeDtypeStruct((8, 128), jnp.int32),
            jax.ShapeDtypeStruct((8,), jnp.int32),
        ),
        in_specs=[smem, vmem, vmem],
        out_specs=(vmem, smem),
        name="plan",
        interpret=INTERPRET,
    )(position.reshape(1), groups, targets)


def deal(table_ref, row, pool, outs):
    lane = 0
    for out in outs:

        def step(k, carry, out=out, lane=lane):
            out[k] = pool[jnp.maximum(table_ref[row, lane + k], 0)]
            return carry

        lax.fori_loop(0, out.shape[0], step, 0)
        lane += out.shape[0]


def leave_kernel(table_ref, own_ref, partner_ref, *refs):
    outs, (pool, sem) = refs[:-2], refs[-2:]
    pairs = own_ref.shape[0]
    half = own_ref.shape[2] // 2
    copies = []
    for part in range(2):
        for b, ref in enumerate((own_ref, partner_ref)):
            copies.append(
                pltpu.make_async_copy(
                    ref.at[:, :, pl.ds(part * half, half), :],
                    pool.at[part, pl.ds(b * pairs, pairs)],
                    sem.at[len(copies)],
                )
            )
    for copy in copies:
        copy.start()
    for part in range(2):
        copies[2 * part].wait()
        copies[2 * part + 1].wait()
        deal(table_ref, part, pool.at[part], outs[3 * part : 3 * part + 3])


def leave(table, own, partner, route):
    (z1, _, _, _), (x1, _), x_stay = route
    pairs, two, length, width = own.shape
    vmem = pl.BlockSpec(memory_space=pltpu.VMEM)
    anywhere = pl.BlockSpec(memory_space=pl.ANY)
    sizes = (z1, z1, Z_STAY, x1, x1, x_stay)
    return pl.pallas_call(
        leave_kernel,
        out_shape=tuple(
            jax.ShapeDtypeStruct((n, two, length // 2, width), own.dtype) for n in sizes
        ),
        in_specs=[pl.BlockSpec(memory_space=pltpu.SMEM), anywhere, anywhere],
        out_specs=(vmem,) * len(sizes),
        scratch_shapes=[
            pltpu.VMEM((2, 2 * pairs, two, length // 2, width), own.dtype),
            pltpu.SemaphoreType.DMA((4,)),
        ],
        compiler_params=pltpu.CompilerParams(vmem_limit_bytes=40 << 20),
        name="leave",
        interpret=INTERPRET,
    )(table, own, partner)


def pooled(refs, pool, sem):
    copies = []
    start = 0
    for ref in refs:
        count = ref.shape[0]
        copies.append(
            pltpu.make_async_copy(ref, pool.at[pl.ds(start, count)], sem.at[len(copies)])
        )
        start += count
    return copies


def turn_kernel(row, count, table_ref, *refs):
    sources, outs, (pool, sem) = refs[:count], refs[count:-2], refs[-2:]
    copies = pooled(sources, pool, sem)
    for copy in copies:
        copy.start()
    for copy in copies:
        copy.wait()
    deal(table_ref, row, pool, outs)


def turn_over(table, row, sources, sizes):
    vmem = pl.BlockSpec(memory_space=pltpu.VMEM)
    anywhere = pl.BlockSpec(memory_space=pl.ANY)
    payload = sources[0].shape[1:]
    return pl.pallas_call(
        functools.partial(turn_kernel, row, len(sources)),
        out_shape=tuple(jax.ShapeDtypeStruct((n,) + payload, sources[0].dtype) for n in sizes),
        in_specs=[pl.BlockSpec(memory_space=pltpu.SMEM)] + [anywhere] * len(sources),
        out_specs=(vmem,) * len(sizes),
        scratch_shapes=[
            pltpu.VMEM((sum(s.shape[0] for s in sources),) + payload, sources[0].dtype),
            pltpu.SemaphoreType.DMA((len(sources),)),
        ],
        compiler_params=pltpu.CompilerParams(vmem_limit_bytes=40 << 20),
        name="turn_over",
        interpret=INTERPRET,
    )(table, *sources)


def land_kernel(count_a, count_b, table_ref, *refs):
    sources_a, sources_b = refs[:count_a], refs[count_a : count_a + count_b]
    out_ref, live_ref, pool_a, pool_b, done, sem_a, sem_b, out_sem = refs[count_a + count_b :]
    row_count, length, _ = done.shape
    half = length // 2
    copies = pooled(sources_a, pool_a, sem_a) + pooled(sources_b, pool_b, sem_b)
    for copy in copies:
        copy.start()
    for copy in copies:
        copy.wait()

    def step(m, carry):
        live = table_ref[4, m] >= 0
        live_ref[m] = jnp.where(live, 1, 0)
        for part, pool in ((0, pool_a), (1, pool_b)):
            code = jnp.maximum(table_ref[4 + part, m], 0)
            value = pool[code >> 1, code & 1]
            done[m, pl.ds(part * half, half), :] = jnp.where(live, value, jnp.zeros_like(value))
        return carry

    lax.fori_loop(0, row_count, step, 0)
    copy = pltpu.make_async_copy(done, out_ref, out_sem)
    copy.start()
    copy.wait()


def land(table, sources_a, sources_b, row_count, length):
    anywhere = pl.BlockSpec(memory_space=pl.ANY)
    smem = pl.BlockSpec(memory_space=pltpu.SMEM)
    two, half, width = sources_a[0].shape[1:]
    dtype = sources_a[0].dtype
    return pl.pallas_call(
        functools.partial(land_kernel, len(sources_a), len(sources_b)),
        out_shape=(
            jax.ShapeDtypeStruct((row_count, length, width), dtype),
            jax.ShapeDtypeStruct((row_count,), jnp.int32),
        ),
        in_specs=[smem] + [anywhere] * (len(sources_a) + len(sources_b)),
        out_specs=(pl.BlockSpec(memory_space=pltpu.HBM), smem),
        scratch_shapes=[
            pltpu.VMEM((sum(s.shape[0] for s in sources_a), two, half, width), dtype),
            pltpu.VMEM((sum(s.shape[0] for s in sources_b), two, half, width), dtype),
            pltpu.VMEM((row_count, length, width), dtype),
            pltpu.SemaphoreType.DMA((len(sources_a),)),
            pltpu.SemaphoreType.DMA((len(sources_b),)),
            pltpu.SemaphoreType.DMA,
        ],
        compiler_params=pltpu.CompilerParams(vmem_limit_bytes=40 << 20),
        name="land",
        interpret=INTERPRET,
    )(table, *sources_a, *sources_b)


def chain(forward, backward, caps, step, ring):
    def moved(i, by):
        return (i // (step * ring)) * step * ring + (i + by * step) % (step * ring)

    devices = range(lax.axis_size("depth"))
    onward, returning = [], []
    for cap in caps:
        forward = lax.ppermute(forward[:cap], "depth", [(i, moved(i, 1)) for i in devices])
        backward = lax.ppermute(backward[:cap], "depth", [(i, moved(i, -1)) for i in devices])
        onward.append(forward)
        returning.append(backward)
    return onward + returning


def routed(route, table, own, partner):
    z_caps, x_caps, x_stay = route
    z_sizes = (z_caps[0], z_caps[0], Z_STAY)
    x_sizes = (x_caps[0], x_caps[0], x_stay)
    z_plus, z_minus, z_still, x_plus, x_minus, x_still = leave(table, own, partner, route)
    along_x = chain(x_plus, x_minus, x_caps, 2 * RING_Z, RING_X)
    along_z = chain(z_plus, z_minus, z_caps, 2, RING_Z)
    later = turn_over(table, 3, along_x + [x_still], z_sizes)
    last_b = chain(later[0], later[1], z_caps, 2, RING_Z)
    turned = turn_over(table, 2, along_z + [z_still], x_sizes)
    last_a = chain(turned[0], turned[1], x_caps, 2 * RING_Z, RING_X)
    return land(
        table,
        last_a + [turned[2]],
        last_b + [later[2]],
        own.shape[0] * own.shape[1],
        own.shape[2],
    )


def dense(targets, everywhere, own):
    row_count = targets.shape[0]
    _, _, length, width = own.shape
    peers = lax.axis_size("depth")
    position = lax.axis_index("depth")
    capacity = max(2, (row_count + peers - 1) // peers)
    slots = jnp.where(
        targets >= 0,
        targets // row_count * capacity + jnp.arange(row_count) % capacity,
        -1,
    )
    outgoing = spread(own.reshape(row_count, length, width), slots, peers * capacity)
    got = lax.all_to_all(
        outgoing.reshape((peers, capacity, length, width)),
        "depth",
        split_axis=0,
        concat_axis=0,
        tiled=True,
    ).reshape(peers * capacity, length, width)
    local = everywhere - position * row_count
    mine = jnp.logical_and(local >= 0, local < row_count)
    code = (
        lax.broadcasted_iota(jnp.int32, (peers, row_count), 0) * capacity
        + lax.broadcasted_iota(jnp.int32, (peers, row_count), 1) % capacity
    )
    wanted = jnp.where(mine, local, -1).reshape(1, -1)
    hit = jnp.arange(row_count)[:, None] == wanted
    source = jnp.max(jnp.where(hit, code.reshape(1, -1), -1), axis=1)
    return settle(source, got), (source >= 0).astype(jnp.int32)


def layer(
    alignment_input,
    target_slot,
    device_alignment,
    layer_norm_gain,
    layer_norm_bias,
    query_key_value_weight,
    output_weight,
):
    targets = target_slot[0]
    row_count, length, width = alignment_input.shape[1:]
    peers = lax.axis_size("depth")
    position = lax.axis_index("depth")
    own = alignment_input.reshape(row_count // 2, 2, length, width)
    everywhere = lax.all_to_all(
        jnp.broadcast_to(targets[None, None], (peers, 1, row_count)),
        "depth",
        split_axis=0,
        concat_axis=0,
        tiled=True,
    ).reshape(peers, row_count)
    partner = lax.ppermute(own, "depth", [(i, i ^ 1) for i in range(peers)])
    value_weight = shifted(query_key_value_weight[0, :, 2 * width :], "section", 1, True)
    out_weight = shifted(output_weight[0], "section", 1, True)
    affine = shifted(
        jnp.concatenate([layer_norm_gain, layer_norm_bias], axis=0), "section", 1, True
    )
    table, meta = plan(position, device_alignment, everywhere)
    settled, live = lax.switch(
        meta[4],
        [
            lambda t, o, p, a, b: dense(a, b, o),
            lambda t, o, p, a, b: routed(ROUTE, t, o, p),
        ],
        table,
        own,
        partner,
        targets,
        everywhere,
    )
    balanced = settled.reshape(row_count * length, width)
    earlier = shifted(balanced, "section", 1, True)
    tied, tied_low = front(
        live, balanced, layer_norm_gain, layer_norm_bias, query_key_value_weight[0]
    )
    neighbours = [shifted(tied_low, "depth", d, False) for d in STEPS]
    attention = shifted(middle(live, meta, tied, neighbours), "section", 1, True)
    handed = back(attention, earlier, affine, value_weight, out_weight, row_count)
    return handed.reshape(1, row_count, length, width)


def solution(mesh):
    placed = (
        P("section", "depth", None, None),
        P("section", "depth"),
        P("section", None),
        P("section", None),
        P("section", None),
        P("section", None, None),
        P("section", None, None),
    )
    return jax.shard_map(
        layer,
        mesh=mesh,
        in_specs=placed,
        out_specs=P("section", "depth", None, None),
        check_vma=False,
    )
```

```python
import functools

import jax
import jax.numpy as jnp
from jax import lax
from jax.experimental import pallas as pl
from jax.experimental.pallas import tpu as pltpu
from jax.sharding import PartitionSpec as P


H = 12
DH = 64
PAIRS = H // 2
EPSILON = 1e-05
CHUNK_ROWS = 8
PARTS = 2
INTERPRET = False


def spread_kernel(slot_ref, rows_ref, out_ref, sem):
    count = rows_ref.shape[0]

    def copy_of(i):
        return pltpu.make_async_copy(
            rows_ref.at[i], out_ref.at[jnp.maximum(slot_ref[i], 0)], sem.at[i]
        )

    def begin(i, carry):
        @pl.when(slot_ref[i] >= 0)
        def _():
            copy_of(i).start()

        return carry

    def finish(i, carry):
        @pl.when(slot_ref[i] >= 0)
        def _():
            copy_of(i).wait()

        return carry

    lax.fori_loop(0, count, begin, 0)
    lax.fori_loop(0, count, finish, 0)


def spread(rows, slots, slot_count):
    return pl.pallas_call(
        spread_kernel,
        out_shape=jax.ShapeDtypeStruct((slot_count,) + rows.shape[1:], rows.dtype),
        in_specs=[
            pl.BlockSpec(memory_space=pltpu.SMEM),
            pl.BlockSpec(memory_space=pltpu.VMEM),
        ],
        out_specs=pl.BlockSpec(memory_space=pltpu.HBM),
        scratch_shapes=[pltpu.SemaphoreType.DMA((rows.shape[0],))],
        name="spread",
        interpret=INTERPRET,
    )(slots, rows)


def settle_kernel(source_ref, rows_ref, *refs):
    outs, (landed, in_sem, out_sem) = refs[:PARTS], refs[PARTS:]
    row_count = landed.shape[0]
    part = row_count // PARTS

    def arrival(m):
        return pltpu.make_async_copy(
            rows_ref.at[jnp.maximum(source_ref[m], 0)], landed.at[m], in_sem.at[m]
        )

    def begin(m, carry):
        arrival(m).start()
        return carry

    def empty(m, carry):
        arrival(m).wait()

        @pl.when(source_ref[m] < 0)
        def _():
            landed[m] = jnp.zeros_like(landed[m])

        return carry

    lax.fori_loop(0, row_count, begin, 0)
    lax.fori_loop(0, row_count, empty, 0)
    leaving = [
        pltpu.make_async_copy(landed.at[pl.ds(k * part, part)], out, out_sem.at[k])
        for k, out in enumerate(outs)
    ]
    for copy in leaving:
        copy.start()
    for copy in leaving:
        copy.wait()


def settle(source, rows):
    row_count = source.shape[0]
    length, width = rows.shape[1:]
    return pl.pallas_call(
        settle_kernel,
        out_shape=(jax.ShapeDtypeStruct((row_count // PARTS, length, width), rows.dtype),) * PARTS,
        in_specs=[
            pl.BlockSpec(memory_space=pltpu.SMEM),
            pl.BlockSpec(memory_space=pl.ANY),
        ],
        out_specs=(pl.BlockSpec(memory_space=pltpu.HBM),) * PARTS,
        scratch_shapes=[
            pltpu.VMEM((row_count, length, width), rows.dtype),
            pltpu.SemaphoreType.DMA((row_count,)),
            pltpu.SemaphoreType.DMA((PARTS,)),
        ],
        name="settle",
        interpret=INTERPRET,
    )(source, rows)


def lane_mask(shape):
    return lax.broadcasted_iota(jnp.int32, shape, len(shape) - 1) % 128 < DH


def normalized(block, gain, bias):
    widened = block.astype(jnp.float32)
    average = jnp.mean(widened, axis=-1, keepdims=True)
    centred = widened - average
    spread_of = jnp.mean(centred * centred, axis=-1, keepdims=True)
    return (centred * lax.rsqrt(spread_of + EPSILON) * gain + bias).astype(jnp.bfloat16)


def front_kernel(
    live_ref,
    rows_0_ref,
    rows_1_ref,
    gain_ref,
    bias_ref,
    weight_ref,
    tied_ref,
    tied_low_ref,
    landed,
    acc,
    sem,
):
    row_count = live_ref.shape[0]
    width = rows_0_ref.shape[1]
    length = rows_0_ref.shape[0] * PARTS // row_count
    span = CHUNK_ROWS * length
    chunks = row_count // CHUNK_ROWS
    each = chunks // PARTS
    copies = [
        pltpu.make_async_copy(
            (rows_0_ref, rows_1_ref)[c // each].at[pl.ds(c % each * span, span), :],
            landed.at[c],
            sem.at[c],
        )
        for c in range(chunks)
    ]
    for copy in copies:
        copy.start()
    gain = gain_ref[...]
    bias = bias_ref[...]
    weight = weight_ref[:, : 2 * width]
    first = lane_mask((length, 256))
    for c in range(chunks):
        copies[c].wait()
        start = c * CHUNK_ROWS
        normed = normalized(landed[c], gain, bias)
        packed = jnp.dot(normed, weight, preferred_element_type=jnp.float32).astype(jnp.bfloat16)
        for pair in range(PAIRS):
            lanes = slice(pair * 128, pair * 128 + 128)
            key_lanes = slice(width + pair * 128, width + pair * 128 + 128)
            total = None
            for r in range(0, CHUNK_ROWS, 2):
                query_parts = []
                key_parts = []
                for k in (r, r + 1):
                    own = slice(k * length, (k + 1) * length)
                    query = packed[own, lanes]
                    query_parts.append(
                        jnp.where(live_ref[start + k] > 0, query, jnp.zeros_like(query))
                    )
                    key_parts.append(packed[own, key_lanes])
                query = jnp.concatenate(query_parts, axis=1)
                key = jnp.concatenate(key_parts, axis=1)
                zero = jnp.zeros_like(query)
                both = jnp.concatenate(
                    [jnp.where(first, query, zero), jnp.where(first, zero, query)], axis=0
                )
                part = lax.dot_general(
                    both, key, (((1,), (1,)), ((), ())), preferred_element_type=jnp.float32
                )
                total = part if total is None else total + part
            own = pl.ds(pair * 2 * length, 2 * length)
            if c == 0:
                acc[own, :] = total
            else:
                acc[own, :] += total
    quarter = H * length // 4
    tied = jnp.concatenate([acc[pl.ds(q * quarter, quarter), :] for q in range(4)], axis=1)
    tied_ref[...] = tied
    tied_low_ref[...] = tied.astype(jnp.bfloat16)


def front(live, rows, gain, bias, weight):
    row_count = live.shape[0]
    width = rows[0].shape[1]
    length = rows[0].shape[0] * PARTS // row_count
    quarter = H * length // 4
    vmem = pl.BlockSpec(memory_space=pltpu.VMEM)
    smem = pl.BlockSpec(memory_space=pltpu.SMEM)
    return pl.pallas_call(
        front_kernel,
        out_shape=(
            jax.ShapeDtypeStruct((quarter, 4 * length), jnp.float32),
            jax.ShapeDtypeStruct((quarter, 4 * length), jnp.bfloat16),
        ),
        in_specs=[smem] + [pl.BlockSpec(memory_space=pltpu.HBM)] * PARTS + [vmem, vmem, vmem],
        out_specs=(vmem, vmem),
        scratch_shapes=[
            pltpu.VMEM((row_count // CHUNK_ROWS, CHUNK_ROWS * length, width), jnp.bfloat16),
            pltpu.VMEM((H * length, length), jnp.float32),
            pltpu.SemaphoreType.DMA((row_count // CHUNK_ROWS,)),
        ],
        compiler_params=pltpu.CompilerParams(vmem_limit_bytes=40 << 20),
        name="front",
        interpret=INTERPRET,
    )(live, *rows, gain, bias, weight)


def belongs(meta_ref, step):
    other = meta_ref[0] + step
    return jnp.logical_and(other >= meta_ref[1], other < meta_ref[2])


def join_kernel(meta_ref, tied_ref, below_ref, above_ref, sum_ref, up_ref, down_ref):
    tied = tied_ref[...]
    below = jnp.where(belongs(meta_ref, -1), below_ref[...].astype(jnp.float32), 0.0)
    above = jnp.where(belongs(meta_ref, 1), above_ref[...].astype(jnp.float32), 0.0)
    sum_ref[...] = tied + below + above
    up_ref[...] = (tied + below).astype(jnp.bfloat16)
    down_ref[...] = (tied + above).astype(jnp.bfloat16)


def join(meta, tied, below, above):
    vmem = pl.BlockSpec(memory_space=pltpu.VMEM)
    return pl.pallas_call(
        join_kernel,
        out_shape=(
            jax.ShapeDtypeStruct(tied.shape, jnp.float32),
            jax.ShapeDtypeStruct(tied.shape, jnp.bfloat16),
            jax.ShapeDtypeStruct(tied.shape, jnp.bfloat16),
        ),
        in_specs=[pl.BlockSpec(memory_space=pltpu.SMEM), vmem, vmem, vmem],
        out_specs=(vmem, vmem, vmem),
        name="join",
        interpret=INTERPRET,
    )(meta, tied, below, above)


def middle_kernel(live_ref, meta_ref, tied_ref, below_ref, above_ref, out_ref):
    length = tied_ref.shape[1] // 4
    tied = tied_ref[...]
    tied = tied + jnp.where(belongs(meta_ref, -2), below_ref[...].astype(jnp.float32), 0.0)
    tied = tied + jnp.where(belongs(meta_ref, 2), above_ref[...].astype(jnp.float32), 0.0)
    quarter = tied.shape[0]
    count = jnp.full((1, length), meta_ref[3], jnp.int32).astype(jnp.float32)
    scale = DH ** (-0.5) / jnp.sqrt(count)
    logits = (
        jnp.concatenate([tied[:, q * length : (q + 1) * length] for q in range(4)], axis=0) * scale
    )
    top = jnp.max(logits, axis=-1, keepdims=True)
    raised = jnp.exp(logits - top)
    attention = raised / jnp.sum(raised, axis=-1, keepdims=True)
    out_ref[pl.ds(0, quarter), :] = jnp.concatenate(
        [attention[q * quarter : (q + 1) * quarter] for q in range(4)], axis=1
    ).astype(jnp.bfloat16)
    lane = lax.broadcasted_iota(jnp.int32, (16, 4 * length), 1)
    live = jnp.zeros((16, 4 * length), jnp.float32)
    for m in range(live_ref.shape[0]):
        live = jnp.where(jnp.logical_and(lane == m, live_ref[m] > 0), 1.0, live)
    out_ref[pl.ds(quarter, 16), :] = live.astype(jnp.bfloat16)


def middle(live, meta, tied, neighbours):
    vmem = pl.BlockSpec(memory_space=pltpu.VMEM)
    smem = pl.BlockSpec(memory_space=pltpu.SMEM)
    return pl.pallas_call(
        middle_kernel,
        out_shape=jax.ShapeDtypeStruct((tied.shape[0] + 16, tied.shape[1]), jnp.bfloat16),
        in_specs=[smem, smem] + [vmem] * (1 + len(neighbours)),
        out_specs=vmem,
        name="middle",
        interpret=INTERPRET,
    )(live, meta, tied, *neighbours)


def back_kernel(
    offset, attention_ref, rows_ref, affine_ref, value_weight_ref, weight_ref, *refs
):
    out_ref, landed, ready, in_sem, out_sem = refs[-5:]
    chunks = landed.shape[0]
    span, _ = landed.shape[1:]
    length = span // CHUNK_ROWS
    quarter = H * length // 4
    arrivals = [
        pltpu.make_async_copy(rows_ref.at[pl.ds(c * span, span), :], landed.at[c], in_sem.at[c])
        for c in range(chunks)
    ]
    leavings = [
        pltpu.make_async_copy(
            ready.at[c], out_ref.at[pl.ds((offset + c) * span, span), :], out_sem.at[c]
        )
        for c in range(chunks)
    ]
    for copy in arrivals:
        copy.start()
    packed = attention_ref[pl.ds(0, quarter), :]
    attention = jnp.concatenate(
        [packed[:, q * length : (q + 1) * length] for q in range(4)], axis=0
    )
    live = attention_ref[pl.ds(quarter, 16), :].astype(jnp.float32)
    wide = jnp.concatenate([attention] * CHUNK_ROWS, axis=1)
    diagonal = (
        lax.broadcasted_iota(jnp.int32, (span, span), 0) // length
        == lax.broadcasted_iota(jnp.int32, (span, span), 1) // length
    )
    first = lane_mask((span, 128))
    mixers = []
    for h in range(H):
        tall = jnp.concatenate([wide[h * length : (h + 1) * length]] * CHUNK_ROWS, axis=0)
        mixers.append(jnp.where(diagonal, tall, jnp.zeros_like(tall)))
    gain = affine_ref[0:1, :]
    bias = affine_ref[1:2, :]
    value_weight = value_weight_ref[...]
    weight = weight_ref[...]
    for c in range(chunks):
        arrivals[c].wait()
        block = landed[c]
        values = jnp.dot(
            normalized(block, gain, bias), value_weight, preferred_element_type=jnp.float32
        ).astype(jnp.bfloat16)
        parts = []
        for pair in range(PAIRS):
            lanes = values[:, pair * 128 : pair * 128 + 128]
            low = jnp.dot(mixers[2 * pair], lanes, preferred_element_type=jnp.float32)
            high = jnp.dot(mixers[2 * pair + 1], lanes, preferred_element_type=jnp.float32)
            parts.append(jnp.where(first, low, high).astype(jnp.bfloat16))
        attended = jnp.concatenate(parts, axis=1)
        mixed = jnp.dot(attended, weight, preferred_element_type=jnp.float32)
        mixed = mixed + block.astype(jnp.float32)
        for k in range(CHUNK_ROWS):
            m = (offset + c) * CHUNK_ROWS + k
            own = mixed[k * length : (k + 1) * length]
            ready[c, pl.ds(k * length, length), :] = (
                own * jnp.broadcast_to(live[0:1, m : m + 1], own.shape)
            ).astype(jnp.bfloat16)
        leavings[c].start()
    for copy in leavings:
        copy.wait()


def back(index, attention, rows, affine, value_weight, weight, row_count, begun):
    vmem = pl.BlockSpec(memory_space=pltpu.VMEM)
    anywhere = pl.BlockSpec(memory_space=pltpu.HBM)
    tokens, width = rows.shape
    chunks = row_count // PARTS // CHUNK_ROWS
    span = tokens // chunks
    return pl.pallas_call(
        functools.partial(back_kernel, index * chunks),
        out_shape=jax.ShapeDtypeStruct((tokens * PARTS, width), jnp.bfloat16),
        in_specs=[vmem, anywhere, vmem, vmem, vmem] + [anywhere] * len(begun),
        out_specs=anywhere,
        scratch_shapes=[
            pltpu.VMEM((chunks, span, width), jnp.bfloat16),
            pltpu.VMEM((chunks, span, width), jnp.bfloat16),
            pltpu.SemaphoreType.DMA((chunks,)),
            pltpu.SemaphoreType.DMA((chunks,)),
        ],
        input_output_aliases={5: 0} if begun else {},
        compiler_params=pltpu.CompilerParams(vmem_limit_bytes=40 << 20),
        name="back",
        interpret=INTERPRET,
    )(attention, rows, affine, value_weight, weight, *begun)


def shifted(value, axis, steps, wrap):
    count = lax.axis_size(axis)
    if wrap:
        route = [(i, (i + steps) % count) for i in range(count)]
    else:
        route = [(i, i + steps) for i in range(count) if 0 <= i + steps < count]
    return lax.ppermute(value, axis, route)


ROUTE = ((11, 9, 6, 4), (10, 5), 12)
Z_STAY = 8
RING_Z = 8
RING_X = 4


def plan_kernel(
    position_ref, groups_ref, targets_ref, weight_ref, table_ref, meta_ref, cut_ref, held, sem
):
    width = held.shape[0]
    load = pltpu.make_async_copy(weight_ref.at[:, pl.ds(2 * width, width)], held, sem.at[0])
    store = pltpu.make_async_copy(held, cut_ref, sem.at[1])
    load.start()
    peers, row_count = targets_ref.shape
    pair_count = row_count // 2
    position = position_ref[0]
    shape = (peers, 128)
    down = lax.broadcasted_iota(jnp.int32, shape, 0)
    across = lax.broadcasted_iota(jnp.int32, shape, 1)
    zero = jnp.zeros(shape, jnp.int32)

    def over_lanes(value):
        return jnp.broadcast_to(jnp.sum(value, axis=1, keepdims=True), shape)

    def over_rows(value):
        return jnp.broadcast_to(jnp.sum(value, axis=0, keepdims=True), shape)

    def top_rows(value):
        return jnp.max(value, axis=0, keepdims=True)

    def flag(condition):
        return jnp.where(condition, 1, zero)

    def to_lanes(value):
        return over_rows(jnp.where(down == across, value, zero))

    def to_rows(value):
        return over_lanes(jnp.where(down == across, value, zero))

    load.wait()
    store.start()
    targets = jnp.concatenate(
        [targets_ref[...], jnp.full((peers, 128 - row_count), -1, jnp.int32)], axis=1
    )
    device = targets >> 5
    offset = jnp.where(targets >= 0, (device - down) & (peers - 1), -1)
    seen = zero
    for i in range(row_count):
        seen = seen | flag(jnp.broadcast_to(offset[:, i : i + 1], shape) == across)
    present_l = flag(over_rows(seen) > 0)
    present = to_rows(present_l)
    odd = down & 1
    odd_l = across & 1

    def turns(core):
        step = ((down + odd * (1 - 2 * core)) >> 1) & 31
        step_l = ((across + odd_l * (1 - 2 * core)) >> 1) & 31
        u, u_l = step & 7, step_l & 7
        order = u * 64 + down
        order_l = u_l * 64 + across
        moving = present * flag(u > 0)
        moving_l = present_l * flag(u_l > 0)
        rank = over_lanes(moving_l * flag(order_l < order))
        rest = over_lanes((present_l - moving_l) * flag(order_l < order))
        return step >> 3, u, moving, rank, rest

    def split_of(core):
        caps = ROUTE[0]
        _, u, moving, rank, _ = turns(core)
        early = moving * flag(rank < across)
        late = moving - early
        good = flag(across <= pair_count)
        for h in range(1, 6):
            cap = caps[h - 1] if h <= len(caps) else 0
            good = good * flag(over_rows(early * flag(u >= h)) <= cap)
            good = good * flag(over_rows(late * flag(RING_Z - u >= h)) <= cap)
        split = jnp.min(jnp.where(good > 0, across, 127), axis=1, keepdims=True)
        return jnp.broadcast_to(split, shape)

    def z_lanes(core, split):
        (z1, z2, z3, z4) = ROUTE[0]
        _, u, moving, rank, rest = turns(core)
        plus = moving * flag(rank < split)
        staying = present - moving
        hops = jnp.where(plus > 0, u, RING_Z - u)
        place = jnp.where(plus > 0, split - 1 - rank, rank - split)
        base = jnp.where(
            hops == 1, 0, jnp.where(hops == 2, z1, jnp.where(hops == 3, z1 + z2, z1 + z2 + z3))
        )
        side = moving - plus
        z_all = z1 + z2 + z3 + z4
        z_leave = jnp.where(staying > 0, 2 * z1 + rest, side * z1 + place)
        z_land = jnp.where(staying > 0, 2 * z_all + rest, side * z_all + base + place)
        return jnp.where(present > 0, z_leave, -1), jnp.where(present > 0, z_land, -1)

    def x_counts(core, line):
        high, u, _, _, _ = turns(core)
        turn = (high + flag(line < u)) & (RING_X - 1)
        turn = jnp.where(present > 0, turn, -1)
        count = [over_rows(flag(turn == v)) for v in range(RING_X)]
        x2 = ROUTE[1][1]
        ahead = (count[2] + count[3] - count[1] + 1) >> 1
        ahead = jnp.minimum(
            jnp.maximum(ahead, jnp.maximum(count[2] - x2, 0)), jnp.minimum(count[2], x2)
        )
        return turn, count, ahead

    def fits(core):
        x1, x2 = ROUTE[1]
        _, count, ahead = x_counts(core, across)
        behind = count[2] - ahead
        good = (
            flag(ahead <= x2)
            * flag(behind <= x2)
            * flag(ahead + count[1] <= x1)
            * flag(behind + count[3] <= x1)
            * flag(count[0] <= ROUTE[2])
        )
        return jnp.min(jnp.where(across < RING_Z, good, 1))

    def x_lanes(core, line):
        x1, x2 = ROUTE[1]
        turn, count, ahead = x_counts(core, line)
        turn_l = to_lanes(turn)
        level = over_lanes(present_l * flag(turn_l == turn) * flag(across < down))
        double = flag(turn == 2)
        near = double * flag(level < ahead)
        forward = flag(turn == 1) + near
        spot = jnp.where(
            double > 0,
            level - jnp.where(near > 0, 0, ahead),
            level + jnp.where(turn == 1, ahead, count[2] - ahead),
        )
        side = 1 - forward
        x_leave = jnp.where(turn == 0, 2 * x1 + level, side * x1 + spot)
        x_land = jnp.where(
            turn == 0, 2 * (x1 + x2) + level, side * (x1 + x2) + double * x1 + spot
        )
        return jnp.where(present > 0, x_leave, -1), jnp.where(present > 0, x_land, -1)

    core = position & 1
    split = split_of(core)
    z_leave, z_land = z_lanes(core, split)
    line = (position >> 1) & (RING_Z - 1)
    x_leave_a, x_land_a = x_lanes(core, line)
    x_leave_b, x_land_b = x_lanes(core, RING_Z - 1 - line)
    other_split = split_of(1 - core)
    good = jnp.where(
        jnp.max(jnp.maximum(split, other_split)) <= pair_count, fits(core) * fits(1 - core), 0
    )

    lane_row = lax.broadcasted_iota(jnp.int32, (1, 128), 1)
    origin = -1 + zero
    for b in range(2):
        sender = position if b == 0 else position ^ 1
        mine = targets_ref[pl.ds(sender, 1), :]
        mine = jnp.concatenate([mine, jnp.full((1, 128 - row_count), -1, jnp.int32)], axis=1)
        away = ((mine >> 5) - sender) & (peers - 1)
        away = jnp.where(mine >= 0, away, -1)
        away = jnp.where((away & 1) == b, away, -1)
        hit = jnp.broadcast_to(away, shape) == down
        code = b * pair_count + (jnp.broadcast_to(lane_row, shape) >> 1)
        found = jnp.max(jnp.where(hit, code, -1), axis=1, keepdims=True)
        origin = jnp.maximum(origin, jnp.broadcast_to(found, shape))

    def gathered(slot_of, value):
        return top_rows(jnp.where(slot_of == across, value, -1))

    local = targets - position * row_count
    here = jnp.logical_and(local >= 0, local < row_count)
    settled_a = jnp.full((1, 128), -1, jnp.int32)
    settled_b = settled_a
    lane_full = across & 1
    for r in range(2):
        slot = jnp.max(
            jnp.where(jnp.logical_and(here, lane_full == r), local, -1), axis=1, keepdims=True
        )
        slot = jnp.broadcast_to(slot, shape)
        slot_l = over_rows(jnp.where(down == across, slot + 1, zero)) - 1
        match = across == ((position - down) & (peers - 1))
        slot_by_offset = over_lanes(jnp.where(match, slot_l + 1, zero)) - 1
        settled_a = jnp.maximum(settled_a, gathered(slot_by_offset, x_land_a * 2 + r))
        settled_b = jnp.maximum(settled_b, gathered(slot_by_offset, z_land * 2 + r))
    empty = jnp.full((1, 128), -1, jnp.int32)
    table_ref[...] = jnp.concatenate(
        [
            gathered(z_leave, origin),
            gathered(x_leave_b, origin),
            gathered(x_leave_a, z_land),
            gathered(z_leave, x_land_b),
            settled_a,
            settled_b,
            empty,
            empty,
        ],
        axis=0,
    )
    groups = groups_ref[...]
    lane = lax.broadcasted_iota(jnp.int32, groups.shape, 1)
    own_group = jnp.sum(jnp.where(lane == position, groups, 0))
    low = jnp.sum(jnp.where(groups < own_group, 1, 0))
    high = low + jnp.sum(jnp.where(groups == own_group, 1, 0))
    inside = jnp.logical_and(targets >= low * row_count, targets < high * row_count)
    meta_ref[0] = position
    meta_ref[1] = low
    meta_ref[2] = high
    meta_ref[3] = jnp.sum(jnp.where(inside, 1, 0))
    meta_ref[4] = good
    store.wait()


def plan(position, groups, targets, weight):
    width = weight.shape[0]
    vmem = pl.BlockSpec(memory_space=pltpu.VMEM)
    smem = pl.BlockSpec(memory_space=pltpu.SMEM)
    return pl.pallas_call(
        plan_kernel,
        out_shape=(
            jax.ShapeDtypeStruct((8, 128), jnp.int32),
            jax.ShapeDtypeStruct((8,), jnp.int32),
            jax.ShapeDtypeStruct((width, width), weight.dtype),
        ),
        in_specs=[smem, vmem, vmem, pl.BlockSpec(memory_space=pltpu.HBM)],
        out_specs=(vmem, smem, pl.BlockSpec(memory_space=pltpu.HBM)),
        scratch_shapes=[
            pltpu.VMEM((width, width), weight.dtype),
            pltpu.SemaphoreType.DMA((2,)),
        ],
        name="plan",
        interpret=INTERPRET,
    )(position.reshape(1), groups, targets, weight)


def deal(table_ref, row, pool, outs):
    lane = 0
    for out in outs:

        def step(k, carry, out=out, lane=lane):
            out[k] = pool[jnp.maximum(table_ref[row, lane + k], 0)]
            return carry

        lax.fori_loop(0, out.shape[0], step, 0)
        lane += out.shape[0]


def leave_kernel(table_ref, own_ref, partner_ref, *refs):
    outs, (pool, sem) = refs[:-2], refs[-2:]
    pairs = own_ref.shape[0]
    half = own_ref.shape[2] // 2
    copies = []
    for part in range(2):
        for b, ref in enumerate((own_ref, partner_ref)):
            copies.append(
                pltpu.make_async_copy(
                    ref.at[:, :, pl.ds(part * half, half), :],
                    pool.at[part, pl.ds(b * pairs, pairs)],
                    sem.at[len(copies)],
                )
            )
    for copy in copies:
        copy.start()
    for part in range(2):
        copies[2 * part].wait()
        copies[2 * part + 1].wait()
        deal(table_ref, part, pool.at[part], outs[3 * part : 3 * part + 3])


def leave(table, own, partner, route):
    (z1, _, _, _), (x1, _), x_stay = route
    pairs, two, length, width = own.shape
    vmem = pl.BlockSpec(memory_space=pltpu.VMEM)
    anywhere = pl.BlockSpec(memory_space=pl.ANY)
    sizes = (z1, z1, Z_STAY, x1, x1, x_stay)
    return pl.pallas_call(
        leave_kernel,
        out_shape=tuple(
            jax.ShapeDtypeStruct((n, two, length // 2, width), own.dtype) for n in sizes
        ),
        in_specs=[pl.BlockSpec(memory_space=pltpu.SMEM), anywhere, anywhere],
        out_specs=(vmem,) * len(sizes),
        scratch_shapes=[
            pltpu.VMEM((2, 2 * pairs, two, length // 2, width), own.dtype),
            pltpu.SemaphoreType.DMA((4,)),
        ],
        compiler_params=pltpu.CompilerParams(vmem_limit_bytes=40 << 20),
        name="leave",
        interpret=INTERPRET,
    )(table, own, partner)


def pooled(refs, pool, sem):
    copies = []
    start = 0
    for ref in refs:
        count = ref.shape[0]
        copies.append(
            pltpu.make_async_copy(ref, pool.at[pl.ds(start, count)], sem.at[len(copies)])
        )
        start += count
    return copies


def turn_kernel(row, count, table_ref, *refs):
    sources, outs, (pool, sem) = refs[:count], refs[count:-2], refs[-2:]
    copies = pooled(sources, pool, sem)
    for copy in copies:
        copy.start()
    for copy in copies:
        copy.wait()
    deal(table_ref, row, pool, outs)


def turn_over(table, row, sources, sizes):
    vmem = pl.BlockSpec(memory_space=pltpu.VMEM)
    anywhere = pl.BlockSpec(memory_space=pl.ANY)
    payload = sources[0].shape[1:]
    return pl.pallas_call(
        functools.partial(turn_kernel, row, len(sources)),
        out_shape=tuple(jax.ShapeDtypeStruct((n,) + payload, sources[0].dtype) for n in sizes),
        in_specs=[pl.BlockSpec(memory_space=pltpu.SMEM)] + [anywhere] * len(sources),
        out_specs=(vmem,) * len(sizes),
        scratch_shapes=[
            pltpu.VMEM((sum(s.shape[0] for s in sources),) + payload, sources[0].dtype),
            pltpu.SemaphoreType.DMA((len(sources),)),
        ],
        compiler_params=pltpu.CompilerParams(vmem_limit_bytes=40 << 20),
        name="turn_over",
        interpret=INTERPRET,
    )(table, *sources)


def land_kernel(count_a, count_b, table_ref, *refs):
    sources_a, sources_b = refs[:count_a], refs[count_a : count_a + count_b]
    outs = refs[count_a + count_b : count_a + count_b + PARTS]
    live_ref, pool_a, pool_b, done, sem_a, sem_b, out_sem = refs[count_a + count_b + PARTS :]
    row_count, length, _ = done.shape
    half = length // 2
    copies = pooled(sources_a, pool_a, sem_a) + pooled(sources_b, pool_b, sem_b)
    for copy in copies:
        copy.start()
    for copy in copies:
        copy.wait()

    def step(m, carry):
        live = table_ref[4, m] >= 0
        live_ref[m] = jnp.where(live, 1, 0)
        for part, pool in ((0, pool_a), (1, pool_b)):
            code = jnp.maximum(table_ref[4 + part, m], 0)
            value = pool[code >> 1, code & 1]
            done[m, pl.ds(part * half, half), :] = jnp.where(live, value, jnp.zeros_like(value))
        return carry

    rows = row_count // PARTS
    leaving = [
        pltpu.make_async_copy(done.at[pl.ds(k * rows, rows)], out, out_sem.at[k])
        for k, out in enumerate(outs)
    ]
    for k in range(PARTS):
        lax.fori_loop(k * rows, (k + 1) * rows, step, 0)
        leaving[k].start()
    for copy in leaving:
        copy.wait()


def land(table, sources_a, sources_b, row_count, length):
    anywhere = pl.BlockSpec(memory_space=pl.ANY)
    smem = pl.BlockSpec(memory_space=pltpu.SMEM)
    two, half, width = sources_a[0].shape[1:]
    dtype = sources_a[0].dtype
    return pl.pallas_call(
        functools.partial(land_kernel, len(sources_a), len(sources_b)),
        out_shape=(jax.ShapeDtypeStruct((row_count // PARTS, length, width), dtype),) * PARTS
        + (jax.ShapeDtypeStruct((row_count,), jnp.int32),),
        in_specs=[smem] + [anywhere] * (len(sources_a) + len(sources_b)),
        out_specs=(pl.BlockSpec(memory_space=pltpu.HBM),) * PARTS + (smem,),
        scratch_shapes=[
            pltpu.VMEM((sum(s.shape[0] for s in sources_a), two, half, width), dtype),
            pltpu.VMEM((sum(s.shape[0] for s in sources_b), two, half, width), dtype),
            pltpu.VMEM((row_count, length, width), dtype),
            pltpu.SemaphoreType.DMA((len(sources_a),)),
            pltpu.SemaphoreType.DMA((len(sources_b),)),
            pltpu.SemaphoreType.DMA((PARTS,)),
        ],
        compiler_params=pltpu.CompilerParams(vmem_limit_bytes=40 << 20),
        name="land",
        interpret=INTERPRET,
    )(table, *sources_a, *sources_b)


def chain(forward, backward, caps, step, ring):
    def moved(i, by):
        return (i // (step * ring)) * step * ring + (i + by * step) % (step * ring)

    devices = range(lax.axis_size("depth"))
    onward, returning = [], []
    for cap in caps:
        forward = lax.ppermute(forward[:cap], "depth", [(i, moved(i, 1)) for i in devices])
        backward = lax.ppermute(backward[:cap], "depth", [(i, moved(i, -1)) for i in devices])
        onward.append(forward)
        returning.append(backward)
    return onward + returning


def routed(route, table, own, partner):
    z_caps, x_caps, x_stay = route
    z_sizes = (z_caps[0], z_caps[0], Z_STAY)
    x_sizes = (x_caps[0], x_caps[0], x_stay)
    z_plus, z_minus, z_still, x_plus, x_minus, x_still = leave(table, own, partner, route)
    along_x = chain(x_plus, x_minus, x_caps, 2 * RING_Z, RING_X)
    along_z = chain(z_plus, z_minus, z_caps, 2, RING_Z)
    later = turn_over(table, 3, along_x + [x_still], z_sizes)
    last_b = chain(later[0], later[1], z_caps, 2, RING_Z)
    turned = turn_over(table, 2, along_z + [z_still], x_sizes)
    last_a = chain(turned[0], turned[1], x_caps, 2 * RING_Z, RING_X)
    return land(
        table,
        last_a + [turned[2]],
        last_b + [later[2]],
        own.shape[0] * own.shape[1],
        own.shape[2],
    )


def dense(targets, everywhere, own):
    row_count = targets.shape[0]
    _, _, length, width = own.shape
    peers = lax.axis_size("depth")
    position = lax.axis_index("depth")
    capacity = max(2, (row_count + peers - 1) // peers)
    slots = jnp.where(
        targets >= 0,
        targets // row_count * capacity + jnp.arange(row_count) % capacity,
        -1,
    )
    outgoing = spread(own.reshape(row_count, length, width), slots, peers * capacity)
    got = lax.all_to_all(
        outgoing.reshape((peers, capacity, length, width)),
        "depth",
        split_axis=0,
        concat_axis=0,
        tiled=True,
    ).reshape(peers * capacity, length, width)
    local = everywhere - position * row_count
    mine = jnp.logical_and(local >= 0, local < row_count)
    code = (
        lax.broadcasted_iota(jnp.int32, (peers, row_count), 0) * capacity
        + lax.broadcasted_iota(jnp.int32, (peers, row_count), 1) % capacity
    )
    wanted = jnp.where(mine, local, -1).reshape(1, -1)
    hit = jnp.arange(row_count)[:, None] == wanted
    source = jnp.max(jnp.where(hit, code.reshape(1, -1), -1), axis=1)
    return (*settle(source, got), (source >= 0).astype(jnp.int32))


def layer(
    alignment_input,
    target_slot,
    device_alignment,
    layer_norm_gain,
    layer_norm_bias,
    query_key_value_weight,
    output_weight,
):
    targets = target_slot[0]
    row_count, length, width = alignment_input.shape[1:]
    peers = lax.axis_size("depth")
    position = lax.axis_index("depth")
    own = alignment_input.reshape(row_count // 2, 2, length, width)
    everywhere = lax.all_to_all(
        jnp.broadcast_to(targets[None, None], (peers, 1, row_count)),
        "depth",
        split_axis=0,
        concat_axis=0,
        tiled=True,
    ).reshape(peers, row_count)
    partner = lax.ppermute(own, "depth", [(i, i ^ 1) for i in range(peers)])
    table, meta, value_part = plan(
        position, device_alignment, everywhere, query_key_value_weight[0]
    )
    value_weight = shifted(value_part, "section", 1, True)
    out_weight = shifted(output_weight[0], "section", 1, True)
    affine = shifted(
        jnp.concatenate([layer_norm_gain, layer_norm_bias], axis=0), "section", 1, True
    )
    *settled, live = lax.switch(
        meta[4],
        [
            lambda t, o, p, a, b: dense(a, b, o),
            lambda t, o, p, a, b: routed(ROUTE, t, o, p),
        ],
        table,
        own,
        partner,
        targets,
        everywhere,
    )
    balanced = [part.reshape(-1, width) for part in settled]
    earlier = [shifted(part, "section", 1, True) for part in balanced]
    tied, tied_low = front(
        live, balanced, layer_norm_gain, layer_norm_bias, query_key_value_weight[0]
    )
    tied, up, down = join(
        meta, tied, shifted(tied_low, "depth", 1, False), shifted(tied_low, "depth", -1, False)
    )
    neighbours = [shifted(up, "depth", 2, False), shifted(down, "depth", -2, False)]
    attention = shifted(middle(live, meta, tied, neighbours), "section", 1, True)
    begun = ()
    for index, rows in enumerate(earlier):
        begun = (
            back(
                index, attention, rows, affine, value_weight, out_weight, row_count, begun
            ),
        )
    return begun[0].reshape(1, row_count, length, width)


def solution(mesh):
    placed = (
        P("section", "depth", None, None),
        P("section", "depth"),
        P("section", None),
        P("section", None),
        P("section", None),
        P("section", None, None),
        P("section", None, None),
    )
    return jax.shard_map(
        layer,
        mesh=mesh,
        in_specs=placed,
        out_specs=P("section", "depth", None, None),
        check_vma=False,
    )
```

```python
import functools

import jax
import jax.numpy as jnp
from jax import lax
from jax.experimental import pallas as pl
from jax.experimental.pallas import tpu as pltpu
from jax.sharding import PartitionSpec as P


H = 12
DH = 64
PAIRS = H // 2
EPSILON = 1e-05
CHUNK_ROWS = 8
PARTS = 2
INTERPRET = False


def spread_kernel(slot_ref, rows_ref, out_ref, sem):
    count = rows_ref.shape[0]

    def copy_of(i):
        return pltpu.make_async_copy(
            rows_ref.at[i], out_ref.at[jnp.maximum(slot_ref[i], 0)], sem.at[i]
        )

    def begin(i, carry):
        @pl.when(slot_ref[i] >= 0)
        def _():
            copy_of(i).start()

        return carry

    def finish(i, carry):
        @pl.when(slot_ref[i] >= 0)
        def _():
            copy_of(i).wait()

        return carry

    lax.fori_loop(0, count, begin, 0)
    lax.fori_loop(0, count, finish, 0)


def spread(rows, slots, slot_count):
    return pl.pallas_call(
        spread_kernel,
        out_shape=jax.ShapeDtypeStruct((slot_count,) + rows.shape[1:], rows.dtype),
        in_specs=[
            pl.BlockSpec(memory_space=pltpu.SMEM),
            pl.BlockSpec(memory_space=pltpu.VMEM),
        ],
        out_specs=pl.BlockSpec(memory_space=pltpu.HBM),
        scratch_shapes=[pltpu.SemaphoreType.DMA((rows.shape[0],))],
        name="spread",
        interpret=INTERPRET,
    )(slots, rows)


def settle_kernel(source_ref, rows_ref, *refs):
    outs, (landed, in_sem, out_sem) = refs[:PARTS], refs[PARTS:]
    row_count = landed.shape[0]
    part = row_count // PARTS

    def arrival(m):
        return pltpu.make_async_copy(
            rows_ref.at[jnp.maximum(source_ref[m], 0)], landed.at[m], in_sem.at[m]
        )

    def begin(m, carry):
        arrival(m).start()
        return carry

    def empty(m, carry):
        arrival(m).wait()

        @pl.when(source_ref[m] < 0)
        def _():
            landed[m] = jnp.zeros_like(landed[m])

        return carry

    lax.fori_loop(0, row_count, begin, 0)
    lax.fori_loop(0, row_count, empty, 0)
    leaving = [
        pltpu.make_async_copy(landed.at[pl.ds(k * part, part)], out, out_sem.at[k])
        for k, out in enumerate(outs)
    ]
    for copy in leaving:
        copy.start()
    for copy in leaving:
        copy.wait()


def settle(source, rows):
    row_count = source.shape[0]
    length, width = rows.shape[1:]
    return pl.pallas_call(
        settle_kernel,
        out_shape=(jax.ShapeDtypeStruct((row_count // PARTS, length, width), rows.dtype),) * PARTS,
        in_specs=[
            pl.BlockSpec(memory_space=pltpu.SMEM),
            pl.BlockSpec(memory_space=pl.ANY),
        ],
        out_specs=(pl.BlockSpec(memory_space=pltpu.HBM),) * PARTS,
        scratch_shapes=[
            pltpu.VMEM((row_count, length, width), rows.dtype),
            pltpu.SemaphoreType.DMA((row_count,)),
            pltpu.SemaphoreType.DMA((PARTS,)),
        ],
        name="settle",
        interpret=INTERPRET,
    )(source, rows)


def lane_mask(shape):
    return lax.broadcasted_iota(jnp.int32, shape, len(shape) - 1) % 128 < DH


def normalized(block, gain, bias):
    widened = block.astype(jnp.float32)
    average = jnp.mean(widened, axis=-1, keepdims=True)
    centred = widened - average
    spread_of = jnp.mean(centred * centred, axis=-1, keepdims=True)
    return (centred * lax.rsqrt(spread_of + EPSILON) * gain + bias).astype(jnp.bfloat16)


def front_kernel(
    live_ref,
    rows_0_ref,
    rows_1_ref,
    gain_ref,
    bias_ref,
    weight_ref,
    tied_ref,
    tied_low_ref,
    landed,
    acc,
    sem,
):
    row_count = live_ref.shape[0]
    width = rows_0_ref.shape[1]
    length = rows_0_ref.shape[0] * PARTS // row_count
    span = CHUNK_ROWS * length
    chunks = row_count // CHUNK_ROWS
    each = chunks // PARTS
    copies = [
        pltpu.make_async_copy(
            (rows_0_ref, rows_1_ref)[c // each].at[pl.ds(c % each * span, span), :],
            landed.at[c],
            sem.at[c],
        )
        for c in range(chunks)
    ]
    for copy in copies:
        copy.start()
    gain = gain_ref[...]
    bias = bias_ref[...]
    weight = weight_ref[:, : 2 * width]
    first = lane_mask((length, 256))
    acc[...] = jnp.zeros_like(acc)

    def step(c, carry):
        pltpu.make_async_copy(rows_0_ref.at[pl.ds(0, span), :], landed.at[c], sem.at[c]).wait()
        start = c * CHUNK_ROWS
        normed = normalized(landed[c], gain, bias)
        packed = jnp.dot(normed, weight, preferred_element_type=jnp.float32).astype(jnp.bfloat16)
        for pair in range(PAIRS):
            lanes = slice(pair * 128, pair * 128 + 128)
            key_lanes = slice(width + pair * 128, width + pair * 128 + 128)
            total = None
            for r in range(0, CHUNK_ROWS, 2):
                query_parts = []
                key_parts = []
                for k in (r, r + 1):
                    own = slice(k * length, (k + 1) * length)
                    query = packed[own, lanes]
                    query_parts.append(
                        jnp.where(live_ref[start + k] > 0, query, jnp.zeros_like(query))
                    )
                    key_parts.append(packed[own, key_lanes])
                query = jnp.concatenate(query_parts, axis=1)
                key = jnp.concatenate(key_parts, axis=1)
                zero = jnp.zeros_like(query)
                both = jnp.concatenate(
                    [jnp.where(first, query, zero), jnp.where(first, zero, query)], axis=0
                )
                part = lax.dot_general(
                    both, key, (((1,), (1,)), ((), ())), preferred_element_type=jnp.float32
                )
                total = part if total is None else total + part
            acc[pl.ds(pair * 2 * length, 2 * length), :] += total
        return carry

    lax.fori_loop(0, chunks, step, 0)
    quarter = H * length // 4
    tied = jnp.concatenate([acc[pl.ds(q * quarter, quarter), :] for q in range(4)], axis=1)
    tied_ref[...] = tied
    tied_low_ref[...] = tied.astype(jnp.bfloat16)


def front(live, rows, gain, bias, weight):
    row_count = live.shape[0]
    width = rows[0].shape[1]
    length = rows[0].shape[0] * PARTS // row_count
    quarter = H * length // 4
    vmem = pl.BlockSpec(memory_space=pltpu.VMEM)
    smem = pl.BlockSpec(memory_space=pltpu.SMEM)
    return pl.pallas_call(
        front_kernel,
        out_shape=(
            jax.ShapeDtypeStruct((quarter, 4 * length), jnp.float32),
            jax.ShapeDtypeStruct((quarter, 4 * length), jnp.bfloat16),
        ),
        in_specs=[smem] + [pl.BlockSpec(memory_space=pltpu.HBM)] * PARTS + [vmem, vmem, vmem],
        out_specs=(vmem, vmem),
        scratch_shapes=[
            pltpu.VMEM((row_count // CHUNK_ROWS, CHUNK_ROWS * length, width), jnp.bfloat16),
            pltpu.VMEM((H * length, length), jnp.float32),
            pltpu.SemaphoreType.DMA((row_count // CHUNK_ROWS,)),
        ],
        compiler_params=pltpu.CompilerParams(vmem_limit_bytes=40 << 20),
        name="front",
        interpret=INTERPRET,
    )(live, *rows, gain, bias, weight)


def belongs(meta_ref, step):
    other = meta_ref[0] + step
    return jnp.logical_and(other >= meta_ref[1], other < meta_ref[2])


def join_kernel(meta_ref, tied_ref, below_ref, above_ref, sum_ref, up_ref, down_ref):
    tied = tied_ref[...]
    below = jnp.where(belongs(meta_ref, -1), below_ref[...].astype(jnp.float32), 0.0)
    above = jnp.where(belongs(meta_ref, 1), above_ref[...].astype(jnp.float32), 0.0)
    sum_ref[...] = tied + below + above
    up_ref[...] = (tied + below).astype(jnp.bfloat16)
    down_ref[...] = (tied + above).astype(jnp.bfloat16)


def join(meta, tied, below, above):
    vmem = pl.BlockSpec(memory_space=pltpu.VMEM)
    return pl.pallas_call(
        join_kernel,
        out_shape=(
            jax.ShapeDtypeStruct(tied.shape, jnp.float32),
            jax.ShapeDtypeStruct(tied.shape, jnp.bfloat16),
            jax.ShapeDtypeStruct(tied.shape, jnp.bfloat16),
        ),
        in_specs=[pl.BlockSpec(memory_space=pltpu.SMEM), vmem, vmem, vmem],
        out_specs=(vmem, vmem, vmem),
        name="join",
        interpret=INTERPRET,
    )(meta, tied, below, above)


def middle_kernel(live_ref, meta_ref, tied_ref, below_ref, above_ref, out_ref):
    length = tied_ref.shape[1] // 4
    tied = tied_ref[...]
    tied = tied + jnp.where(belongs(meta_ref, -2), below_ref[...].astype(jnp.float32), 0.0)
    tied = tied + jnp.where(belongs(meta_ref, 2), above_ref[...].astype(jnp.float32), 0.0)
    quarter = tied.shape[0]
    count = jnp.full((1, length), meta_ref[3], jnp.int32).astype(jnp.float32)
    scale = DH ** (-0.5) / jnp.sqrt(count)
    logits = (
        jnp.concatenate([tied[:, q * length : (q + 1) * length] for q in range(4)], axis=0) * scale
    )
    top = jnp.max(logits, axis=-1, keepdims=True)
    raised = jnp.exp(logits - top)
    attention = raised / jnp.sum(raised, axis=-1, keepdims=True)
    out_ref[pl.ds(0, quarter), :] = jnp.concatenate(
        [attention[q * quarter : (q + 1) * quarter] for q in range(4)], axis=1
    ).astype(jnp.bfloat16)
    lane = lax.broadcasted_iota(jnp.int32, (16, 4 * length), 1)
    live = jnp.zeros((16, 4 * length), jnp.float32)
    for m in range(live_ref.shape[0]):
        live = jnp.where(jnp.logical_and(lane == m, live_ref[m] > 0), 1.0, live)
    out_ref[pl.ds(quarter, 16), :] = live.astype(jnp.bfloat16)


def middle(live, meta, tied, neighbours):
    vmem = pl.BlockSpec(memory_space=pltpu.VMEM)
    smem = pl.BlockSpec(memory_space=pltpu.SMEM)
    return pl.pallas_call(
        middle_kernel,
        out_shape=jax.ShapeDtypeStruct((tied.shape[0] + 16, tied.shape[1]), jnp.bfloat16),
        in_specs=[smem, smem] + [vmem] * (1 + len(neighbours)),
        out_specs=vmem,
        name="middle",
        interpret=INTERPRET,
    )(live, meta, tied, *neighbours)


def back_kernel(offset, attention_ref, rows_ref, bundle_ref, *refs):
    out_ref, landed, ready, mask, in_sem, out_sem = refs[-6:]
    chunks = landed.shape[0]
    span, width = landed.shape[1:]
    length = span // CHUNK_ROWS
    quarter = H * length // 4

    def arrival(c):
        return pltpu.make_async_copy(
            rows_ref.at[pl.ds(c * span, span), :], landed.at[c], in_sem.at[c]
        )

    def leaving(c):
        return pltpu.make_async_copy(
            ready.at[c], out_ref.at[pl.ds((offset + c) * span, span), :], out_sem.at[c]
        )

    for c in range(chunks):
        arrival(c).start()
    packed = attention_ref[pl.ds(0, quarter), :]
    attention = jnp.concatenate(
        [packed[:, q * length : (q + 1) * length] for q in range(4)], axis=0
    )
    live = attention_ref[pl.ds(quarter, 16), :].astype(jnp.float32)
    for c in range(chunks):
        for k in range(CHUNK_ROWS):
            m = (offset + c) * CHUNK_ROWS + k
            mask[c, pl.ds(k * length, length), :] = jnp.broadcast_to(
                live[0:1, m : m + 1], (length, 128)
            )
    wide = jnp.concatenate([attention] * CHUNK_ROWS, axis=1)
    diagonal = (
        lax.broadcasted_iota(jnp.int32, (span, span), 0) // length
        == lax.broadcasted_iota(jnp.int32, (span, span), 1) // length
    )
    first = lane_mask((span, 128))
    mixers = []
    for h in range(H):
        tall = jnp.concatenate([wide[h * length : (h + 1) * length]] * CHUNK_ROWS, axis=0)
        mixers.append(jnp.where(diagonal, tall, jnp.zeros_like(tall)))
    affine = bundle_ref[pl.ds(2 * width, 16), :].astype(jnp.float32)
    gain = (affine[0:1] + affine[1:2]) + affine[2:3]
    bias = (affine[3:4] + affine[4:5]) + affine[5:6]
    value_weight = bundle_ref[pl.ds(0, width), :]
    weight = bundle_ref[pl.ds(width, width), :]

    def step(c, carry):
        arrival(c).wait()
        block = landed[c]
        values = jnp.dot(
            normalized(block, gain, bias), value_weight, preferred_element_type=jnp.float32
        ).astype(jnp.bfloat16)
        parts = []
        for pair in range(PAIRS):
            lanes = values[:, pair * 128 : pair * 128 + 128]
            low = jnp.dot(mixers[2 * pair], lanes, preferred_element_type=jnp.float32)
            high = jnp.dot(mixers[2 * pair + 1], lanes, preferred_element_type=jnp.float32)
            parts.append(jnp.where(first, low, high).astype(jnp.bfloat16))
        attended = jnp.concatenate(parts, axis=1)
        mixed = jnp.dot(attended, weight, preferred_element_type=jnp.float32)
        mixed = mixed + block.astype(jnp.float32)
        ready[c] = (mixed * jnp.concatenate([mask[c]] * (width // 128), axis=1)).astype(
            jnp.bfloat16
        )
        leaving(c).start()
        return carry

    lax.fori_loop(0, chunks, step, 0)
    for c in range(chunks):
        leaving(c).wait()


def back(index, attention, rows, bundled, row_count, begun):
    vmem = pl.BlockSpec(memory_space=pltpu.VMEM)
    anywhere = pl.BlockSpec(memory_space=pltpu.HBM)
    tokens, width = rows.shape
    chunks = row_count // PARTS // CHUNK_ROWS
    span = tokens // chunks
    return pl.pallas_call(
        functools.partial(back_kernel, index * chunks),
        out_shape=jax.ShapeDtypeStruct((tokens * PARTS, width), jnp.bfloat16),
        in_specs=[vmem, anywhere, vmem] + [anywhere] * len(begun),
        out_specs=anywhere,
        scratch_shapes=[
            pltpu.VMEM((chunks, span, width), jnp.bfloat16),
            pltpu.VMEM((chunks, span, width), jnp.bfloat16),
            pltpu.VMEM((chunks, span, 128), jnp.float32),
            pltpu.SemaphoreType.DMA((chunks,)),
            pltpu.SemaphoreType.DMA((chunks,)),
        ],
        input_output_aliases={3: 0} if begun else {},
        compiler_params=pltpu.CompilerParams(vmem_limit_bytes=40 << 20),
        name="back",
        interpret=INTERPRET,
    )(attention, rows, bundled, *begun)


def shifted(value, axis, steps, wrap):
    count = lax.axis_size(axis)
    if wrap:
        route = [(i, (i + steps) % count) for i in range(count)]
    else:
        route = [(i, i + steps) for i in range(count) if 0 <= i + steps < count]
    return lax.ppermute(value, axis, route)


ROUTE = ((11, 9, 6, 4), (10, 5), 12)
Z_STAY = 8
RING_Z = 8
RING_X = 4


def plan_kernel(
    position_ref, groups_ref, targets_ref, partner_ref, table_ref, meta_ref, pick_ref
):
    peers, row_count = targets_ref.shape
    pair_count = row_count // 2
    position = position_ref[0]
    shape = (peers, 128)
    down = lax.broadcasted_iota(jnp.int32, shape, 0)
    across = lax.broadcasted_iota(jnp.int32, shape, 1)
    zero = jnp.zeros(shape, jnp.int32)

    def over_lanes(value):
        return jnp.broadcast_to(jnp.sum(value, axis=1, keepdims=True), shape)

    def over_rows(value):
        return jnp.broadcast_to(jnp.sum(value, axis=0, keepdims=True), shape)

    def top_rows(value):
        return jnp.max(value, axis=0, keepdims=True)

    def flag(condition):
        return jnp.where(condition, 1, zero)

    def to_lanes(value):
        return over_rows(jnp.where(down == across, value, zero))

    def to_rows(value):
        return over_lanes(jnp.where(down == across, value, zero))

    targets = jnp.concatenate(
        [targets_ref[...], jnp.full((peers, 128 - row_count), -1, jnp.int32)], axis=1
    )
    device = targets >> 5
    offset = jnp.where(targets >= 0, (device - down) & (peers - 1), -1)
    seen = zero
    for i in range(row_count):
        seen = seen | flag(jnp.broadcast_to(offset[:, i : i + 1], shape) == across)
    present_l = flag(over_rows(seen) > 0)
    present = to_rows(present_l)
    odd = down & 1
    odd_l = across & 1

    def turns(core):
        step = ((down + odd * (1 - 2 * core)) >> 1) & 31
        step_l = ((across + odd_l * (1 - 2 * core)) >> 1) & 31
        u, u_l = step & 7, step_l & 7
        order = u * 64 + down
        order_l = u_l * 64 + across
        moving = present * flag(u > 0)
        moving_l = present_l * flag(u_l > 0)
        rank = over_lanes(moving_l * flag(order_l < order))
        rest = over_lanes((present_l - moving_l) * flag(order_l < order))
        return step >> 3, u, moving, rank, rest

    def split_of(core):
        caps = ROUTE[0]
        _, u, moving, rank, _ = turns(core)
        early = moving * flag(rank < across)
        late = moving - early
        good = flag(across <= pair_count)
        for h in range(1, 6):
            cap = caps[h - 1] if h <= len(caps) else 0
            good = good * flag(over_rows(early * flag(u >= h)) <= cap)
            good = good * flag(over_rows(late * flag(RING_Z - u >= h)) <= cap)
        split = jnp.min(jnp.where(good > 0, across, 127), axis=1, keepdims=True)
        return jnp.broadcast_to(split, shape)

    def z_lanes(core, split):
        (z1, z2, z3, z4) = ROUTE[0]
        _, u, moving, rank, rest = turns(core)
        plus = moving * flag(rank < split)
        staying = present - moving
        hops = jnp.where(plus > 0, u, RING_Z - u)
        place = jnp.where(plus > 0, split - 1 - rank, rank - split)
        base = jnp.where(
            hops == 1, 0, jnp.where(hops == 2, z1, jnp.where(hops == 3, z1 + z2, z1 + z2 + z3))
        )
        side = moving - plus
        z_all = z1 + z2 + z3 + z4
        z_leave = jnp.where(staying > 0, 2 * z1 + rest, side * z1 + place)
        z_land = jnp.where(staying > 0, 2 * z_all + rest, side * z_all + base + place)
        return jnp.where(present > 0, z_leave, -1), jnp.where(present > 0, z_land, -1)

    def x_counts(core, line):
        high, u, _, _, _ = turns(core)
        turn = (high + flag(line < u)) & (RING_X - 1)
        turn = jnp.where(present > 0, turn, -1)
        count = [over_rows(flag(turn == v)) for v in range(RING_X)]
        x2 = ROUTE[1][1]
        ahead = (count[2] + count[3] - count[1] + 1) >> 1
        ahead = jnp.minimum(
            jnp.maximum(ahead, jnp.maximum(count[2] - x2, 0)), jnp.minimum(count[2], x2)
        )
        return turn, count, ahead

    def fits(core):
        x1, x2 = ROUTE[1]
        _, count, ahead = x_counts(core, across)
        behind = count[2] - ahead
        good = (
            flag(ahead <= x2)
            * flag(behind <= x2)
            * flag(ahead + count[1] <= x1)
            * flag(behind + count[3] <= x1)
            * flag(count[0] <= ROUTE[2])
        )
        return jnp.min(jnp.where(across < RING_Z, good, 1))

    def x_lanes(core, line):
        x1, x2 = ROUTE[1]
        turn, count, ahead = x_counts(core, line)
        turn_l = to_lanes(turn)
        level = over_lanes(present_l * flag(turn_l == turn) * flag(across < down))
        double = flag(turn == 2)
        near = double * flag(level < ahead)
        forward = flag(turn == 1) + near
        spot = jnp.where(
            double > 0,
            level - jnp.where(near > 0, 0, ahead),
            level + jnp.where(turn == 1, ahead, count[2] - ahead),
        )
        side = 1 - forward
        x_leave = jnp.where(turn == 0, 2 * x1 + level, side * x1 + spot)
        x_land = jnp.where(
            turn == 0, 2 * (x1 + x2) + level, side * (x1 + x2) + double * x1 + spot
        )
        return jnp.where(present > 0, x_leave, -1), jnp.where(present > 0, x_land, -1)

    core = position & 1
    split = split_of(core)
    z_leave, z_land = z_lanes(core, split)
    line = (position >> 1) & (RING_Z - 1)
    x_leave_a, x_land_a = x_lanes(core, line)
    x_leave_b, x_land_b = x_lanes(core, RING_Z - 1 - line)
    other_split = split_of(1 - core)
    good = jnp.where(
        jnp.max(jnp.maximum(split, other_split)) <= pair_count, fits(core) * fits(1 - core), 0
    )

    lane_row = lax.broadcasted_iota(jnp.int32, (1, 128), 1)
    origin = -1 + zero
    for b in range(2):
        sender = position if b == 0 else position ^ 1
        mine = targets_ref[pl.ds(sender, 1), :]
        mine = jnp.concatenate([mine, jnp.full((1, 128 - row_count), -1, jnp.int32)], axis=1)
        away = ((mine >> 5) - sender) & (peers - 1)
        away = jnp.where(mine >= 0, away, -1)
        away = jnp.where((away & 1) == b, away, -1)
        hit = jnp.broadcast_to(away, shape) == down
        code = b * pair_count + (jnp.broadcast_to(lane_row, shape) >> 1)
        found = jnp.max(jnp.where(hit, code, -1), axis=1, keepdims=True)
        origin = jnp.maximum(origin, jnp.broadcast_to(found, shape))

    def gathered(slot_of, value):
        return top_rows(jnp.where(slot_of == across, value, -1))

    local = targets - position * row_count
    here = jnp.logical_and(local >= 0, local < row_count)
    settled_a = jnp.full((1, 128), -1, jnp.int32)
    settled_b = settled_a
    lane_full = across & 1
    for r in range(2):
        slot = jnp.max(
            jnp.where(jnp.logical_and(here, lane_full == r), local, -1), axis=1, keepdims=True
        )
        slot = jnp.broadcast_to(slot, shape)
        slot_l = over_rows(jnp.where(down == across, slot + 1, zero)) - 1
        match = across == ((position - down) & (peers - 1))
        slot_by_offset = over_lanes(jnp.where(match, slot_l + 1, zero)) - 1
        settled_a = jnp.maximum(settled_a, gathered(slot_by_offset, x_land_a * 2 + r))
        settled_b = jnp.maximum(settled_b, gathered(slot_by_offset, z_land * 2 + r))
    empty = jnp.full((1, 128), -1, jnp.int32)
    table_ref[...] = jnp.concatenate(
        [
            gathered(z_leave, origin),
            gathered(x_leave_b, origin),
            gathered(x_leave_a, z_land),
            gathered(z_leave, x_land_b),
            settled_a,
            settled_b,
            empty,
            empty,
        ],
        axis=0,
    )
    groups = groups_ref[...]
    lane = lax.broadcasted_iota(jnp.int32, groups.shape, 1)
    own_group = jnp.sum(jnp.where(lane == position, groups, 0))
    low = jnp.sum(jnp.where(groups < own_group, 1, 0))
    high = low + jnp.sum(jnp.where(groups == own_group, 1, 0))
    inside = jnp.logical_and(targets >= low * row_count, targets < high * row_count)
    meta_ref[0] = position
    meta_ref[1] = low
    meta_ref[2] = high
    meta_ref[3] = jnp.sum(jnp.where(inside, 1, 0))
    pick_ref[0] = good


def plan(position, groups, targets, partner):
    vmem = pl.BlockSpec(memory_space=pltpu.VMEM)
    smem = pl.BlockSpec(memory_space=pltpu.SMEM)
    return pl.pallas_call(
        plan_kernel,
        out_shape=(
            jax.ShapeDtypeStruct((8, 128), jnp.int32),
            jax.ShapeDtypeStruct((4,), jnp.int32),
            jax.ShapeDtypeStruct((1,), jnp.int32),
        ),
        in_specs=[smem, vmem, vmem, pl.BlockSpec(memory_space=pltpu.HBM)],
        out_specs=(vmem, smem, smem),
        name="plan",
        interpret=INTERPRET,
    )(position.reshape(1), groups, targets, partner)


def pieces(value):
    parts = []
    for _ in range(3):
        part = value.astype(jnp.bfloat16)
        parts.append(part.astype(jnp.float32))
        value = value - parts[-1]
    return parts


def bundle_kernel(weight_ref, out_weight_ref, gain_ref, bias_ref, out_ref, held, sem):
    width = held.shape[1]
    loads = [
        pltpu.make_async_copy(
            weight_ref.at[:, pl.ds(2 * width, width)], held.at[pl.ds(0, width), :], sem.at[0]
        ),
        pltpu.make_async_copy(out_weight_ref, held.at[pl.ds(width, width), :], sem.at[1]),
    ]
    for load in loads:
        load.start()
    rows = pieces(gain_ref[...]) + pieces(bias_ref[...])
    rows.append(jnp.zeros((16 - len(rows), width), jnp.float32))
    held[pl.ds(2 * width, 16), :] = jnp.concatenate(rows, axis=0).astype(jnp.bfloat16)
    for load in loads:
        load.wait()
    store = pltpu.make_async_copy(held, out_ref, sem.at[2])
    store.start()
    store.wait()


def bundle(weight, out_weight, gain, bias):
    width = weight.shape[0]
    vmem = pl.BlockSpec(memory_space=pltpu.VMEM)
    hbm = pl.BlockSpec(memory_space=pltpu.HBM)
    shape = (2 * width + 16, width)
    return pl.pallas_call(
        bundle_kernel,
        out_shape=jax.ShapeDtypeStruct(shape, weight.dtype),
        in_specs=[hbm, hbm, vmem, vmem],
        out_specs=hbm,
        scratch_shapes=[pltpu.VMEM(shape, weight.dtype), pltpu.SemaphoreType.DMA((3,))],
        name="bundle",
        interpret=INTERPRET,
    )(weight, out_weight, gain, bias)


def deal(table_ref, row, pool, outs):
    lane = 0
    for out in outs:

        def step(k, carry, out=out, lane=lane):
            out[k] = pool[jnp.maximum(table_ref[row, lane + k], 0)]
            return carry

        lax.fori_loop(0, out.shape[0], step, 0)
        lane += out.shape[0]


def leave_kernel(table_ref, own_ref, partner_ref, *refs):
    outs, (pool, sem) = refs[:-2], refs[-2:]
    pairs = own_ref.shape[0]
    half = own_ref.shape[2] // 2
    copies = []
    for part in range(2):
        for b, ref in enumerate((own_ref, partner_ref)):
            copies.append(
                pltpu.make_async_copy(
                    ref.at[:, :, pl.ds(part * half, half), :],
                    pool.at[part, pl.ds(b * pairs, pairs)],
                    sem.at[len(copies)],
                )
            )
    for copy in copies:
        copy.start()
    for part in range(2):
        copies[2 * part].wait()
        copies[2 * part + 1].wait()
        deal(table_ref, part, pool.at[part], outs[3 * part : 3 * part + 3])


def leave(table, own, partner, route):
    (z1, _, _, _), (x1, _), x_stay = route
    pairs, two, length, width = own.shape
    vmem = pl.BlockSpec(memory_space=pltpu.VMEM)
    anywhere = pl.BlockSpec(memory_space=pl.ANY)
    sizes = (z1, z1, Z_STAY, x1, x1, x_stay)
    return pl.pallas_call(
        leave_kernel,
        out_shape=tuple(
            jax.ShapeDtypeStruct((n, two, length // 2, width), own.dtype) for n in sizes
        ),
        in_specs=[pl.BlockSpec(memory_space=pltpu.SMEM), anywhere, anywhere],
        out_specs=(vmem,) * len(sizes),
        scratch_shapes=[
            pltpu.VMEM((2, 2 * pairs, two, length // 2, width), own.dtype),
            pltpu.SemaphoreType.DMA((4,)),
        ],
        compiler_params=pltpu.CompilerParams(vmem_limit_bytes=40 << 20),
        name="leave",
        interpret=INTERPRET,
    )(table, own, partner)


def pooled(refs, pool, sem):
    copies = []
    start = 0
    for ref in refs:
        count = ref.shape[0]
        copies.append(
            pltpu.make_async_copy(ref, pool.at[pl.ds(start, count)], sem.at[len(copies)])
        )
        start += count
    return copies


def turn_kernel(row, count, table_ref, *refs):
    sources, outs, (pool, sem) = refs[:count], refs[count:-2], refs[-2:]
    copies = pooled(sources, pool, sem)
    for copy in copies:
        copy.start()
    for copy in copies:
        copy.wait()
    deal(table_ref, row, pool, outs)


def turn_over(table, row, sources, sizes):
    vmem = pl.BlockSpec(memory_space=pltpu.VMEM)
    anywhere = pl.BlockSpec(memory_space=pl.ANY)
    payload = sources[0].shape[1:]
    return pl.pallas_call(
        functools.partial(turn_kernel, row, len(sources)),
        out_shape=tuple(jax.ShapeDtypeStruct((n,) + payload, sources[0].dtype) for n in sizes),
        in_specs=[pl.BlockSpec(memory_space=pltpu.SMEM)] + [anywhere] * len(sources),
        out_specs=(vmem,) * len(sizes),
        scratch_shapes=[
            pltpu.VMEM((sum(s.shape[0] for s in sources),) + payload, sources[0].dtype),
            pltpu.SemaphoreType.DMA((len(sources),)),
        ],
        compiler_params=pltpu.CompilerParams(vmem_limit_bytes=40 << 20),
        name="turn_over",
        interpret=INTERPRET,
    )(table, *sources)


def land_kernel(count_a, count_b, table_ref, *refs):
    sources_a, sources_b = refs[:count_a], refs[count_a : count_a + count_b]
    outs = refs[count_a + count_b : count_a + count_b + PARTS]
    live_ref, pool_a, pool_b, done, sem_a, sem_b, out_sem = refs[count_a + count_b + PARTS :]
    row_count, length, _ = done.shape
    half = length // 2
    copies = pooled(sources_a, pool_a, sem_a) + pooled(sources_b, pool_b, sem_b)
    for copy in copies:
        copy.start()
    for copy in copies:
        copy.wait()

    def step(m, carry):
        live = table_ref[4, m] >= 0
        live_ref[m] = jnp.where(live, 1, 0)
        for part, pool in ((0, pool_a), (1, pool_b)):
            code = jnp.maximum(table_ref[4 + part, m], 0)
            value = pool[code >> 1, code & 1]
            done[m, pl.ds(part * half, half), :] = jnp.where(live, value, jnp.zeros_like(value))
        return carry

    rows = row_count // PARTS
    leaving = [
        pltpu.make_async_copy(done.at[pl.ds(k * rows, rows)], out, out_sem.at[k])
        for k, out in enumerate(outs)
    ]
    for k in range(PARTS):
        lax.fori_loop(k * rows, (k + 1) * rows, step, 0)
        leaving[k].start()
    for copy in leaving:
        copy.wait()


def land(table, sources_a, sources_b, row_count, length):
    anywhere = pl.BlockSpec(memory_space=pl.ANY)
    smem = pl.BlockSpec(memory_space=pltpu.SMEM)
    two, half, width = sources_a[0].shape[1:]
    dtype = sources_a[0].dtype
    return pl.pallas_call(
        functools.partial(land_kernel, len(sources_a), len(sources_b)),
        out_shape=(jax.ShapeDtypeStruct((row_count // PARTS, length, width), dtype),) * PARTS
        + (jax.ShapeDtypeStruct((row_count,), jnp.int32),),
        in_specs=[smem] + [anywhere] * (len(sources_a) + len(sources_b)),
        out_specs=(pl.BlockSpec(memory_space=pltpu.HBM),) * PARTS + (smem,),
        scratch_shapes=[
            pltpu.VMEM((sum(s.shape[0] for s in sources_a), two, half, width), dtype),
            pltpu.VMEM((sum(s.shape[0] for s in sources_b), two, half, width), dtype),
            pltpu.VMEM((row_count, length, width), dtype),
            pltpu.SemaphoreType.DMA((len(sources_a),)),
            pltpu.SemaphoreType.DMA((len(sources_b),)),
            pltpu.SemaphoreType.DMA((PARTS,)),
        ],
        compiler_params=pltpu.CompilerParams(vmem_limit_bytes=40 << 20),
        name="land",
        interpret=INTERPRET,
    )(table, *sources_a, *sources_b)


def chain(forward, backward, caps, step, ring):
    def moved(i, by):
        return (i // (step * ring)) * step * ring + (i + by * step) % (step * ring)

    devices = range(lax.axis_size("depth"))
    onward, returning = [], []
    for cap in caps:
        forward = lax.ppermute(forward[:cap], "depth", [(i, moved(i, 1)) for i in devices])
        backward = lax.ppermute(backward[:cap], "depth", [(i, moved(i, -1)) for i in devices])
        onward.append(forward)
        returning.append(backward)
    return onward + returning


def routed(route, table, own, partner):
    z_caps, x_caps, x_stay = route
    z_sizes = (z_caps[0], z_caps[0], Z_STAY)
    x_sizes = (x_caps[0], x_caps[0], x_stay)
    z_plus, z_minus, z_still, x_plus, x_minus, x_still = leave(table, own, partner, route)
    along_x = chain(x_plus, x_minus, x_caps, 2 * RING_Z, RING_X)
    along_z = chain(z_plus, z_minus, z_caps, 2, RING_Z)
    later = turn_over(table, 3, along_x + [x_still], z_sizes)
    last_b = chain(later[0], later[1], z_caps, 2, RING_Z)
    turned = turn_over(table, 2, along_z + [z_still], x_sizes)
    last_a = chain(turned[0], turned[1], x_caps, 2 * RING_Z, RING_X)
    return land(
        table,
        last_a + [turned[2]],
        last_b + [later[2]],
        own.shape[0] * own.shape[1],
        own.shape[2],
    )


def dense(targets, everywhere, own):
    row_count = targets.shape[0]
    _, _, length, width = own.shape
    peers = lax.axis_size("depth")
    position = lax.axis_index("depth")
    capacity = max(2, (row_count + peers - 1) // peers)
    slots = jnp.where(
        targets >= 0,
        targets // row_count * capacity + jnp.arange(row_count) % capacity,
        -1,
    )
    outgoing = spread(own.reshape(row_count, length, width), slots, peers * capacity)
    got = lax.all_to_all(
        outgoing.reshape((peers, capacity, length, width)),
        "depth",
        split_axis=0,
        concat_axis=0,
        tiled=True,
    ).reshape(peers * capacity, length, width)
    local = everywhere - position * row_count
    mine = jnp.logical_and(local >= 0, local < row_count)
    code = (
        lax.broadcasted_iota(jnp.int32, (peers, row_count), 0) * capacity
        + lax.broadcasted_iota(jnp.int32, (peers, row_count), 1) % capacity
    )
    wanted = jnp.where(mine, local, -1).reshape(1, -1)
    hit = jnp.arange(row_count)[:, None] == wanted
    source = jnp.max(jnp.where(hit, code.reshape(1, -1), -1), axis=1)
    return (*settle(source, got), (source >= 0).astype(jnp.int32))


def layer(
    alignment_input,
    target_slot,
    device_alignment,
    layer_norm_gain,
    layer_norm_bias,
    query_key_value_weight,
    output_weight,
):
    targets = target_slot[0]
    row_count, length, width = alignment_input.shape[1:]
    peers = lax.axis_size("depth")
    position = lax.axis_index("depth")
    own = alignment_input.reshape(row_count // 2, 2, length, width)
    everywhere = lax.all_to_all(
        jnp.broadcast_to(targets[None, None], (peers, 1, row_count)),
        "depth",
        split_axis=0,
        concat_axis=0,
        tiled=True,
    ).reshape(peers, row_count)
    partner = lax.ppermute(own, "depth", [(i, i ^ 1) for i in range(peers)])
    bundled = bundle(query_key_value_weight[0], output_weight[0], layer_norm_gain, layer_norm_bias)
    bundled = shifted(bundled, "section", 1, True)
    table, meta, pick = plan(position, device_alignment, everywhere, partner)
    *settled, live = lax.switch(
        pick[0],
        [
            lambda t, o, p, a, b: dense(a, b, o),
            lambda t, o, p, a, b: routed(ROUTE, t, o, p),
        ],
        table,
        own,
        partner,
        targets,
        everywhere,
    )
    balanced = [part.reshape(-1, width) for part in settled]
    earlier = [shifted(part, "section", 1, True) for part in balanced]
    tied, tied_low = front(
        live, balanced, layer_norm_gain, layer_norm_bias, query_key_value_weight[0]
    )
    tied, up, down = join(
        meta, tied, shifted(tied_low, "depth", 1, False), shifted(tied_low, "depth", -1, False)
    )
    neighbours = [shifted(up, "depth", 2, False), shifted(down, "depth", -2, False)]
    attention = shifted(middle(live, meta, tied, neighbours), "section", 1, True)
    begun = ()
    for index, rows in enumerate(earlier):
        begun = (
            back(
                index, attention, rows, bundled, row_count, begun
            ),
        )
    return begun[0].reshape(1, row_count, length, width)


def solution(mesh):
    placed = (
        P("section", "depth", None, None),
        P("section", "depth"),
        P("section", None),
        P("section", None),
        P("section", None),
        P("section", None, None),
        P("section", None, None),
    )
    return jax.shard_map(
        layer,
        mesh=mesh,
        in_specs=placed,
        out_specs=P("section", "depth", None, None),
        check_vma=False,
    )
```

```python
import functools

import jax
import jax.numpy as jnp
from jax import lax
from jax.experimental import pallas as pl
from jax.experimental.pallas import tpu as pltpu
from jax.sharding import PartitionSpec as P


H = 12
DH = 64
PAIRS = H // 2
EPSILON = 1e-05
CHUNK_ROWS = 8
PARTS = 2
INTERPRET = False


def spread_kernel(slot_ref, rows_ref, out_ref, sem):
    count = rows_ref.shape[0]

    def copy_of(i):
        return pltpu.make_async_copy(
            rows_ref.at[i], out_ref.at[jnp.maximum(slot_ref[i], 0)], sem.at[i]
        )

    def begin(i, carry):
        @pl.when(slot_ref[i] >= 0)
        def _():
            copy_of(i).start()

        return carry

    def finish(i, carry):
        @pl.when(slot_ref[i] >= 0)
        def _():
            copy_of(i).wait()

        return carry

    lax.fori_loop(0, count, begin, 0)
    lax.fori_loop(0, count, finish, 0)


def spread(rows, slots, slot_count):
    return pl.pallas_call(
        spread_kernel,
        out_shape=jax.ShapeDtypeStruct((slot_count,) + rows.shape[1:], rows.dtype),
        in_specs=[
            pl.BlockSpec(memory_space=pltpu.SMEM),
            pl.BlockSpec(memory_space=pltpu.VMEM),
        ],
        out_specs=pl.BlockSpec(memory_space=pltpu.HBM),
        scratch_shapes=[pltpu.SemaphoreType.DMA((rows.shape[0],))],
        name="spread",
        interpret=INTERPRET,
    )(slots, rows)


def settle_kernel(source_ref, rows_ref, *refs):
    outs, (landed, in_sem, out_sem) = refs[:PARTS], refs[PARTS:]
    row_count = landed.shape[0]
    part = row_count // PARTS

    def arrival(m):
        return pltpu.make_async_copy(
            rows_ref.at[jnp.maximum(source_ref[m], 0)], landed.at[m], in_sem.at[m]
        )

    def begin(m, carry):
        arrival(m).start()
        return carry

    def empty(m, carry):
        arrival(m).wait()

        @pl.when(source_ref[m] < 0)
        def _():
            landed[m] = jnp.zeros_like(landed[m])

        return carry

    lax.fori_loop(0, row_count, begin, 0)
    lax.fori_loop(0, row_count, empty, 0)
    leaving = [
        pltpu.make_async_copy(landed.at[pl.ds(k * part, part)], out, out_sem.at[k])
        for k, out in enumerate(outs)
    ]
    for copy in leaving:
        copy.start()
    for copy in leaving:
        copy.wait()


def settle(source, rows):
    row_count = source.shape[0]
    length, width = rows.shape[1:]
    return pl.pallas_call(
        settle_kernel,
        out_shape=(jax.ShapeDtypeStruct((row_count // PARTS, length, width), rows.dtype),) * PARTS,
        in_specs=[
            pl.BlockSpec(memory_space=pltpu.SMEM),
            pl.BlockSpec(memory_space=pl.ANY),
        ],
        out_specs=(pl.BlockSpec(memory_space=pltpu.HBM),) * PARTS,
        scratch_shapes=[
            pltpu.VMEM((row_count, length, width), rows.dtype),
            pltpu.SemaphoreType.DMA((row_count,)),
            pltpu.SemaphoreType.DMA((PARTS,)),
        ],
        name="settle",
        interpret=INTERPRET,
    )(source, rows)


def lane_mask(shape):
    return lax.broadcasted_iota(jnp.int32, shape, len(shape) - 1) % 128 < DH


def normalized(block, gain, bias):
    widened = block.astype(jnp.float32)
    average = jnp.mean(widened, axis=-1, keepdims=True)
    centred = widened - average
    spread_of = jnp.mean(centred * centred, axis=-1, keepdims=True)
    return (centred * lax.rsqrt(spread_of + EPSILON) * gain + bias).astype(jnp.bfloat16)


def front_kernel(
    live_ref,
    rows_0_ref,
    rows_1_ref,
    gain_ref,
    bias_ref,
    weight_ref,
    tied_ref,
    tied_low_ref,
    landed,
    acc,
    sem,
):
    row_count = live_ref.shape[0]
    width = rows_0_ref.shape[1]
    length = rows_0_ref.shape[0] * PARTS // row_count
    span = CHUNK_ROWS * length
    chunks = row_count // CHUNK_ROWS
    each = chunks // PARTS
    copies = [
        pltpu.make_async_copy(
            (rows_0_ref, rows_1_ref)[c // each].at[pl.ds(c % each * span, span), :],
            landed.at[c],
            sem.at[c],
        )
        for c in range(chunks)
    ]
    for copy in copies:
        copy.start()
    gain = gain_ref[...]
    bias = bias_ref[...]
    weight = weight_ref[:, : 2 * width]
    first = lane_mask((length, 256))
    acc[...] = jnp.zeros_like(acc)

    def step(c, carry):
        pltpu.make_async_copy(rows_0_ref.at[pl.ds(0, span), :], landed.at[c], sem.at[c]).wait()
        start = c * CHUNK_ROWS
        normed = normalized(landed[c], gain, bias)
        packed = jnp.dot(normed, weight, preferred_element_type=jnp.float32).astype(jnp.bfloat16)
        for pair in range(PAIRS):
            lanes = slice(pair * 128, pair * 128 + 128)
            key_lanes = slice(width + pair * 128, width + pair * 128 + 128)
            total = None
            for r in range(0, CHUNK_ROWS, 2):
                query_parts = []
                key_parts = []
                for k in (r, r + 1):
                    own = slice(k * length, (k + 1) * length)
                    query = packed[own, lanes]
                    query_parts.append(
                        jnp.where(live_ref[start + k] > 0, query, jnp.zeros_like(query))
                    )
                    key_parts.append(packed[own, key_lanes])
                query = jnp.concatenate(query_parts, axis=1)
                key = jnp.concatenate(key_parts, axis=1)
                zero = jnp.zeros_like(query)
                both = jnp.concatenate(
                    [jnp.where(first, query, zero), jnp.where(first, zero, query)], axis=0
                )
                part = lax.dot_general(
                    both, key, (((1,), (1,)), ((), ())), preferred_element_type=jnp.float32
                )
                total = part if total is None else total + part
            acc[pl.ds(pair * 2 * length, 2 * length), :] += total
        return carry

    lax.fori_loop(0, chunks, step, 0)
    quarter = H * length // 4
    tied = jnp.concatenate([acc[pl.ds(q * quarter, quarter), :] for q in range(4)], axis=1)
    tied_ref[...] = tied
    tied_low_ref[...] = tied.astype(jnp.bfloat16)


def front(live, rows, gain, bias, weight):
    row_count = live.shape[0]
    width = rows[0].shape[1]
    length = rows[0].shape[0] * PARTS // row_count
    quarter = H * length // 4
    vmem = pl.BlockSpec(memory_space=pltpu.VMEM)
    smem = pl.BlockSpec(memory_space=pltpu.SMEM)
    return pl.pallas_call(
        front_kernel,
        out_shape=(
            jax.ShapeDtypeStruct((quarter, 4 * length), jnp.float32),
            jax.ShapeDtypeStruct((quarter, 4 * length), jnp.bfloat16),
        ),
        in_specs=[smem] + [pl.BlockSpec(memory_space=pltpu.HBM)] * PARTS + [vmem, vmem, vmem],
        out_specs=(vmem, vmem),
        scratch_shapes=[
            pltpu.VMEM((row_count // CHUNK_ROWS, CHUNK_ROWS * length, width), jnp.bfloat16),
            pltpu.VMEM((H * length, length), jnp.float32),
            pltpu.SemaphoreType.DMA((row_count // CHUNK_ROWS,)),
        ],
        compiler_params=pltpu.CompilerParams(vmem_limit_bytes=40 << 20),
        name="front",
        interpret=INTERPRET,
    )(live, *rows, gain, bias, weight)


def belongs(meta_ref, step):
    other = meta_ref[0] + step
    return jnp.logical_and(other >= meta_ref[1], other < meta_ref[2])


def join_kernel(meta_ref, tied_ref, below_ref, above_ref, sum_ref, up_ref, down_ref):
    tied = tied_ref[...]
    below = jnp.where(belongs(meta_ref, -1), below_ref[...].astype(jnp.float32), 0.0)
    above = jnp.where(belongs(meta_ref, 1), above_ref[...].astype(jnp.float32), 0.0)
    sum_ref[...] = tied + below + above
    up_ref[...] = (tied + below).astype(jnp.bfloat16)
    down_ref[...] = (tied + above).astype(jnp.bfloat16)


def join(meta, tied, below, above):
    vmem = pl.BlockSpec(memory_space=pltpu.VMEM)
    return pl.pallas_call(
        join_kernel,
        out_shape=(
            jax.ShapeDtypeStruct(tied.shape, jnp.float32),
            jax.ShapeDtypeStruct(tied.shape, jnp.bfloat16),
            jax.ShapeDtypeStruct(tied.shape, jnp.bfloat16),
        ),
        in_specs=[pl.BlockSpec(memory_space=pltpu.SMEM), vmem, vmem, vmem],
        out_specs=(vmem, vmem, vmem),
        name="join",
        interpret=INTERPRET,
    )(meta, tied, below, above)


def middle_kernel(live_ref, meta_ref, tied_ref, below_ref, above_ref, out_ref):
    length = tied_ref.shape[1] // 4
    tied = tied_ref[...]
    tied = tied + jnp.where(belongs(meta_ref, -2), below_ref[...].astype(jnp.float32), 0.0)
    tied = tied + jnp.where(belongs(meta_ref, 2), above_ref[...].astype(jnp.float32), 0.0)
    quarter = tied.shape[0]
    count = jnp.full((1, length), meta_ref[3], jnp.int32).astype(jnp.float32)
    scale = DH ** (-0.5) / jnp.sqrt(count)
    logits = (
        jnp.concatenate([tied[:, q * length : (q + 1) * length] for q in range(4)], axis=0) * scale
    )
    top = jnp.max(logits, axis=-1, keepdims=True)
    raised = jnp.exp(logits - top)
    attention = raised / jnp.sum(raised, axis=-1, keepdims=True)
    out_ref[pl.ds(0, quarter), :] = jnp.concatenate(
        [attention[q * quarter : (q + 1) * quarter] for q in range(4)], axis=1
    ).astype(jnp.bfloat16)
    lane = lax.broadcasted_iota(jnp.int32, (16, 4 * length), 1)
    live = jnp.zeros((16, 4 * length), jnp.float32)
    for m in range(live_ref.shape[0]):
        live = jnp.where(jnp.logical_and(lane == m, live_ref[m] > 0), 1.0, live)
    out_ref[pl.ds(quarter, 16), :] = live.astype(jnp.bfloat16)


def middle(live, meta, tied, neighbours):
    vmem = pl.BlockSpec(memory_space=pltpu.VMEM)
    smem = pl.BlockSpec(memory_space=pltpu.SMEM)
    return pl.pallas_call(
        middle_kernel,
        out_shape=jax.ShapeDtypeStruct((tied.shape[0] + 16, tied.shape[1]), jnp.bfloat16),
        in_specs=[smem, smem] + [vmem] * (1 + len(neighbours)),
        out_specs=vmem,
        name="middle",
        interpret=INTERPRET,
    )(live, meta, tied, *neighbours)


def values_kernel(rows_ref, bundle_ref, out_ref, landed, sem):
    chunks = landed.shape[0]
    span, width = landed.shape[1:]

    def arrival(c):
        return pltpu.make_async_copy(
            rows_ref.at[pl.ds(c * span, span), :], landed.at[c], sem.at[c]
        )

    for c in range(chunks):
        arrival(c).start()
    affine = bundle_ref[pl.ds(2 * width, 16), :].astype(jnp.float32)
    gain = (affine[0:1] + affine[1:2]) + affine[2:3]
    bias = (affine[3:4] + affine[4:5]) + affine[5:6]
    weight = bundle_ref[pl.ds(0, width), :]

    def step(c, carry):
        arrival(c).wait()
        out_ref[c] = jnp.dot(
            normalized(landed[c], gain, bias), weight, preferred_element_type=jnp.float32
        ).astype(jnp.bfloat16)
        return carry

    lax.fori_loop(0, chunks, step, 0)


def values_of(rows, bundled, row_count):
    vmem = pl.BlockSpec(memory_space=pltpu.VMEM)
    tokens, width = rows.shape
    chunks = row_count // PARTS // CHUNK_ROWS
    shape = (chunks, tokens // chunks, width)
    return pl.pallas_call(
        values_kernel,
        out_shape=jax.ShapeDtypeStruct(shape, jnp.bfloat16),
        in_specs=[pl.BlockSpec(memory_space=pltpu.HBM), vmem],
        out_specs=vmem,
        scratch_shapes=[pltpu.VMEM(shape, jnp.bfloat16), pltpu.SemaphoreType.DMA((chunks,))],
        compiler_params=pltpu.CompilerParams(vmem_limit_bytes=40 << 20),
        name="values",
        interpret=INTERPRET,
    )(rows, bundled)


def finish_kernel(attention_ref, bundle_ref, *refs):
    rows_refs, values_refs = refs[:PARTS], refs[PARTS : 2 * PARTS]
    out_ref, landed, held, mask, row_sem, value_sem, out_sem = refs[2 * PARTS :]
    chunks = landed.shape[0]
    span, width = landed.shape[1:]
    length = span // CHUNK_ROWS
    quarter = H * length // 4
    each = chunks // PARTS
    for c in range(chunks):
        part = c // each
        pltpu.make_async_copy(values_refs[part].at[c % each], held.at[c], value_sem.at[c]).start()
        pltpu.make_async_copy(
            rows_refs[part].at[pl.ds(c % each * span, span), :], landed.at[c], row_sem.at[c]
        ).start()

    def leaving(c):
        return pltpu.make_async_copy(
            held.at[c], out_ref.at[pl.ds(c * span, span), :], out_sem.at[c]
        )

    packed = attention_ref[pl.ds(0, quarter), :]
    attention = jnp.concatenate(
        [packed[:, q * length : (q + 1) * length] for q in range(4)], axis=0
    )
    live = attention_ref[pl.ds(quarter, 16), :].astype(jnp.float32)
    for m in range(chunks * CHUNK_ROWS):
        mask[m // CHUNK_ROWS, pl.ds(m % CHUNK_ROWS * length, length), :] = jnp.broadcast_to(
            live[0:1, m : m + 1], (length, 128)
        )
    wide = jnp.concatenate([attention] * CHUNK_ROWS, axis=1)
    diagonal = (
        lax.broadcasted_iota(jnp.int32, (span, span), 0) // length
        == lax.broadcasted_iota(jnp.int32, (span, span), 1) // length
    )
    first = lane_mask((span, 128))
    mixers = []
    for h in range(H):
        tall = jnp.concatenate([wide[h * length : (h + 1) * length]] * CHUNK_ROWS, axis=0)
        mixers.append(jnp.where(diagonal, tall, jnp.zeros_like(tall)))
    weight = bundle_ref[pl.ds(width, width), :]

    def step(c, carry):
        pltpu.make_async_copy(values_refs[0].at[0], held.at[c], value_sem.at[c]).wait()
        values = held[c]
        parts = []
        for pair in range(PAIRS):
            lanes = values[:, pair * 128 : pair * 128 + 128]
            low = jnp.dot(mixers[2 * pair], lanes, preferred_element_type=jnp.float32)
            high = jnp.dot(mixers[2 * pair + 1], lanes, preferred_element_type=jnp.float32)
            parts.append(jnp.where(first, low, high).astype(jnp.bfloat16))
        attended = jnp.concatenate(parts, axis=1)
        mixed = jnp.dot(attended, weight, preferred_element_type=jnp.float32)
        pltpu.make_async_copy(
            rows_refs[0].at[pl.ds(0, span), :], landed.at[c], row_sem.at[c]
        ).wait()
        mixed = mixed + landed[c].astype(jnp.float32)
        held[c] = (mixed * jnp.concatenate([mask[c]] * (width // 128), axis=1)).astype(
            jnp.bfloat16
        )
        leaving(c).start()
        return carry

    lax.fori_loop(0, chunks, step, 0)
    for c in range(chunks):
        leaving(c).wait()


def finish(attention, bundled, rows, values):
    vmem = pl.BlockSpec(memory_space=pltpu.VMEM)
    hbm = pl.BlockSpec(memory_space=pltpu.HBM)
    anywhere = pl.BlockSpec(memory_space=pl.ANY)
    tokens, width = rows[0].shape
    each, span, _ = values[0].shape
    shape = (each * PARTS, span, width)
    return pl.pallas_call(
        finish_kernel,
        out_shape=jax.ShapeDtypeStruct((tokens * PARTS, width), jnp.bfloat16),
        in_specs=[vmem, vmem] + [hbm] * PARTS + [anywhere] * PARTS,
        out_specs=hbm,
        scratch_shapes=[
            pltpu.VMEM(shape, jnp.bfloat16),
            pltpu.VMEM(shape, jnp.bfloat16),
            pltpu.VMEM((each * PARTS, span, 128), jnp.float32),
            pltpu.SemaphoreType.DMA((each * PARTS,)),
            pltpu.SemaphoreType.DMA((each * PARTS,)),
            pltpu.SemaphoreType.DMA((each * PARTS,)),
        ],
        compiler_params=pltpu.CompilerParams(vmem_limit_bytes=40 << 20),
        name="finish",
        interpret=INTERPRET,
    )(attention, bundled, *rows, *values)


def shifted(value, axis, steps, wrap):
    count = lax.axis_size(axis)
    if wrap:
        route = [(i, (i + steps) % count) for i in range(count)]
    else:
        route = [(i, i + steps) for i in range(count) if 0 <= i + steps < count]
    return lax.ppermute(value, axis, route)


ROUTE = ((11, 9, 6, 4), (10, 5), 12)
Z_STAY = 8
RING_Z = 8
RING_X = 4


def plan_kernel(
    position_ref, groups_ref, targets_ref, partner_ref, table_ref, meta_ref, pick_ref
):
    peers, row_count = targets_ref.shape
    pair_count = row_count // 2
    position = position_ref[0]
    shape = (peers, 128)
    down = lax.broadcasted_iota(jnp.int32, shape, 0)
    across = lax.broadcasted_iota(jnp.int32, shape, 1)
    zero = jnp.zeros(shape, jnp.int32)

    def over_lanes(value):
        return jnp.broadcast_to(jnp.sum(value, axis=1, keepdims=True), shape)

    def over_rows(value):
        return jnp.broadcast_to(jnp.sum(value, axis=0, keepdims=True), shape)

    def top_rows(value):
        return jnp.max(value, axis=0, keepdims=True)

    def flag(condition):
        return jnp.where(condition, 1, zero)

    def to_lanes(value):
        return over_rows(jnp.where(down == across, value, zero))

    def to_rows(value):
        return over_lanes(jnp.where(down == across, value, zero))

    targets = jnp.concatenate(
        [targets_ref[...], jnp.full((peers, 128 - row_count), -1, jnp.int32)], axis=1
    )
    device = targets >> 5
    offset = jnp.where(targets >= 0, (device - down) & (peers - 1), -1)
    seen = zero
    for i in range(row_count):
        seen = seen | flag(jnp.broadcast_to(offset[:, i : i + 1], shape) == across)
    present_l = flag(over_rows(seen) > 0)
    present = to_rows(present_l)
    odd = down & 1
    odd_l = across & 1

    def turns(core):
        step = ((down + odd * (1 - 2 * core)) >> 1) & 31
        step_l = ((across + odd_l * (1 - 2 * core)) >> 1) & 31
        u, u_l = step & 7, step_l & 7
        order = u * 64 + down
        order_l = u_l * 64 + across
        moving = present * flag(u > 0)
        moving_l = present_l * flag(u_l > 0)
        rank = over_lanes(moving_l * flag(order_l < order))
        rest = over_lanes((present_l - moving_l) * flag(order_l < order))
        return step >> 3, u, moving, rank, rest

    def split_of(core):
        caps = ROUTE[0]
        _, u, moving, rank, _ = turns(core)
        early = moving * flag(rank < across)
        late = moving - early
        good = flag(across <= pair_count)
        for h in range(1, 6):
            cap = caps[h - 1] if h <= len(caps) else 0
            good = good * flag(over_rows(early * flag(u >= h)) <= cap)
            good = good * flag(over_rows(late * flag(RING_Z - u >= h)) <= cap)
        split = jnp.min(jnp.where(good > 0, across, 127), axis=1, keepdims=True)
        return jnp.broadcast_to(split, shape)

    def z_lanes(core, split):
        (z1, z2, z3, z4) = ROUTE[0]
        _, u, moving, rank, rest = turns(core)
        plus = moving * flag(rank < split)
        staying = present - moving
        hops = jnp.where(plus > 0, u, RING_Z - u)
        place = jnp.where(plus > 0, split - 1 - rank, rank - split)
        base = jnp.where(
            hops == 1, 0, jnp.where(hops == 2, z1, jnp.where(hops == 3, z1 + z2, z1 + z2 + z3))
        )
        side = moving - plus
        z_all = z1 + z2 + z3 + z4
        z_leave = jnp.where(staying > 0, 2 * z1 + rest, side * z1 + place)
        z_land = jnp.where(staying > 0, 2 * z_all + rest, side * z_all + base + place)
        return jnp.where(present > 0, z_leave, -1), jnp.where(present > 0, z_land, -1)

    def x_counts(core, line):
        high, u, _, _, _ = turns(core)
        turn = (high + flag(line < u)) & (RING_X - 1)
        turn = jnp.where(present > 0, turn, -1)
        count = [over_rows(flag(turn == v)) for v in range(RING_X)]
        x2 = ROUTE[1][1]
        ahead = (count[2] + count[3] - count[1] + 1) >> 1
        ahead = jnp.minimum(
            jnp.maximum(ahead, jnp.maximum(count[2] - x2, 0)), jnp.minimum(count[2], x2)
        )
        return turn, count, ahead

    def fits(core):
        x1, x2 = ROUTE[1]
        _, count, ahead = x_counts(core, across)
        behind = count[2] - ahead
        good = (
            flag(ahead <= x2)
            * flag(behind <= x2)
            * flag(ahead + count[1] <= x1)
            * flag(behind + count[3] <= x1)
            * flag(count[0] <= ROUTE[2])
        )
        return jnp.min(jnp.where(across < RING_Z, good, 1))

    def x_lanes(core, line):
        x1, x2 = ROUTE[1]
        turn, count, ahead = x_counts(core, line)
        turn_l = to_lanes(turn)
        level = over_lanes(present_l * flag(turn_l == turn) * flag(across < down))
        double = flag(turn == 2)
        near = double * flag(level < ahead)
        forward = flag(turn == 1) + near
        spot = jnp.where(
            double > 0,
            level - jnp.where(near > 0, 0, ahead),
            level + jnp.where(turn == 1, ahead, count[2] - ahead),
        )
        side = 1 - forward
        x_leave = jnp.where(turn == 0, 2 * x1 + level, side * x1 + spot)
        x_land = jnp.where(
            turn == 0, 2 * (x1 + x2) + level, side * (x1 + x2) + double * x1 + spot
        )
        return jnp.where(present > 0, x_leave, -1), jnp.where(present > 0, x_land, -1)

    core = position & 1
    split = split_of(core)
    z_leave, z_land = z_lanes(core, split)
    line = (position >> 1) & (RING_Z - 1)
    x_leave_a, x_land_a = x_lanes(core, line)
    x_leave_b, x_land_b = x_lanes(core, RING_Z - 1 - line)
    other_split = split_of(1 - core)
    good = jnp.where(
        jnp.max(jnp.maximum(split, other_split)) <= pair_count, fits(core) * fits(1 - core), 0
    )

    lane_row = lax.broadcasted_iota(jnp.int32, (1, 128), 1)
    origin = -1 + zero
    for b in range(2):
        sender = position if b == 0 else position ^ 1
        mine = targets_ref[pl.ds(sender, 1), :]
        mine = jnp.concatenate([mine, jnp.full((1, 128 - row_count), -1, jnp.int32)], axis=1)
        away = ((mine >> 5) - sender) & (peers - 1)
        away = jnp.where(mine >= 0, away, -1)
        away = jnp.where((away & 1) == b, away, -1)
        hit = jnp.broadcast_to(away, shape) == down
        code = b * pair_count + (jnp.broadcast_to(lane_row, shape) >> 1)
        found = jnp.max(jnp.where(hit, code, -1), axis=1, keepdims=True)
        origin = jnp.maximum(origin, jnp.broadcast_to(found, shape))

    def gathered(slot_of, value):
        return top_rows(jnp.where(slot_of == across, value, -1))

    local = targets - position * row_count
    here = jnp.logical_and(local >= 0, local < row_count)
    settled_a = jnp.full((1, 128), -1, jnp.int32)
    settled_b = settled_a
    lane_full = across & 1
    for r in range(2):
        slot = jnp.max(
            jnp.where(jnp.logical_and(here, lane_full == r), local, -1), axis=1, keepdims=True
        )
        slot = jnp.broadcast_to(slot, shape)
        slot_l = over_rows(jnp.where(down == across, slot + 1, zero)) - 1
        match = across == ((position - down) & (peers - 1))
        slot_by_offset = over_lanes(jnp.where(match, slot_l + 1, zero)) - 1
        settled_a = jnp.maximum(settled_a, gathered(slot_by_offset, x_land_a * 2 + r))
        settled_b = jnp.maximum(settled_b, gathered(slot_by_offset, z_land * 2 + r))
    empty = jnp.full((1, 128), -1, jnp.int32)
    table_ref[...] = jnp.concatenate(
        [
            gathered(z_leave, origin),
            gathered(x_leave_b, origin),
            gathered(x_leave_a, z_land),
            gathered(z_leave, x_land_b),
            settled_a,
            settled_b,
            empty,
            empty,
        ],
        axis=0,
    )
    groups = groups_ref[...]
    lane = lax.broadcasted_iota(jnp.int32, groups.shape, 1)
    own_group = jnp.sum(jnp.where(lane == position, groups, 0))
    low = jnp.sum(jnp.where(groups < own_group, 1, 0))
    high = low + jnp.sum(jnp.where(groups == own_group, 1, 0))
    inside = jnp.logical_and(targets >= low * row_count, targets < high * row_count)
    meta_ref[0] = position
    meta_ref[1] = low
    meta_ref[2] = high
    meta_ref[3] = jnp.sum(jnp.where(inside, 1, 0))
    pick_ref[0] = good


def plan(position, groups, targets, partner):
    vmem = pl.BlockSpec(memory_space=pltpu.VMEM)
    smem = pl.BlockSpec(memory_space=pltpu.SMEM)
    return pl.pallas_call(
        plan_kernel,
        out_shape=(
            jax.ShapeDtypeStruct((8, 128), jnp.int32),
            jax.ShapeDtypeStruct((4,), jnp.int32),
            jax.ShapeDtypeStruct((1,), jnp.int32),
        ),
        in_specs=[smem, vmem, vmem, pl.BlockSpec(memory_space=pltpu.HBM)],
        out_specs=(vmem, smem, smem),
        name="plan",
        interpret=INTERPRET,
    )(position.reshape(1), groups, targets, partner)


def pieces(value):
    parts = []
    for _ in range(3):
        part = value.astype(jnp.bfloat16)
        parts.append(part.astype(jnp.float32))
        value = value - parts[-1]
    return parts


def bundle_kernel(weight_ref, out_weight_ref, gain_ref, bias_ref, out_ref, held, sem):
    width = held.shape[1]
    loads = [
        pltpu.make_async_copy(
            weight_ref.at[:, pl.ds(2 * width, width)], held.at[pl.ds(0, width), :], sem.at[0]
        ),
        pltpu.make_async_copy(out_weight_ref, held.at[pl.ds(width, width), :], sem.at[1]),
    ]
    for load in loads:
        load.start()
    rows = pieces(gain_ref[...]) + pieces(bias_ref[...])
    rows.append(jnp.zeros((16 - len(rows), width), jnp.float32))
    held[pl.ds(2 * width, 16), :] = jnp.concatenate(rows, axis=0).astype(jnp.bfloat16)
    for load in loads:
        load.wait()
    store = pltpu.make_async_copy(held, out_ref, sem.at[2])
    store.start()
    store.wait()


def bundle(weight, out_weight, gain, bias):
    width = weight.shape[0]
    vmem = pl.BlockSpec(memory_space=pltpu.VMEM)
    hbm = pl.BlockSpec(memory_space=pltpu.HBM)
    shape = (2 * width + 16, width)
    return pl.pallas_call(
        bundle_kernel,
        out_shape=jax.ShapeDtypeStruct(shape, weight.dtype),
        in_specs=[hbm, hbm, vmem, vmem],
        out_specs=hbm,
        scratch_shapes=[pltpu.VMEM(shape, weight.dtype), pltpu.SemaphoreType.DMA((3,))],
        name="bundle",
        interpret=INTERPRET,
    )(weight, out_weight, gain, bias)


def deal(table_ref, row, pool, outs):
    lane = 0
    for out in outs:

        def step(k, carry, out=out, lane=lane):
            out[k] = pool[jnp.maximum(table_ref[row, lane + k], 0)]
            return carry

        lax.fori_loop(0, out.shape[0], step, 0)
        lane += out.shape[0]


def leave_kernel(part, table_ref, own_ref, partner_ref, *refs):
    outs, (pool, sem) = refs[:-2], refs[-2:]
    pairs = own_ref.shape[0]
    half = own_ref.shape[2] // 2
    copies = [
        pltpu.make_async_copy(
            ref.at[:, :, pl.ds(part * half, half), :],
            pool.at[pl.ds(b * pairs, pairs)],
            sem.at[b],
        )
        for b, ref in enumerate((own_ref, partner_ref))
    ]
    for copy in copies:
        copy.start()
    for copy in copies:
        copy.wait()
    deal(table_ref, part, pool, outs)


def leave(part, table, own, partner, sizes):
    pairs, two, length, width = own.shape
    vmem = pl.BlockSpec(memory_space=pltpu.VMEM)
    anywhere = pl.BlockSpec(memory_space=pl.ANY)
    return pl.pallas_call(
        functools.partial(leave_kernel, part),
        out_shape=tuple(
            jax.ShapeDtypeStruct((n, two, length // 2, width), own.dtype) for n in sizes
        ),
        in_specs=[pl.BlockSpec(memory_space=pltpu.SMEM), anywhere, anywhere],
        out_specs=(vmem,) * len(sizes),
        scratch_shapes=[
            pltpu.VMEM((2 * pairs, two, length // 2, width), own.dtype),
            pltpu.SemaphoreType.DMA((2,)),
        ],
        compiler_params=pltpu.CompilerParams(vmem_limit_bytes=40 << 20),
        name="leave",
        interpret=INTERPRET,
    )(table, own, partner)


def pooled(refs, pool, sem):
    copies = []
    start = 0
    for ref in refs:
        count = ref.shape[0]
        copies.append(
            pltpu.make_async_copy(ref, pool.at[pl.ds(start, count)], sem.at[len(copies)])
        )
        start += count
    return copies


def turn_kernel(row, count, table_ref, *refs):
    sources, outs, (pool, sem) = refs[:count], refs[count:-2], refs[-2:]
    copies = pooled(sources, pool, sem)
    for copy in copies:
        copy.start()
    for copy in copies:
        copy.wait()
    deal(table_ref, row, pool, outs)


def turn_over(table, row, sources, sizes):
    vmem = pl.BlockSpec(memory_space=pltpu.VMEM)
    anywhere = pl.BlockSpec(memory_space=pl.ANY)
    payload = sources[0].shape[1:]
    return pl.pallas_call(
        functools.partial(turn_kernel, row, len(sources)),
        out_shape=tuple(jax.ShapeDtypeStruct((n,) + payload, sources[0].dtype) for n in sizes),
        in_specs=[pl.BlockSpec(memory_space=pltpu.SMEM)] + [anywhere] * len(sources),
        out_specs=(vmem,) * len(sizes),
        scratch_shapes=[
            pltpu.VMEM((sum(s.shape[0] for s in sources),) + payload, sources[0].dtype),
            pltpu.SemaphoreType.DMA((len(sources),)),
        ],
        compiler_params=pltpu.CompilerParams(vmem_limit_bytes=40 << 20),
        name="turn_over",
        interpret=INTERPRET,
    )(table, *sources)


def land_kernel(part, count, table_ref, *refs):
    sources = refs[:count]
    outs = refs[-PARTS - 5 : -5]
    live_ref, pool, done, in_sem, out_sem = refs[-5:]
    row_count, half, _ = done.shape
    copies = pooled(sources, pool, in_sem)
    for copy in copies:
        copy.start()
    for copy in copies:
        copy.wait()

    def step(m, carry):
        live = table_ref[4 + part, m] >= 0
        live_ref[m] = jnp.where(live, 1, 0)
        code = jnp.maximum(table_ref[4 + part, m], 0)
        value = pool[code >> 1, code & 1]
        done[m] = jnp.where(live, value, jnp.zeros_like(value))
        return carry

    rows = row_count // PARTS
    leaving = [
        pltpu.make_async_copy(
            done.at[pl.ds(k * rows, rows)],
            out.at[:, pl.ds(part * half, half), :],
            out_sem.at[k],
        )
        for k, out in enumerate(outs)
    ]
    for k in range(PARTS):
        lax.fori_loop(k * rows, (k + 1) * rows, step, 0)
        leaving[k].start()
    for copy in leaving:
        copy.wait()


def land(part, table, sources, row_count, length, begun):
    anywhere = pl.BlockSpec(memory_space=pl.ANY)
    smem = pl.BlockSpec(memory_space=pltpu.SMEM)
    hbm = pl.BlockSpec(memory_space=pltpu.HBM)
    two, half, width = sources[0].shape[1:]
    dtype = sources[0].dtype
    count = len(sources)
    return pl.pallas_call(
        functools.partial(land_kernel, part, count),
        out_shape=(jax.ShapeDtypeStruct((row_count // PARTS, length, width), dtype),) * PARTS
        + (jax.ShapeDtypeStruct((row_count,), jnp.int32),),
        in_specs=[smem] + [anywhere] * count + [hbm] * len(begun),
        out_specs=(hbm,) * PARTS + (smem,),
        scratch_shapes=[
            pltpu.VMEM((sum(s.shape[0] for s in sources), two, half, width), dtype),
            pltpu.VMEM((row_count, half, width), dtype),
            pltpu.SemaphoreType.DMA((count,)),
            pltpu.SemaphoreType.DMA((PARTS,)),
        ],
        input_output_aliases={1 + count + k: k for k in range(len(begun))},
        compiler_params=pltpu.CompilerParams(vmem_limit_bytes=40 << 20),
        name="land",
        interpret=INTERPRET,
    )(table, *sources, *begun)


def chain(forward, backward, caps, step, ring):
    def moved(i, by):
        return (i // (step * ring)) * step * ring + (i + by * step) % (step * ring)

    devices = range(lax.axis_size("depth"))
    onward, returning = [], []
    for cap in caps:
        forward = lax.ppermute(forward[:cap], "depth", [(i, moved(i, 1)) for i in devices])
        backward = lax.ppermute(backward[:cap], "depth", [(i, moved(i, -1)) for i in devices])
        onward.append(forward)
        returning.append(backward)
    return onward + returning


def routed(route, table, own, partner):
    z_caps, x_caps, x_stay = route
    z_sizes = (z_caps[0], z_caps[0], Z_STAY)
    x_sizes = (x_caps[0], x_caps[0], x_stay)
    z_plus, z_minus, z_still = leave(0, table, own, partner, z_sizes)
    x_plus, x_minus, x_still = leave(1, table, own, partner, x_sizes)
    along_x = chain(x_plus, x_minus, x_caps, 2 * RING_Z, RING_X)
    along_z = chain(z_plus, z_minus, z_caps, 2, RING_Z)
    later = turn_over(table, 3, along_x + [x_still], z_sizes)
    last_b = chain(later[0], later[1], z_caps, 2, RING_Z)
    turned = turn_over(table, 2, along_z + [z_still], x_sizes)
    last_a = chain(turned[0], turned[1], x_caps, 2 * RING_Z, RING_X)
    row_count, length = own.shape[0] * own.shape[1], own.shape[2]
    *begun, _ = land(0, table, last_a + [turned[2]], row_count, length, ())
    return land(1, table, last_b + [later[2]], row_count, length, begun)


def dense(targets, everywhere, own):
    row_count = targets.shape[0]
    _, _, length, width = own.shape
    peers = lax.axis_size("depth")
    position = lax.axis_index("depth")
    capacity = max(2, (row_count + peers - 1) // peers)
    slots = jnp.where(
        targets >= 0,
        targets // row_count * capacity + jnp.arange(row_count) % capacity,
        -1,
    )
    outgoing = spread(own.reshape(row_count, length, width), slots, peers * capacity)
    got = lax.all_to_all(
        outgoing.reshape((peers, capacity, length, width)),
        "depth",
        split_axis=0,
        concat_axis=0,
        tiled=True,
    ).reshape(peers * capacity, length, width)
    local = everywhere - position * row_count
    mine = jnp.logical_and(local >= 0, local < row_count)
    code = (
        lax.broadcasted_iota(jnp.int32, (peers, row_count), 0) * capacity
        + lax.broadcasted_iota(jnp.int32, (peers, row_count), 1) % capacity
    )
    wanted = jnp.where(mine, local, -1).reshape(1, -1)
    hit = jnp.arange(row_count)[:, None] == wanted
    source = jnp.max(jnp.where(hit, code.reshape(1, -1), -1), axis=1)
    return (*settle(source, got), (source >= 0).astype(jnp.int32))


def layer(
    alignment_input,
    target_slot,
    device_alignment,
    layer_norm_gain,
    layer_norm_bias,
    query_key_value_weight,
    output_weight,
):
    targets = target_slot[0]
    row_count, length, width = alignment_input.shape[1:]
    peers = lax.axis_size("depth")
    position = lax.axis_index("depth")
    own = alignment_input.reshape(row_count // 2, 2, length, width)
    everywhere = lax.all_to_all(
        jnp.broadcast_to(targets[None, None], (peers, 1, row_count)),
        "depth",
        split_axis=0,
        concat_axis=0,
        tiled=True,
    ).reshape(peers, row_count)
    partner = lax.ppermute(own, "depth", [(i, i ^ 1) for i in range(peers)])
    bundled = bundle(query_key_value_weight[0], output_weight[0], layer_norm_gain, layer_norm_bias)
    bundled = shifted(bundled, "section", 1, True)
    table, meta, pick = plan(position, device_alignment, everywhere, partner)
    *settled, live = lax.switch(
        pick[0],
        [
            lambda t, o, p, a, b: dense(a, b, o),
            lambda t, o, p, a, b: routed(ROUTE, t, o, p),
        ],
        table,
        own,
        partner,
        targets,
        everywhere,
    )
    balanced = [part.reshape(-1, width) for part in settled]
    earlier = [shifted(part, "section", 1, True) for part in balanced]
    tied, tied_low = front(
        live, balanced, layer_norm_gain, layer_norm_bias, query_key_value_weight[0]
    )
    tied, up, down = join(
        meta, tied, shifted(tied_low, "depth", 1, False), shifted(tied_low, "depth", -1, False)
    )
    neighbours = [shifted(up, "depth", 2, False), shifted(down, "depth", -2, False)]
    attention = middle(live, meta, tied, neighbours)
    attention = shifted(attention, "section", 1, True)
    values = []
    for rows in earlier:
        values.append(values_of(rows, bundled, row_count))
    handed = finish(attention, bundled, earlier, values)
    return handed.reshape(1, row_count, length, width)


def solution(mesh):
    placed = (
        P("section", "depth", None, None),
        P("section", "depth"),
        P("section", None),
        P("section", None),
        P("section", None),
        P("section", None, None),
        P("section", None, None),
    )
    return jax.shard_map(
        layer,
        mesh=mesh,
        in_specs=placed,
        out_specs=P("section", "depth", None, None),
        check_vma=False,
    )
```

```python
import functools

import jax
import jax.numpy as jnp
from jax import lax
from jax.experimental import pallas as pl
from jax.experimental.pallas import tpu as pltpu
from jax.sharding import PartitionSpec as P


H = 12
DH = 64
PAIRS = H // 2
EPSILON = 1e-05
CHUNK_ROWS = 8
PARTS = 2
INTERPRET = False


def spread_kernel(slot_ref, rows_ref, out_ref, sem):
    count = rows_ref.shape[0]

    def copy_of(i):
        return pltpu.make_async_copy(
            rows_ref.at[i], out_ref.at[jnp.maximum(slot_ref[i], 0)], sem.at[i]
        )

    def begin(i, carry):
        @pl.when(slot_ref[i] >= 0)
        def _():
            copy_of(i).start()

        return carry

    def finish(i, carry):
        @pl.when(slot_ref[i] >= 0)
        def _():
            copy_of(i).wait()

        return carry

    lax.fori_loop(0, count, begin, 0)
    lax.fori_loop(0, count, finish, 0)


def spread(rows, slots, slot_count):
    return pl.pallas_call(
        spread_kernel,
        out_shape=jax.ShapeDtypeStruct((slot_count,) + rows.shape[1:], rows.dtype),
        in_specs=[
            pl.BlockSpec(memory_space=pltpu.SMEM),
            pl.BlockSpec(memory_space=pltpu.VMEM),
        ],
        out_specs=pl.BlockSpec(memory_space=pltpu.HBM),
        scratch_shapes=[pltpu.SemaphoreType.DMA((rows.shape[0],))],
        name="spread",
        interpret=INTERPRET,
    )(slots, rows)


def settle_kernel(source_ref, rows_ref, *refs):
    outs, (landed, in_sem, out_sem) = refs[:PARTS], refs[PARTS:]
    row_count = landed.shape[0]
    part = row_count // PARTS

    def arrival(m):
        return pltpu.make_async_copy(
            rows_ref.at[jnp.maximum(source_ref[m], 0)], landed.at[m], in_sem.at[m]
        )

    def begin(m, carry):
        arrival(m).start()
        return carry

    def empty(m, carry):
        arrival(m).wait()

        @pl.when(source_ref[m] < 0)
        def _():
            landed[m] = jnp.zeros_like(landed[m])

        return carry

    lax.fori_loop(0, row_count, begin, 0)
    lax.fori_loop(0, row_count, empty, 0)
    leaving = [
        pltpu.make_async_copy(landed.at[pl.ds(k * part, part)], out, out_sem.at[k])
        for k, out in enumerate(outs)
    ]
    for copy in leaving:
        copy.start()
    for copy in leaving:
        copy.wait()


def settle(source, rows):
    row_count = source.shape[0]
    length, width = rows.shape[1:]
    return pl.pallas_call(
        settle_kernel,
        out_shape=(jax.ShapeDtypeStruct((row_count // PARTS, length, width), rows.dtype),) * PARTS,
        in_specs=[
            pl.BlockSpec(memory_space=pltpu.SMEM),
            pl.BlockSpec(memory_space=pl.ANY),
        ],
        out_specs=(pl.BlockSpec(memory_space=pltpu.HBM),) * PARTS,
        scratch_shapes=[
            pltpu.VMEM((row_count, length, width), rows.dtype),
            pltpu.SemaphoreType.DMA((row_count,)),
            pltpu.SemaphoreType.DMA((PARTS,)),
        ],
        name="settle",
        interpret=INTERPRET,
    )(source, rows)


def lane_mask(shape):
    return lax.broadcasted_iota(jnp.int32, shape, len(shape) - 1) % 128 < DH


def normalized(block, gain, bias):
    widened = block.astype(jnp.float32)
    average = jnp.mean(widened, axis=-1, keepdims=True)
    centred = widened - average
    spread_of = jnp.mean(centred * centred, axis=-1, keepdims=True)
    return (centred * lax.rsqrt(spread_of + EPSILON) * gain + bias).astype(jnp.bfloat16)


def front_kernel(
    live_ref,
    rows_0_ref,
    rows_1_ref,
    gain_ref,
    bias_ref,
    weight_ref,
    tied_ref,
    tied_low_ref,
    landed,
    weight,
    acc,
    sem,
    weight_sem,
):
    row_count = live_ref.shape[0]
    width = rows_0_ref.shape[1]
    length = rows_0_ref.shape[0] * PARTS // row_count
    span = CHUNK_ROWS * length
    chunks = row_count // CHUNK_ROWS
    each = chunks // PARTS
    copies = [
        pltpu.make_async_copy(
            (rows_0_ref, rows_1_ref)[c // each].at[pl.ds(c % each * span, span), :],
            landed.at[c],
            sem.at[c],
        )
        for c in range(chunks)
    ]
    copies[0].start()
    weights = pltpu.make_async_copy(weight_ref.at[:, pl.ds(0, 2 * width)], weight, weight_sem)
    weights.start()
    for copy in copies[1:]:
        copy.start()
    gain = gain_ref[...]
    bias = bias_ref[...]
    first = lane_mask((length, 256))
    acc[...] = jnp.zeros_like(acc)

    def step(c, carry):
        pltpu.make_async_copy(rows_0_ref.at[pl.ds(0, span), :], landed.at[c], sem.at[c]).wait()
        start = c * CHUNK_ROWS
        normed = normalized(landed[c], gain, bias)

        @pl.when(c == 0)
        def _():
            weights.wait()

        packed = jnp.dot(
            normed, weight[...], preferred_element_type=jnp.float32
        ).astype(jnp.bfloat16)
        for pair in range(PAIRS):
            lanes = slice(pair * 128, pair * 128 + 128)
            key_lanes = slice(width + pair * 128, width + pair * 128 + 128)
            total = None
            for r in range(0, CHUNK_ROWS, 2):
                query_parts = []
                key_parts = []
                for k in (r, r + 1):
                    own = slice(k * length, (k + 1) * length)
                    query = packed[own, lanes]
                    query_parts.append(
                        jnp.where(live_ref[start + k] > 0, query, jnp.zeros_like(query))
                    )
                    key_parts.append(packed[own, key_lanes])
                query = jnp.concatenate(query_parts, axis=1)
                key = jnp.concatenate(key_parts, axis=1)
                zero = jnp.zeros_like(query)
                both = jnp.concatenate(
                    [jnp.where(first, query, zero), jnp.where(first, zero, query)], axis=0
                )
                part = lax.dot_general(
                    both, key, (((1,), (1,)), ((), ())), preferred_element_type=jnp.float32
                )
                total = part if total is None else total + part
            acc[pl.ds(pair * 2 * length, 2 * length), :] += total
        return carry

    lax.fori_loop(0, chunks, step, 0)
    quarter = H * length // 4
    tied = jnp.concatenate([acc[pl.ds(q * quarter, quarter), :] for q in range(4)], axis=1)
    tied_ref[...] = tied
    tied_low_ref[...] = tied.astype(jnp.bfloat16)


def front(live, rows, gain, bias, weight):
    row_count = live.shape[0]
    width = rows[0].shape[1]
    length = rows[0].shape[0] * PARTS // row_count
    quarter = H * length // 4
    vmem = pl.BlockSpec(memory_space=pltpu.VMEM)
    smem = pl.BlockSpec(memory_space=pltpu.SMEM)
    return pl.pallas_call(
        front_kernel,
        out_shape=(
            jax.ShapeDtypeStruct((quarter, 4 * length), jnp.float32),
            jax.ShapeDtypeStruct((quarter, 4 * length), jnp.bfloat16),
        ),
        in_specs=[smem]
        + [pl.BlockSpec(memory_space=pltpu.HBM)] * PARTS
        + [vmem, vmem, pl.BlockSpec(memory_space=pltpu.HBM)],
        out_specs=(vmem, vmem),
        scratch_shapes=[
            pltpu.VMEM((row_count // CHUNK_ROWS, CHUNK_ROWS * length, width), jnp.bfloat16),
            pltpu.VMEM((width, 2 * width), jnp.bfloat16),
            pltpu.VMEM((H * length, length), jnp.float32),
            pltpu.SemaphoreType.DMA((row_count // CHUNK_ROWS,)),
            pltpu.SemaphoreType.DMA,
        ],
        compiler_params=pltpu.CompilerParams(vmem_limit_bytes=40 << 20),
        name="front",
        interpret=INTERPRET,
    )(live, *rows, gain, bias, pltpu.with_memory_space_constraint(weight, pltpu.HBM))


def belongs(meta_ref, step):
    other = meta_ref[0] + step
    return jnp.logical_and(other >= meta_ref[1], other < meta_ref[2])


def join_kernel(meta_ref, tied_ref, below_ref, above_ref, sum_ref, up_ref, down_ref):
    tied = tied_ref[...]
    below = jnp.where(belongs(meta_ref, -1), below_ref[...].astype(jnp.float32), 0.0)
    above = jnp.where(belongs(meta_ref, 1), above_ref[...].astype(jnp.float32), 0.0)
    sum_ref[...] = tied + below + above
    up_ref[...] = (tied + below).astype(jnp.bfloat16)
    down_ref[...] = (tied + above).astype(jnp.bfloat16)


def join(meta, tied, below, above):
    vmem = pl.BlockSpec(memory_space=pltpu.VMEM)
    return pl.pallas_call(
        join_kernel,
        out_shape=(
            jax.ShapeDtypeStruct(tied.shape, jnp.float32),
            jax.ShapeDtypeStruct(tied.shape, jnp.bfloat16),
            jax.ShapeDtypeStruct(tied.shape, jnp.bfloat16),
        ),
        in_specs=[pl.BlockSpec(memory_space=pltpu.SMEM), vmem, vmem, vmem],
        out_specs=(vmem, vmem, vmem),
        name="join",
        interpret=INTERPRET,
    )(meta, tied, below, above)


def middle_kernel(live_ref, meta_ref, tied_ref, below_ref, above_ref, out_ref):
    length = tied_ref.shape[1] // 4
    tied = tied_ref[...]
    tied = tied + jnp.where(belongs(meta_ref, -2), below_ref[...].astype(jnp.float32), 0.0)
    tied = tied + jnp.where(belongs(meta_ref, 2), above_ref[...].astype(jnp.float32), 0.0)
    quarter = tied.shape[0]
    count = jnp.full((1, length), meta_ref[3], jnp.int32).astype(jnp.float32)
    scale = DH ** (-0.5) / jnp.sqrt(count)
    logits = (
        jnp.concatenate([tied[:, q * length : (q + 1) * length] for q in range(4)], axis=0) * scale
    )
    top = jnp.max(logits, axis=-1, keepdims=True)
    raised = jnp.exp(logits - top)
    attention = raised / jnp.sum(raised, axis=-1, keepdims=True)
    out_ref[pl.ds(0, quarter), :] = jnp.concatenate(
        [attention[q * quarter : (q + 1) * quarter] for q in range(4)], axis=1
    ).astype(jnp.bfloat16)
    lane = lax.broadcasted_iota(jnp.int32, (16, 4 * length), 1)
    live = jnp.zeros((16, 4 * length), jnp.float32)
    for m in range(live_ref.shape[0]):
        live = jnp.where(jnp.logical_and(lane == m, live_ref[m] > 0), 1.0, live)
    out_ref[pl.ds(quarter, 16), :] = live.astype(jnp.bfloat16)


def middle(live, meta, tied, neighbours):
    vmem = pl.BlockSpec(memory_space=pltpu.VMEM)
    smem = pl.BlockSpec(memory_space=pltpu.SMEM)
    return pl.pallas_call(
        middle_kernel,
        out_shape=jax.ShapeDtypeStruct((tied.shape[0] + 16, tied.shape[1]), jnp.bfloat16),
        in_specs=[smem, smem] + [vmem] * (1 + len(neighbours)),
        out_specs=vmem,
        name="middle",
        interpret=INTERPRET,
    )(live, meta, tied, *neighbours)


def values_kernel(rows_ref, bundle_ref, out_ref, landed, sem):
    chunks = landed.shape[0]
    span, width = landed.shape[1:]

    def arrival(c):
        return pltpu.make_async_copy(
            rows_ref.at[pl.ds(c * span, span), :], landed.at[c], sem.at[c]
        )

    for c in range(chunks):
        arrival(c).start()
    affine = bundle_ref[pl.ds(2 * width, 16), :].astype(jnp.float32)
    gain = (affine[0:1] + affine[1:2]) + affine[2:3]
    bias = (affine[3:4] + affine[4:5]) + affine[5:6]
    weight = bundle_ref[pl.ds(0, width), :]

    def step(c, carry):
        arrival(c).wait()
        out_ref[c] = jnp.dot(
            normalized(landed[c], gain, bias), weight, preferred_element_type=jnp.float32
        ).astype(jnp.bfloat16)
        return carry

    lax.fori_loop(0, chunks, step, 0)


def values_of(rows, bundled, row_count):
    vmem = pl.BlockSpec(memory_space=pltpu.VMEM)
    tokens, width = rows.shape
    chunks = row_count // PARTS // CHUNK_ROWS
    shape = (chunks, tokens // chunks, width)
    return pl.pallas_call(
        values_kernel,
        out_shape=jax.ShapeDtypeStruct(shape, jnp.bfloat16),
        in_specs=[pl.BlockSpec(memory_space=pltpu.HBM), vmem],
        out_specs=vmem,
        scratch_shapes=[pltpu.VMEM(shape, jnp.bfloat16), pltpu.SemaphoreType.DMA((chunks,))],
        compiler_params=pltpu.CompilerParams(vmem_limit_bytes=40 << 20),
        name="values",
        interpret=INTERPRET,
    )(rows, bundled)


def finish_kernel(attention_ref, bundle_ref, *refs):
    rows_refs, values_refs = refs[:PARTS], refs[PARTS : 2 * PARTS]
    out_ref, landed, held, mask, row_sem, value_sem, out_sem = refs[2 * PARTS :]
    chunks = landed.shape[0]
    span, width = landed.shape[1:]
    length = span // CHUNK_ROWS
    quarter = H * length // 4
    each = chunks // PARTS
    for c in range(chunks):
        part = c // each
        pltpu.make_async_copy(values_refs[part].at[c % each], held.at[c], value_sem.at[c]).start()
        pltpu.make_async_copy(
            rows_refs[part].at[pl.ds(c % each * span, span), :], landed.at[c], row_sem.at[c]
        ).start()

    def leaving(c):
        return pltpu.make_async_copy(
            held.at[c], out_ref.at[pl.ds(c * span, span), :], out_sem.at[c]
        )

    packed = attention_ref[pl.ds(0, quarter), :]
    attention = jnp.concatenate(
        [packed[:, q * length : (q + 1) * length] for q in range(4)], axis=0
    )
    live = attention_ref[pl.ds(quarter, 16), :].astype(jnp.float32)
    for m in range(chunks * CHUNK_ROWS):
        mask[m // CHUNK_ROWS, pl.ds(m % CHUNK_ROWS * length, length), :] = jnp.broadcast_to(
            live[0:1, m : m + 1], (length, 128)
        )
    wide = jnp.concatenate([attention] * CHUNK_ROWS, axis=1)
    diagonal = (
        lax.broadcasted_iota(jnp.int32, (span, span), 0) // length
        == lax.broadcasted_iota(jnp.int32, (span, span), 1) // length
    )
    first = lane_mask((span, 128))
    mixers = []
    for h in range(H):
        tall = jnp.concatenate([wide[h * length : (h + 1) * length]] * CHUNK_ROWS, axis=0)
        mixers.append(jnp.where(diagonal, tall, jnp.zeros_like(tall)))
    weight = bundle_ref[pl.ds(width, width), :]

    def step(c, carry):
        pltpu.make_async_copy(values_refs[0].at[0], held.at[c], value_sem.at[c]).wait()
        values = held[c]
        parts = []
        for pair in range(PAIRS):
            lanes = values[:, pair * 128 : pair * 128 + 128]
            low = jnp.dot(mixers[2 * pair], lanes, preferred_element_type=jnp.float32)
            high = jnp.dot(mixers[2 * pair + 1], lanes, preferred_element_type=jnp.float32)
            parts.append(jnp.where(first, low, high).astype(jnp.bfloat16))
        attended = jnp.concatenate(parts, axis=1)
        mixed = jnp.dot(attended, weight, preferred_element_type=jnp.float32)
        pltpu.make_async_copy(
            rows_refs[0].at[pl.ds(0, span), :], landed.at[c], row_sem.at[c]
        ).wait()
        mixed = mixed + landed[c].astype(jnp.float32)
        held[c] = (mixed * jnp.concatenate([mask[c]] * (width // 128), axis=1)).astype(
            jnp.bfloat16
        )
        leaving(c).start()
        return carry

    lax.fori_loop(0, chunks, step, 0)
    for c in range(chunks):
        leaving(c).wait()


def finish(attention, bundled, rows, values):
    vmem = pl.BlockSpec(memory_space=pltpu.VMEM)
    hbm = pl.BlockSpec(memory_space=pltpu.HBM)
    anywhere = pl.BlockSpec(memory_space=pl.ANY)
    tokens, width = rows[0].shape
    each, span, _ = values[0].shape
    shape = (each * PARTS, span, width)
    return pl.pallas_call(
        finish_kernel,
        out_shape=jax.ShapeDtypeStruct((tokens * PARTS, width), jnp.bfloat16),
        in_specs=[vmem, vmem] + [hbm] * PARTS + [anywhere] * PARTS,
        out_specs=hbm,
        scratch_shapes=[
            pltpu.VMEM(shape, jnp.bfloat16),
            pltpu.VMEM(shape, jnp.bfloat16),
            pltpu.VMEM((each * PARTS, span, 128), jnp.float32),
            pltpu.SemaphoreType.DMA((each * PARTS,)),
            pltpu.SemaphoreType.DMA((each * PARTS,)),
            pltpu.SemaphoreType.DMA((each * PARTS,)),
        ],
        compiler_params=pltpu.CompilerParams(vmem_limit_bytes=40 << 20),
        name="finish",
        interpret=INTERPRET,
    )(attention, bundled, *rows, *values)


def shifted(value, axis, steps, wrap):
    count = lax.axis_size(axis)
    if wrap:
        route = [(i, (i + steps) % count) for i in range(count)]
    else:
        route = [(i, i + steps) for i in range(count) if 0 <= i + steps < count]
    return lax.ppermute(value, axis, route)


ROUTE = ((11, 9, 6, 4), (10, 5), 12)
Z_STAY = 8
RING_Z = 8
RING_X = 4


def plan_kernel(
    position_ref, groups_ref, targets_ref, partner_ref, table_ref, meta_ref, pick_ref
):
    peers, row_count = targets_ref.shape
    pair_count = row_count // 2
    position = position_ref[0]
    shape = (peers, 128)
    down = lax.broadcasted_iota(jnp.int32, shape, 0)
    across = lax.broadcasted_iota(jnp.int32, shape, 1)
    zero = jnp.zeros(shape, jnp.int32)

    def over_lanes(value):
        return jnp.broadcast_to(jnp.sum(value, axis=1, keepdims=True), shape)

    def over_rows(value):
        return jnp.broadcast_to(jnp.sum(value, axis=0, keepdims=True), shape)

    def top_rows(value):
        return jnp.max(value, axis=0, keepdims=True)

    def flag(condition):
        return jnp.where(condition, 1, zero)

    def to_lanes(value):
        return over_rows(jnp.where(down == across, value, zero))

    def to_rows(value):
        return over_lanes(jnp.where(down == across, value, zero))

    targets = jnp.concatenate(
        [targets_ref[...], jnp.full((peers, 128 - row_count), -1, jnp.int32)], axis=1
    )
    device = targets >> 5
    offset = jnp.where(targets >= 0, (device - down) & (peers - 1), -1)
    seen = zero
    for i in range(row_count):
        seen = seen | flag(jnp.broadcast_to(offset[:, i : i + 1], shape) == across)
    present_l = flag(over_rows(seen) > 0)
    present = to_rows(present_l)
    odd = down & 1
    odd_l = across & 1

    def turns(core):
        step = ((down + odd * (1 - 2 * core)) >> 1) & 31
        step_l = ((across + odd_l * (1 - 2 * core)) >> 1) & 31
        u, u_l = step & 7, step_l & 7
        order = u * 64 + down
        order_l = u_l * 64 + across
        moving = present * flag(u > 0)
        moving_l = present_l * flag(u_l > 0)
        rank = over_lanes(moving_l * flag(order_l < order))
        rest = over_lanes((present_l - moving_l) * flag(order_l < order))
        return step >> 3, u, moving, rank, rest

    def split_of(core):
        caps = ROUTE[0]
        _, u, moving, rank, _ = turns(core)
        early = moving * flag(rank < across)
        late = moving - early
        good = flag(across <= pair_count)
        for h in range(1, 6):
            cap = caps[h - 1] if h <= len(caps) else 0
            good = good * flag(over_rows(early * flag(u >= h)) <= cap)
            good = good * flag(over_rows(late * flag(RING_Z - u >= h)) <= cap)
        split = jnp.min(jnp.where(good > 0, across, 127), axis=1, keepdims=True)
        return jnp.broadcast_to(split, shape)

    def z_lanes(core, split):
        (z1, z2, z3, z4) = ROUTE[0]
        _, u, moving, rank, rest = turns(core)
        plus = moving * flag(rank < split)
        staying = present - moving
        hops = jnp.where(plus > 0, u, RING_Z - u)
        place = jnp.where(plus > 0, split - 1 - rank, rank - split)
        base = jnp.where(
            hops == 1, 0, jnp.where(hops == 2, z1, jnp.where(hops == 3, z1 + z2, z1 + z2 + z3))
        )
        side = moving - plus
        z_all = z1 + z2 + z3 + z4
        z_leave = jnp.where(staying > 0, 2 * z1 + rest, side * z1 + place)
        z_land = jnp.where(staying > 0, 2 * z_all + rest, side * z_all + base + place)
        return jnp.where(present > 0, z_leave, -1), jnp.where(present > 0, z_land, -1)

    def x_counts(core, line):
        high, u, _, _, _ = turns(core)
        turn = (high + flag(line < u)) & (RING_X - 1)
        turn = jnp.where(present > 0, turn, -1)
        count = [over_rows(flag(turn == v)) for v in range(RING_X)]
        x2 = ROUTE[1][1]
        ahead = (count[2] + count[3] - count[1] + 1) >> 1
        ahead = jnp.minimum(
            jnp.maximum(ahead, jnp.maximum(count[2] - x2, 0)), jnp.minimum(count[2], x2)
        )
        return turn, count, ahead

    def fits(core):
        x1, x2 = ROUTE[1]
        _, count, ahead = x_counts(core, across)
        behind = count[2] - ahead
        good = (
            flag(ahead <= x2)
            * flag(behind <= x2)
            * flag(ahead + count[1] <= x1)
            * flag(behind + count[3] <= x1)
            * flag(count[0] <= ROUTE[2])
        )
        return jnp.min(jnp.where(across < RING_Z, good, 1))

    def x_lanes(core, line):
        x1, x2 = ROUTE[1]
        turn, count, ahead = x_counts(core, line)
        turn_l = to_lanes(turn)
        level = over_lanes(present_l * flag(turn_l == turn) * flag(across < down))
        double = flag(turn == 2)
        near = double * flag(level < ahead)
        forward = flag(turn == 1) + near
        spot = jnp.where(
            double > 0,
            level - jnp.where(near > 0, 0, ahead),
            level + jnp.where(turn == 1, ahead, count[2] - ahead),
        )
        side = 1 - forward
        x_leave = jnp.where(turn == 0, 2 * x1 + level, side * x1 + spot)
        x_land = jnp.where(
            turn == 0, 2 * (x1 + x2) + level, side * (x1 + x2) + double * x1 + spot
        )
        return jnp.where(present > 0, x_leave, -1), jnp.where(present > 0, x_land, -1)

    core = position & 1
    split = split_of(core)
    z_leave, z_land = z_lanes(core, split)
    line = (position >> 1) & (RING_Z - 1)
    x_leave_a, x_land_a = x_lanes(core, line)
    x_leave_b, x_land_b = x_lanes(core, RING_Z - 1 - line)
    other_split = split_of(1 - core)
    good = jnp.where(
        jnp.max(jnp.maximum(split, other_split)) <= pair_count, fits(core) * fits(1 - core), 0
    )

    lane_row = lax.broadcasted_iota(jnp.int32, (1, 128), 1)
    origin = -1 + zero
    for b in range(2):
        sender = position if b == 0 else position ^ 1
        mine = targets_ref[pl.ds(sender, 1), :]
        mine = jnp.concatenate([mine, jnp.full((1, 128 - row_count), -1, jnp.int32)], axis=1)
        away = ((mine >> 5) - sender) & (peers - 1)
        away = jnp.where(mine >= 0, away, -1)
        away = jnp.where((away & 1) == b, away, -1)
        hit = jnp.broadcast_to(away, shape) == down
        code = b * pair_count + (jnp.broadcast_to(lane_row, shape) >> 1)
        found = jnp.max(jnp.where(hit, code, -1), axis=1, keepdims=True)
        origin = jnp.maximum(origin, jnp.broadcast_to(found, shape))

    def gathered(slot_of, value):
        return top_rows(jnp.where(slot_of == across, value, -1))

    local = targets - position * row_count
    here = jnp.logical_and(local >= 0, local < row_count)
    settled_a = jnp.full((1, 128), -1, jnp.int32)
    settled_b = settled_a
    lane_full = across & 1
    for r in range(2):
        slot = jnp.max(
            jnp.where(jnp.logical_and(here, lane_full == r), local, -1), axis=1, keepdims=True
        )
        slot = jnp.broadcast_to(slot, shape)
        slot_l = over_rows(jnp.where(down == across, slot + 1, zero)) - 1
        match = across == ((position - down) & (peers - 1))
        slot_by_offset = over_lanes(jnp.where(match, slot_l + 1, zero)) - 1
        settled_a = jnp.maximum(settled_a, gathered(slot_by_offset, x_land_a * 2 + r))
        settled_b = jnp.maximum(settled_b, gathered(slot_by_offset, z_land * 2 + r))
    empty = jnp.full((1, 128), -1, jnp.int32)
    table_ref[...] = jnp.concatenate(
        [
            gathered(z_leave, origin),
            gathered(x_leave_b, origin),
            gathered(x_leave_a, z_land),
            gathered(z_leave, x_land_b),
            settled_a,
            settled_b,
            empty,
            empty,
        ],
        axis=0,
    )
    groups = groups_ref[...]
    lane = lax.broadcasted_iota(jnp.int32, groups.shape, 1)
    own_group = jnp.sum(jnp.where(lane == position, groups, 0))
    low = jnp.sum(jnp.where(groups < own_group, 1, 0))
    high = low + jnp.sum(jnp.where(groups == own_group, 1, 0))
    inside = jnp.logical_and(targets >= low * row_count, targets < high * row_count)
    meta_ref[0] = position
    meta_ref[1] = low
    meta_ref[2] = high
    meta_ref[3] = jnp.sum(jnp.where(inside, 1, 0))
    pick_ref[0] = good


def plan(position, groups, targets, partner):
    vmem = pl.BlockSpec(memory_space=pltpu.VMEM)
    smem = pl.BlockSpec(memory_space=pltpu.SMEM)
    return pl.pallas_call(
        plan_kernel,
        out_shape=(
            jax.ShapeDtypeStruct((8, 128), jnp.int32),
            jax.ShapeDtypeStruct((4,), jnp.int32),
            jax.ShapeDtypeStruct((1,), jnp.int32),
        ),
        in_specs=[smem, vmem, vmem, pl.BlockSpec(memory_space=pltpu.HBM)],
        out_specs=(vmem, smem, smem),
        name="plan",
        interpret=INTERPRET,
    )(position.reshape(1), groups, targets, partner)


def pieces(value):
    parts = []
    for _ in range(3):
        part = value.astype(jnp.bfloat16)
        parts.append(part.astype(jnp.float32))
        value = value - parts[-1]
    return parts


def bundle_kernel(weight_ref, out_weight_ref, gain_ref, bias_ref, out_ref, held, sem):
    width = held.shape[1]
    loads = [
        pltpu.make_async_copy(
            weight_ref.at[:, pl.ds(2 * width, width)], held.at[pl.ds(0, width), :], sem.at[0]
        ),
        pltpu.make_async_copy(out_weight_ref, held.at[pl.ds(width, width), :], sem.at[1]),
    ]
    for load in loads:
        load.start()
    rows = pieces(gain_ref[...]) + pieces(bias_ref[...])
    rows.append(jnp.zeros((16 - len(rows), width), jnp.float32))
    held[pl.ds(2 * width, 16), :] = jnp.concatenate(rows, axis=0).astype(jnp.bfloat16)
    for load in loads:
        load.wait()
    store = pltpu.make_async_copy(held, out_ref, sem.at[2])
    store.start()
    store.wait()


def bundle(weight, out_weight, gain, bias):
    width = weight.shape[0]
    vmem = pl.BlockSpec(memory_space=pltpu.VMEM)
    hbm = pl.BlockSpec(memory_space=pltpu.HBM)
    shape = (2 * width + 16, width)
    return pl.pallas_call(
        bundle_kernel,
        out_shape=jax.ShapeDtypeStruct(shape, weight.dtype),
        in_specs=[hbm, hbm, vmem, vmem],
        out_specs=hbm,
        scratch_shapes=[pltpu.VMEM(shape, weight.dtype), pltpu.SemaphoreType.DMA((3,))],
        name="bundle",
        interpret=INTERPRET,
    )(weight, out_weight, gain, bias)


def deal(table_ref, row, pool, outs):
    lane = 0
    for out in outs:

        def step(k, carry, out=out, lane=lane):
            out[k] = pool[jnp.maximum(table_ref[row, lane + k], 0)]
            return carry

        lax.fori_loop(0, out.shape[0], step, 0)
        lane += out.shape[0]


def leave_kernel(part, table_ref, own_ref, partner_ref, *refs):
    outs, (pool, sem) = refs[:-2], refs[-2:]
    pairs = own_ref.shape[0]
    half = own_ref.shape[2] // 2
    copies = [
        pltpu.make_async_copy(
            ref.at[:, :, pl.ds(part * half, half), :],
            pool.at[pl.ds(b * pairs, pairs)],
            sem.at[b],
        )
        for b, ref in enumerate((own_ref, partner_ref))
    ]
    for copy in copies:
        copy.start()
    for copy in copies:
        copy.wait()
    deal(table_ref, part, pool, outs)


def leave(part, table, own, partner, sizes):
    pairs, two, length, width = own.shape
    vmem = pl.BlockSpec(memory_space=pltpu.VMEM)
    anywhere = pl.BlockSpec(memory_space=pl.ANY)
    return pl.pallas_call(
        functools.partial(leave_kernel, part),
        out_shape=tuple(
            jax.ShapeDtypeStruct((n, two, length // 2, width), own.dtype) for n in sizes
        ),
        in_specs=[pl.BlockSpec(memory_space=pltpu.SMEM), anywhere, anywhere],
        out_specs=(vmem,) * len(sizes),
        scratch_shapes=[
            pltpu.VMEM((2 * pairs, two, length // 2, width), own.dtype),
            pltpu.SemaphoreType.DMA((2,)),
        ],
        compiler_params=pltpu.CompilerParams(vmem_limit_bytes=40 << 20),
        name="leave",
        interpret=INTERPRET,
    )(table, own, partner)


def pooled(refs, pool, sem):
    copies = []
    start = 0
    for ref in refs:
        count = ref.shape[0]
        copies.append(
            pltpu.make_async_copy(ref, pool.at[pl.ds(start, count)], sem.at[len(copies)])
        )
        start += count
    return copies


def turn_kernel(row, count, table_ref, *refs):
    sources, outs, (pool, sem) = refs[:count], refs[count:-2], refs[-2:]
    copies = pooled(sources, pool, sem)
    for copy in copies:
        copy.start()
    for copy in copies:
        copy.wait()
    deal(table_ref, row, pool, outs)


def turn_over(table, row, sources, sizes):
    vmem = pl.BlockSpec(memory_space=pltpu.VMEM)
    anywhere = pl.BlockSpec(memory_space=pl.ANY)
    payload = sources[0].shape[1:]
    return pl.pallas_call(
        functools.partial(turn_kernel, row, len(sources)),
        out_shape=tuple(jax.ShapeDtypeStruct((n,) + payload, sources[0].dtype) for n in sizes),
        in_specs=[pl.BlockSpec(memory_space=pltpu.SMEM)] + [anywhere] * len(sources),
        out_specs=(vmem,) * len(sizes),
        scratch_shapes=[
            pltpu.VMEM((sum(s.shape[0] for s in sources),) + payload, sources[0].dtype),
            pltpu.SemaphoreType.DMA((len(sources),)),
        ],
        compiler_params=pltpu.CompilerParams(vmem_limit_bytes=40 << 20),
        name="turn_over",
        interpret=INTERPRET,
    )(table, *sources)


def land_kernel(part, count, table_ref, *refs):
    sources = refs[:count]
    outs = refs[-PARTS - 5 : -5]
    live_ref, pool, done, in_sem, out_sem = refs[-5:]
    row_count, half, _ = done.shape
    copies = pooled(sources, pool, in_sem)
    for copy in copies:
        copy.start()
    for copy in copies:
        copy.wait()

    def step(m, carry):
        live = table_ref[4 + part, m] >= 0
        live_ref[m] = jnp.where(live, 1, 0)
        code = jnp.maximum(table_ref[4 + part, m], 0)
        value = pool[code >> 1, code & 1]
        done[m] = jnp.where(live, value, jnp.zeros_like(value))
        return carry

    rows = row_count // PARTS
    leaving = [
        pltpu.make_async_copy(
            done.at[pl.ds(k * rows, rows)],
            out.at[:, pl.ds(part * half, half), :],
            out_sem.at[k],
        )
        for k, out in enumerate(outs)
    ]
    for k in range(PARTS):
        lax.fori_loop(k * rows, (k + 1) * rows, step, 0)
        leaving[k].start()
    for copy in leaving:
        copy.wait()


def land(part, table, sources, row_count, length, begun):
    anywhere = pl.BlockSpec(memory_space=pl.ANY)
    smem = pl.BlockSpec(memory_space=pltpu.SMEM)
    hbm = pl.BlockSpec(memory_space=pltpu.HBM)
    two, half, width = sources[0].shape[1:]
    dtype = sources[0].dtype
    count = len(sources)
    return pl.pallas_call(
        functools.partial(land_kernel, part, count),
        out_shape=(jax.ShapeDtypeStruct((row_count // PARTS, length, width), dtype),) * PARTS
        + (jax.ShapeDtypeStruct((row_count,), jnp.int32),),
        in_specs=[smem] + [anywhere] * count + [hbm] * len(begun),
        out_specs=(hbm,) * PARTS + (smem,),
        scratch_shapes=[
            pltpu.VMEM((sum(s.shape[0] for s in sources), two, half, width), dtype),
            pltpu.VMEM((row_count, half, width), dtype),
            pltpu.SemaphoreType.DMA((count,)),
            pltpu.SemaphoreType.DMA((PARTS,)),
        ],
        input_output_aliases={1 + count + k: k for k in range(len(begun))},
        compiler_params=pltpu.CompilerParams(vmem_limit_bytes=40 << 20),
        name="land",
        interpret=INTERPRET,
    )(table, *sources, *begun)


def chain(forward, backward, caps, step, ring):
    def moved(i, by):
        return (i // (step * ring)) * step * ring + (i + by * step) % (step * ring)

    devices = range(lax.axis_size("depth"))
    onward, returning = [], []
    for cap in caps:
        forward = lax.ppermute(forward[:cap], "depth", [(i, moved(i, 1)) for i in devices])
        backward = lax.ppermute(backward[:cap], "depth", [(i, moved(i, -1)) for i in devices])
        onward.append(forward)
        returning.append(backward)
    return onward + returning


def routed(route, table, own, partner):
    z_caps, x_caps, x_stay = route
    z_sizes = (z_caps[0], z_caps[0], Z_STAY)
    x_sizes = (x_caps[0], x_caps[0], x_stay)
    z_plus, z_minus, z_still = leave(0, table, own, partner, z_sizes)
    x_plus, x_minus, x_still = leave(1, table, own, partner, x_sizes)
    along_x = chain(x_plus, x_minus, x_caps, 2 * RING_Z, RING_X)
    along_z = chain(z_plus, z_minus, z_caps, 2, RING_Z)
    later = turn_over(table, 3, along_x + [x_still], z_sizes)
    last_b = chain(later[0], later[1], z_caps, 2, RING_Z)
    turned = turn_over(table, 2, along_z + [z_still], x_sizes)
    last_a = chain(turned[0], turned[1], x_caps, 2 * RING_Z, RING_X)
    row_count, length = own.shape[0] * own.shape[1], own.shape[2]
    *begun, _ = land(0, table, last_a + [turned[2]], row_count, length, ())
    return land(1, table, last_b + [later[2]], row_count, length, begun)


def dense(targets, everywhere, own):
    row_count = targets.shape[0]
    _, _, length, width = own.shape
    peers = lax.axis_size("depth")
    position = lax.axis_index("depth")
    capacity = max(2, (row_count + peers - 1) // peers)
    slots = jnp.where(
        targets >= 0,
        targets // row_count * capacity + jnp.arange(row_count) % capacity,
        -1,
    )
    outgoing = spread(own.reshape(row_count, length, width), slots, peers * capacity)
    got = lax.all_to_all(
        outgoing.reshape((peers, capacity, length, width)),
        "depth",
        split_axis=0,
        concat_axis=0,
        tiled=True,
    ).reshape(peers * capacity, length, width)
    local = everywhere - position * row_count
    mine = jnp.logical_and(local >= 0, local < row_count)
    code = (
        lax.broadcasted_iota(jnp.int32, (peers, row_count), 0) * capacity
        + lax.broadcasted_iota(jnp.int32, (peers, row_count), 1) % capacity
    )
    wanted = jnp.where(mine, local, -1).reshape(1, -1)
    hit = jnp.arange(row_count)[:, None] == wanted
    source = jnp.max(jnp.where(hit, code.reshape(1, -1), -1), axis=1)
    return (*settle(source, got), (source >= 0).astype(jnp.int32))


def layer(
    alignment_input,
    target_slot,
    device_alignment,
    layer_norm_gain,
    layer_norm_bias,
    query_key_value_weight,
    output_weight,
):
    targets = target_slot[0]
    row_count, length, width = alignment_input.shape[1:]
    peers = lax.axis_size("depth")
    position = lax.axis_index("depth")
    own = alignment_input.reshape(row_count // 2, 2, length, width)
    everywhere = lax.all_to_all(
        jnp.broadcast_to(targets[None, None], (peers, 1, row_count)),
        "depth",
        split_axis=0,
        concat_axis=0,
        tiled=True,
    ).reshape(peers, row_count)
    partner = lax.ppermute(own, "depth", [(i, i ^ 1) for i in range(peers)])
    bundled = bundle(query_key_value_weight[0], output_weight[0], layer_norm_gain, layer_norm_bias)
    bundled = shifted(bundled, "section", 1, True)
    table, meta, pick = plan(position, device_alignment, everywhere, partner)
    *settled, live = lax.switch(
        pick[0],
        [
            lambda t, o, p, a, b: dense(a, b, o),
            lambda t, o, p, a, b: routed(ROUTE, t, o, p),
        ],
        table,
        own,
        partner,
        targets,
        everywhere,
    )
    balanced = [part.reshape(-1, width) for part in settled]
    earlier = [shifted(part, "section", 1, True) for part in balanced]
    tied, tied_low = front(
        live, balanced, layer_norm_gain, layer_norm_bias, query_key_value_weight[0]
    )
    tied, up, down = join(
        meta, tied, shifted(tied_low, "depth", 1, False), shifted(tied_low, "depth", -1, False)
    )
    neighbours = [shifted(up, "depth", 2, False), shifted(down, "depth", -2, False)]
    attention = middle(live, meta, tied, neighbours)
    attention = shifted(attention, "section", 1, True)
    values = []
    for rows in earlier:
        values.append(values_of(rows, bundled, row_count))
    handed = finish(attention, bundled, earlier, values)
    return handed.reshape(1, row_count, length, width)


def solution(mesh):
    placed = (
        P("section", "depth", None, None),
        P("section", "depth"),
        P("section", None),
        P("section", None),
        P("section", None),
        P("section", None, None),
        P("section", None, None),
    )
    return jax.shard_map(
        layer,
        mesh=mesh,
        in_specs=placed,
        out_specs=P("section", "depth", None, None),
        check_vma=False,
    )
```

```python
import functools

import jax
import jax.numpy as jnp
from jax import lax
from jax.experimental import pallas as pl
from jax.experimental.pallas import tpu as pltpu
from jax.sharding import PartitionSpec as P


H = 12
DH = 64
PAIRS = H // 2
EPSILON = 1e-05
CHUNK_ROWS = 8
PARTS = 2
INTERPRET = False


def spread_kernel(slot_ref, rows_ref, out_ref, sem):
    count = rows_ref.shape[0]

    def copy_of(i):
        return pltpu.make_async_copy(
            rows_ref.at[i], out_ref.at[jnp.maximum(slot_ref[i], 0)], sem.at[i]
        )

    def begin(i, carry):
        @pl.when(slot_ref[i] >= 0)
        def _():
            copy_of(i).start()

        return carry

    def finish(i, carry):
        @pl.when(slot_ref[i] >= 0)
        def _():
            copy_of(i).wait()

        return carry

    lax.fori_loop(0, count, begin, 0)
    lax.fori_loop(0, count, finish, 0)


def spread(rows, slots, slot_count):
    return pl.pallas_call(
        spread_kernel,
        out_shape=jax.ShapeDtypeStruct((slot_count,) + rows.shape[1:], rows.dtype),
        in_specs=[
            pl.BlockSpec(memory_space=pltpu.SMEM),
            pl.BlockSpec(memory_space=pltpu.VMEM),
        ],
        out_specs=pl.BlockSpec(memory_space=pltpu.HBM),
        scratch_shapes=[pltpu.SemaphoreType.DMA((rows.shape[0],))],
        name="spread",
        interpret=INTERPRET,
    )(slots, rows)


def settle_kernel(source_ref, rows_ref, *refs):
    outs, (landed, in_sem, out_sem) = refs[:PARTS], refs[PARTS:]
    row_count = landed.shape[0]
    part = row_count // PARTS

    def arrival(m):
        return pltpu.make_async_copy(
            rows_ref.at[jnp.maximum(source_ref[m], 0)], landed.at[m], in_sem.at[m]
        )

    def begin(m, carry):
        arrival(m).start()
        return carry

    def empty(m, carry):
        arrival(m).wait()

        @pl.when(source_ref[m] < 0)
        def _():
            landed[m] = jnp.zeros_like(landed[m])

        return carry

    lax.fori_loop(0, row_count, begin, 0)
    lax.fori_loop(0, row_count, empty, 0)
    leaving = [
        pltpu.make_async_copy(landed.at[pl.ds(k * part, part)], out, out_sem.at[k])
        for k, out in enumerate(outs)
    ]
    for copy in leaving:
        copy.start()
    for copy in leaving:
        copy.wait()


def settle(source, rows):
    row_count = source.shape[0]
    length, width = rows.shape[1:]
    return pl.pallas_call(
        settle_kernel,
        out_shape=(jax.ShapeDtypeStruct((row_count // PARTS, length, width), rows.dtype),) * PARTS,
        in_specs=[
            pl.BlockSpec(memory_space=pltpu.SMEM),
            pl.BlockSpec(memory_space=pl.ANY),
        ],
        out_specs=(pl.BlockSpec(memory_space=pltpu.HBM),) * PARTS,
        scratch_shapes=[
            pltpu.VMEM((row_count, length, width), rows.dtype),
            pltpu.SemaphoreType.DMA((row_count,)),
            pltpu.SemaphoreType.DMA((PARTS,)),
        ],
        name="settle",
        interpret=INTERPRET,
    )(source, rows)


def lane_mask(shape):
    return lax.broadcasted_iota(jnp.int32, shape, len(shape) - 1) % 128 < DH


def normalized(block, gain, bias):
    widened = block.astype(jnp.float32)
    average = jnp.mean(widened, axis=-1, keepdims=True)
    centred = widened - average
    spread_of = jnp.mean(centred * centred, axis=-1, keepdims=True)
    return (centred * lax.rsqrt(spread_of + EPSILON) * gain + bias).astype(jnp.bfloat16)


def front_kernel(
    live_ref,
    rows_0_ref,
    rows_1_ref,
    gain_ref,
    bias_ref,
    weight_ref,
    tied_ref,
    tied_low_ref,
    landed,
    weight,
    acc,
    sem,
    weight_sem,
):
    row_count = live_ref.shape[0]
    width = rows_0_ref.shape[1]
    length = rows_0_ref.shape[0] * PARTS // row_count
    span = CHUNK_ROWS * length
    chunks = row_count // CHUNK_ROWS
    each = chunks // PARTS
    copies = [
        pltpu.make_async_copy(
            (rows_0_ref, rows_1_ref)[c // each].at[pl.ds(c % each * span, span), :],
            landed.at[c],
            sem.at[c],
        )
        for c in range(chunks)
    ]
    copies[0].start()
    weights = pltpu.make_async_copy(weight_ref.at[:, pl.ds(0, 2 * width)], weight, weight_sem)
    weights.start()
    for copy in copies[1:]:
        copy.start()
    gain = gain_ref[...]
    bias = bias_ref[...]
    first = lane_mask((length, 256))
    acc[...] = jnp.zeros_like(acc)

    def step(c, carry):
        pltpu.make_async_copy(rows_0_ref.at[pl.ds(0, span), :], landed.at[c], sem.at[c]).wait()
        start = c * CHUNK_ROWS
        normed = normalized(landed[c], gain, bias)

        @pl.when(c == 0)
        def _():
            weights.wait()

        packed = jnp.dot(
            normed, weight[...], preferred_element_type=jnp.float32
        ).astype(jnp.bfloat16)
        for pair in range(PAIRS):
            lanes = slice(pair * 128, pair * 128 + 128)
            key_lanes = slice(width + pair * 128, width + pair * 128 + 128)
            total = None
            for r in range(0, CHUNK_ROWS, 2):
                query_parts = []
                key_parts = []
                for k in (r, r + 1):
                    own = slice(k * length, (k + 1) * length)
                    query = packed[own, lanes]
                    query_parts.append(
                        jnp.where(live_ref[start + k] > 0, query, jnp.zeros_like(query))
                    )
                    key_parts.append(packed[own, key_lanes])
                query = jnp.concatenate(query_parts, axis=1)
                key = jnp.concatenate(key_parts, axis=1)
                zero = jnp.zeros_like(query)
                both = jnp.concatenate(
                    [jnp.where(first, query, zero), jnp.where(first, zero, query)], axis=0
                )
                part = lax.dot_general(
                    both, key, (((1,), (1,)), ((), ())), preferred_element_type=jnp.float32
                )
                total = part if total is None else total + part
            acc[pl.ds(pair * 2 * length, 2 * length), :] += total
        return carry

    lax.fori_loop(0, chunks, step, 0)
    quarter = H * length // 4
    tied = jnp.concatenate([acc[pl.ds(q * quarter, quarter), :] for q in range(4)], axis=1)
    tied_ref[...] = tied
    tied_low_ref[...] = tied.astype(jnp.bfloat16)


def front(live, rows, gain, bias, weight):
    row_count = live.shape[0]
    width = rows[0].shape[1]
    length = rows[0].shape[0] * PARTS // row_count
    quarter = H * length // 4
    vmem = pl.BlockSpec(memory_space=pltpu.VMEM)
    smem = pl.BlockSpec(memory_space=pltpu.SMEM)
    return pl.pallas_call(
        front_kernel,
        out_shape=(
            jax.ShapeDtypeStruct((quarter, 4 * length), jnp.float32),
            jax.ShapeDtypeStruct((quarter, 4 * length), jnp.bfloat16),
        ),
        in_specs=[smem]
        + [pl.BlockSpec(memory_space=pltpu.HBM)] * PARTS
        + [vmem, vmem, pl.BlockSpec(memory_space=pltpu.HBM)],
        out_specs=(vmem, vmem),
        scratch_shapes=[
            pltpu.VMEM((row_count // CHUNK_ROWS, CHUNK_ROWS * length, width), jnp.bfloat16),
            pltpu.VMEM((width, 2 * width), jnp.bfloat16),
            pltpu.VMEM((H * length, length), jnp.float32),
            pltpu.SemaphoreType.DMA((row_count // CHUNK_ROWS,)),
            pltpu.SemaphoreType.DMA,
        ],
        compiler_params=pltpu.CompilerParams(vmem_limit_bytes=40 << 20),
        name="front",
        interpret=INTERPRET,
    )(live, *rows, gain, bias, pltpu.with_memory_space_constraint(weight, pltpu.HBM))


def belongs(meta_ref, step):
    other = meta_ref[0] + step
    return jnp.logical_and(other >= meta_ref[1], other < meta_ref[2])


def join_kernel(meta_ref, tied_ref, below_ref, above_ref, sum_ref, up_ref, down_ref):
    tied = tied_ref[...]
    below = jnp.where(belongs(meta_ref, -1), below_ref[...].astype(jnp.float32), 0.0)
    above = jnp.where(belongs(meta_ref, 1), above_ref[...].astype(jnp.float32), 0.0)
    sum_ref[...] = tied + below + above
    up_ref[...] = (tied + below).astype(jnp.bfloat16)
    down_ref[...] = (tied + above).astype(jnp.bfloat16)


def join(meta, tied, below, above):
    vmem = pl.BlockSpec(memory_space=pltpu.VMEM)
    return pl.pallas_call(
        join_kernel,
        out_shape=(
            jax.ShapeDtypeStruct(tied.shape, jnp.float32),
            jax.ShapeDtypeStruct(tied.shape, jnp.bfloat16),
            jax.ShapeDtypeStruct(tied.shape, jnp.bfloat16),
        ),
        in_specs=[pl.BlockSpec(memory_space=pltpu.SMEM), vmem, vmem, vmem],
        out_specs=(vmem, vmem, vmem),
        name="join",
        interpret=INTERPRET,
    )(meta, tied, below, above)


def middle_kernel(live_ref, meta_ref, tied_ref, below_ref, above_ref, out_ref):
    length = tied_ref.shape[1] // 4
    tied = tied_ref[...]
    tied = tied + jnp.where(belongs(meta_ref, -2), below_ref[...].astype(jnp.float32), 0.0)
    tied = tied + jnp.where(belongs(meta_ref, 2), above_ref[...].astype(jnp.float32), 0.0)
    quarter = tied.shape[0]
    count = jnp.full((1, length), meta_ref[3], jnp.int32).astype(jnp.float32)
    scale = DH ** (-0.5) / jnp.sqrt(count)
    logits = (
        jnp.concatenate([tied[:, q * length : (q + 1) * length] for q in range(4)], axis=0) * scale
    )
    top = jnp.max(logits, axis=-1, keepdims=True)
    raised = jnp.exp(logits - top)
    attention = raised / jnp.sum(raised, axis=-1, keepdims=True)
    out_ref[pl.ds(0, quarter), :] = jnp.concatenate(
        [attention[q * quarter : (q + 1) * quarter] for q in range(4)], axis=1
    ).astype(jnp.bfloat16)
    lane = lax.broadcasted_iota(jnp.int32, (16, 4 * length), 1)
    live = jnp.zeros((16, 4 * length), jnp.float32)
    for m in range(live_ref.shape[0]):
        live = jnp.where(jnp.logical_and(lane == m, live_ref[m] > 0), 1.0, live)
    out_ref[pl.ds(quarter, 16), :] = live.astype(jnp.bfloat16)


def middle(live, meta, tied, neighbours):
    vmem = pl.BlockSpec(memory_space=pltpu.VMEM)
    smem = pl.BlockSpec(memory_space=pltpu.SMEM)
    return pl.pallas_call(
        middle_kernel,
        out_shape=jax.ShapeDtypeStruct((tied.shape[0] + 16, tied.shape[1]), jnp.bfloat16),
        in_specs=[smem, smem] + [vmem] * (1 + len(neighbours)),
        out_specs=vmem,
        name="middle",
        interpret=INTERPRET,
    )(live, meta, tied, *neighbours)


def values_kernel(rows_ref, bundle_ref, out_ref, landed, sem):
    chunks = landed.shape[0]
    span, width = landed.shape[1:]

    def arrival(c):
        return pltpu.make_async_copy(
            rows_ref.at[pl.ds(c * span, span), :], landed.at[c], sem.at[c]
        )

    for c in range(chunks):
        arrival(c).start()
    affine = bundle_ref[pl.ds(2 * width, 16), :].astype(jnp.float32)
    gain = (affine[0:1] + affine[1:2]) + affine[2:3]
    bias = (affine[3:4] + affine[4:5]) + affine[5:6]
    weight = bundle_ref[pl.ds(0, width), :]

    def step(c, carry):
        arrival(c).wait()
        out_ref[c] = jnp.dot(
            normalized(landed[c], gain, bias), weight, preferred_element_type=jnp.float32
        ).astype(jnp.bfloat16)
        return carry

    lax.fori_loop(0, chunks, step, 0)


def values_of(rows, bundled, row_count):
    vmem = pl.BlockSpec(memory_space=pltpu.VMEM)
    tokens, width = rows.shape
    chunks = row_count // PARTS // CHUNK_ROWS
    shape = (chunks, tokens // chunks, width)
    return pl.pallas_call(
        values_kernel,
        out_shape=jax.ShapeDtypeStruct(shape, jnp.bfloat16),
        in_specs=[pl.BlockSpec(memory_space=pltpu.HBM), vmem],
        out_specs=vmem,
        scratch_shapes=[pltpu.VMEM(shape, jnp.bfloat16), pltpu.SemaphoreType.DMA((chunks,))],
        compiler_params=pltpu.CompilerParams(vmem_limit_bytes=40 << 20),
        name="values",
        interpret=INTERPRET,
    )(rows, bundled)


def finish_kernel(attention_ref, bundle_ref, *refs):
    rows_refs, values_refs = refs[:PARTS], refs[PARTS : 2 * PARTS]
    out_ref, landed, held, mask, row_sem, value_sem, out_sem = refs[2 * PARTS :]
    chunks = landed.shape[0]
    span, width = landed.shape[1:]
    length = span // CHUNK_ROWS
    quarter = H * length // 4
    each = chunks // PARTS
    for c in range(chunks):
        part = c // each
        pltpu.make_async_copy(values_refs[part].at[c % each], held.at[c], value_sem.at[c]).start()
        pltpu.make_async_copy(
            rows_refs[part].at[pl.ds(c % each * span, span), :], landed.at[c], row_sem.at[c]
        ).start()

    def leaving(c):
        return pltpu.make_async_copy(
            held.at[c], out_ref.at[pl.ds(c * span, span), :], out_sem.at[c]
        )

    packed = attention_ref[pl.ds(0, quarter), :]
    attention = jnp.concatenate(
        [packed[:, q * length : (q + 1) * length] for q in range(4)], axis=0
    )
    live = attention_ref[pl.ds(quarter, 16), :].astype(jnp.float32)
    for m in range(chunks * CHUNK_ROWS):
        mask[m // CHUNK_ROWS, pl.ds(m % CHUNK_ROWS * length, length), :] = jnp.broadcast_to(
            live[0:1, m : m + 1], (length, 128)
        )
    wide = jnp.concatenate([attention] * CHUNK_ROWS, axis=1)
    diagonal = (
        lax.broadcasted_iota(jnp.int32, (span, span), 0) // length
        == lax.broadcasted_iota(jnp.int32, (span, span), 1) // length
    )
    first = lane_mask((span, 128))
    mixers = []
    for h in range(H):
        tall = jnp.concatenate([wide[h * length : (h + 1) * length]] * CHUNK_ROWS, axis=0)
        mixers.append(jnp.where(diagonal, tall, jnp.zeros_like(tall)))
    weight = bundle_ref[pl.ds(width, width), :]

    def step(c, carry):
        pltpu.make_async_copy(values_refs[0].at[0], held.at[c], value_sem.at[c]).wait()
        values = held[c]
        parts = []
        for pair in range(PAIRS):
            lanes = values[:, pair * 128 : pair * 128 + 128]
            low = jnp.dot(mixers[2 * pair], lanes, preferred_element_type=jnp.float32)
            high = jnp.dot(mixers[2 * pair + 1], lanes, preferred_element_type=jnp.float32)
            parts.append(jnp.where(first, low, high).astype(jnp.bfloat16))
        attended = jnp.concatenate(parts, axis=1)
        mixed = jnp.dot(attended, weight, preferred_element_type=jnp.float32)
        pltpu.make_async_copy(
            rows_refs[0].at[pl.ds(0, span), :], landed.at[c], row_sem.at[c]
        ).wait()
        mixed = mixed + landed[c].astype(jnp.float32)
        held[c] = (mixed * jnp.concatenate([mask[c]] * (width // 128), axis=1)).astype(
            jnp.bfloat16
        )
        leaving(c).start()
        return carry

    lax.fori_loop(0, chunks, step, 0)
    for c in range(chunks):
        leaving(c).wait()


def finish(attention, bundled, rows, values):
    vmem = pl.BlockSpec(memory_space=pltpu.VMEM)
    hbm = pl.BlockSpec(memory_space=pltpu.HBM)
    anywhere = pl.BlockSpec(memory_space=pl.ANY)
    tokens, width = rows[0].shape
    each, span, _ = values[0].shape
    shape = (each * PARTS, span, width)
    return pl.pallas_call(
        finish_kernel,
        out_shape=jax.ShapeDtypeStruct((tokens * PARTS, width), jnp.bfloat16),
        in_specs=[vmem, vmem] + [hbm] * PARTS + [anywhere] * PARTS,
        out_specs=hbm,
        scratch_shapes=[
            pltpu.VMEM(shape, jnp.bfloat16),
            pltpu.VMEM(shape, jnp.bfloat16),
            pltpu.VMEM((each * PARTS, span, 128), jnp.float32),
            pltpu.SemaphoreType.DMA((each * PARTS,)),
            pltpu.SemaphoreType.DMA((each * PARTS,)),
            pltpu.SemaphoreType.DMA((each * PARTS,)),
        ],
        compiler_params=pltpu.CompilerParams(vmem_limit_bytes=40 << 20),
        name="finish",
        interpret=INTERPRET,
    )(attention, bundled, *rows, *values)


def shifted(value, axis, steps, wrap):
    count = lax.axis_size(axis)
    if wrap:
        route = [(i, (i + steps) % count) for i in range(count)]
    else:
        route = [(i, i + steps) for i in range(count) if 0 <= i + steps < count]
    return lax.ppermute(value, axis, route)


ROUTE = ((11, 9, 6, 4), (10, 5), 12)
Z_STAY = 8
RING_Z = 8
RING_X = 4


def plan_kernel(
    position_ref, groups_ref, targets_ref, partner_ref, table_ref, meta_ref, pick_ref
):
    peers, row_count = targets_ref.shape
    pair_count = row_count // 2
    position = position_ref[0]
    shape = (peers, 128)
    down = lax.broadcasted_iota(jnp.int32, shape, 0)
    across = lax.broadcasted_iota(jnp.int32, shape, 1)
    zero = jnp.zeros(shape, jnp.int32)

    def over_lanes(value):
        return jnp.broadcast_to(jnp.sum(value, axis=1, keepdims=True), shape)

    def over_rows(value):
        return jnp.broadcast_to(jnp.sum(value, axis=0, keepdims=True), shape)

    def top_rows(value):
        return jnp.max(value, axis=0, keepdims=True)

    def flag(condition):
        return jnp.where(condition, 1, zero)

    def to_lanes(value):
        return over_rows(jnp.where(down == across, value, zero))

    def to_rows(value):
        return over_lanes(jnp.where(down == across, value, zero))

    targets = jnp.concatenate(
        [targets_ref[...], jnp.full((peers, 128 - row_count), -1, jnp.int32)], axis=1
    )
    device = targets >> 5
    offset = jnp.where(targets >= 0, (device - down) & (peers - 1), -1)
    seen = zero
    for i in range(row_count):
        seen = seen | flag(jnp.broadcast_to(offset[:, i : i + 1], shape) == across)
    present_l = flag(over_rows(seen) > 0)
    present = to_rows(present_l)
    odd = down & 1
    odd_l = across & 1

    def turns(core):
        step = ((down + odd * (1 - 2 * core)) >> 1) & 31
        step_l = ((across + odd_l * (1 - 2 * core)) >> 1) & 31
        u, u_l = step & 7, step_l & 7
        order = u * 64 + down
        order_l = u_l * 64 + across
        moving = present * flag(u > 0)
        moving_l = present_l * flag(u_l > 0)
        rank = over_lanes(moving_l * flag(order_l < order))
        rest = over_lanes((present_l - moving_l) * flag(order_l < order))
        return step >> 3, u, moving, rank, rest

    def split_of(core):
        caps = ROUTE[0]
        _, u, moving, rank, _ = turns(core)
        early = moving * flag(rank < across)
        late = moving - early
        good = flag(across <= pair_count)
        for h in range(1, 6):
            cap = caps[h - 1] if h <= len(caps) else 0
            good = good * flag(over_rows(early * flag(u >= h)) <= cap)
            good = good * flag(over_rows(late * flag(RING_Z - u >= h)) <= cap)
        split = jnp.min(jnp.where(good > 0, across, 127), axis=1, keepdims=True)
        return jnp.broadcast_to(split, shape)

    def z_lanes(core, split):
        (z1, z2, z3, z4) = ROUTE[0]
        _, u, moving, rank, rest = turns(core)
        plus = moving * flag(rank < split)
        staying = present - moving
        hops = jnp.where(plus > 0, u, RING_Z - u)
        place = jnp.where(plus > 0, split - 1 - rank, rank - split)
        base = jnp.where(
            hops == 1, 0, jnp.where(hops == 2, z1, jnp.where(hops == 3, z1 + z2, z1 + z2 + z3))
        )
        side = moving - plus
        z_all = z1 + z2 + z3 + z4
        z_leave = jnp.where(staying > 0, 2 * z1 + rest, side * z1 + place)
        z_land = jnp.where(staying > 0, 2 * z_all + rest, side * z_all + base + place)
        return jnp.where(present > 0, z_leave, -1), jnp.where(present > 0, z_land, -1)

    def x_counts(core, line):
        high, u, _, _, _ = turns(core)
        turn = (high + flag(line < u)) & (RING_X - 1)
        turn = jnp.where(present > 0, turn, -1)
        count = [over_rows(flag(turn == v)) for v in range(RING_X)]
        x2 = ROUTE[1][1]
        ahead = (count[2] + count[3] - count[1] + 1) >> 1
        ahead = jnp.minimum(
            jnp.maximum(ahead, jnp.maximum(count[2] - x2, 0)), jnp.minimum(count[2], x2)
        )
        return turn, count, ahead

    def fits(core):
        x1, x2 = ROUTE[1]
        _, count, ahead = x_counts(core, across)
        behind = count[2] - ahead
        good = (
            flag(ahead <= x2)
            * flag(behind <= x2)
            * flag(ahead + count[1] <= x1)
            * flag(behind + count[3] <= x1)
            * flag(count[0] <= ROUTE[2])
        )
        return jnp.min(jnp.where(across < RING_Z, good, 1))

    def x_lanes(core, line):
        x1, x2 = ROUTE[1]
        turn, count, ahead = x_counts(core, line)
        turn_l = to_lanes(turn)
        level = over_lanes(present_l * flag(turn_l == turn) * flag(across < down))
        double = flag(turn == 2)
        near = double * flag(level < ahead)
        forward = flag(turn == 1) + near
        spot = jnp.where(
            double > 0,
            level - jnp.where(near > 0, 0, ahead),
            level + jnp.where(turn == 1, ahead, count[2] - ahead),
        )
        side = 1 - forward
        x_leave = jnp.where(turn == 0, 2 * x1 + level, side * x1 + spot)
        x_land = jnp.where(
            turn == 0, 2 * (x1 + x2) + level, side * (x1 + x2) + double * x1 + spot
        )
        return jnp.where(present > 0, x_leave, -1), jnp.where(present > 0, x_land, -1)

    core = position & 1
    split = split_of(core)
    z_leave, z_land = z_lanes(core, split)
    line = (position >> 1) & (RING_Z - 1)
    x_leave_a, x_land_a = x_lanes(core, line)
    x_leave_b, x_land_b = x_lanes(core, RING_Z - 1 - line)
    other_split = split_of(1 - core)
    good = jnp.where(
        jnp.max(jnp.maximum(split, other_split)) <= pair_count, fits(core) * fits(1 - core), 0
    )

    lane_row = lax.broadcasted_iota(jnp.int32, (1, 128), 1)
    origin = -1 + zero
    for b in range(2):
        sender = position if b == 0 else position ^ 1
        mine = targets_ref[pl.ds(sender, 1), :]
        mine = jnp.concatenate([mine, jnp.full((1, 128 - row_count), -1, jnp.int32)], axis=1)
        away = ((mine >> 5) - sender) & (peers - 1)
        away = jnp.where(mine >= 0, away, -1)
        away = jnp.where((away & 1) == b, away, -1)
        hit = jnp.broadcast_to(away, shape) == down
        code = b * pair_count + (jnp.broadcast_to(lane_row, shape) >> 1)
        found = jnp.max(jnp.where(hit, code, -1), axis=1, keepdims=True)
        origin = jnp.maximum(origin, jnp.broadcast_to(found, shape))

    def gathered(slot_of, value):
        return top_rows(jnp.where(slot_of == across, value, -1))

    local = targets - position * row_count
    here = jnp.logical_and(local >= 0, local < row_count)
    settled_a = jnp.full((1, 128), -1, jnp.int32)
    settled_b = settled_a
    lane_full = across & 1
    for r in range(2):
        slot = jnp.max(
            jnp.where(jnp.logical_and(here, lane_full == r), local, -1), axis=1, keepdims=True
        )
        slot = jnp.broadcast_to(slot, shape)
        slot_l = over_rows(jnp.where(down == across, slot + 1, zero)) - 1
        match = across == ((position - down) & (peers - 1))
        slot_by_offset = over_lanes(jnp.where(match, slot_l + 1, zero)) - 1
        settled_a = jnp.maximum(settled_a, gathered(slot_by_offset, x_land_a * 2 + r))
        settled_b = jnp.maximum(settled_b, gathered(slot_by_offset, z_land * 2 + r))
    empty = jnp.full((1, 128), -1, jnp.int32)
    table_ref[...] = jnp.concatenate(
        [
            gathered(z_leave, origin),
            gathered(x_leave_b, origin),
            gathered(x_leave_a, z_land),
            gathered(z_leave, x_land_b),
            settled_a,
            settled_b,
            empty,
            empty,
        ],
        axis=0,
    )
    groups = groups_ref[...]
    lane = lax.broadcasted_iota(jnp.int32, groups.shape, 1)
    own_group = jnp.sum(jnp.where(lane == position, groups, 0))
    low = jnp.sum(jnp.where(groups < own_group, 1, 0))
    high = low + jnp.sum(jnp.where(groups == own_group, 1, 0))
    inside = jnp.logical_and(targets >= low * row_count, targets < high * row_count)
    meta_ref[0] = position
    meta_ref[1] = low
    meta_ref[2] = high
    meta_ref[3] = jnp.sum(jnp.where(inside, 1, 0))
    pick_ref[0] = good


def plan(position, groups, targets, partner):
    vmem = pl.BlockSpec(memory_space=pltpu.VMEM)
    smem = pl.BlockSpec(memory_space=pltpu.SMEM)
    return pl.pallas_call(
        plan_kernel,
        out_shape=(
            jax.ShapeDtypeStruct((8, 128), jnp.int32),
            jax.ShapeDtypeStruct((4,), jnp.int32),
            jax.ShapeDtypeStruct((1,), jnp.int32),
        ),
        in_specs=[smem, vmem, vmem, pl.BlockSpec(memory_space=pltpu.HBM)],
        out_specs=(vmem, smem, smem),
        name="plan",
        interpret=INTERPRET,
    )(position.reshape(1), groups, targets, partner)


def pieces(value):
    parts = []
    for _ in range(3):
        part = value.astype(jnp.bfloat16)
        parts.append(part.astype(jnp.float32))
        value = value - parts[-1]
    return parts


def bundle_kernel(weight_ref, out_weight_ref, gain_ref, bias_ref, out_ref, held, sem):
    width = held.shape[1]
    loads = [
        pltpu.make_async_copy(
            weight_ref.at[:, pl.ds(2 * width, width)], held.at[pl.ds(0, width), :], sem.at[0]
        ),
        pltpu.make_async_copy(out_weight_ref, held.at[pl.ds(width, width), :], sem.at[1]),
    ]
    for load in loads:
        load.start()
    rows = pieces(gain_ref[...]) + pieces(bias_ref[...])
    rows.append(jnp.zeros((16 - len(rows), width), jnp.float32))
    held[pl.ds(2 * width, 16), :] = jnp.concatenate(rows, axis=0).astype(jnp.bfloat16)
    for load in loads:
        load.wait()
    store = pltpu.make_async_copy(held, out_ref, sem.at[2])
    store.start()
    store.wait()


def bundle(weight, out_weight, gain, bias):
    width = weight.shape[0]
    vmem = pl.BlockSpec(memory_space=pltpu.VMEM)
    hbm = pl.BlockSpec(memory_space=pltpu.HBM)
    shape = (2 * width + 16, width)
    return pl.pallas_call(
        bundle_kernel,
        out_shape=jax.ShapeDtypeStruct(shape, weight.dtype),
        in_specs=[hbm, hbm, vmem, vmem],
        out_specs=hbm,
        scratch_shapes=[pltpu.VMEM(shape, weight.dtype), pltpu.SemaphoreType.DMA((3,))],
        name="bundle",
        interpret=INTERPRET,
    )(weight, out_weight, gain, bias)


def deal(table_ref, row, pool, outs):
    lane = 0
    for out in outs:

        def step(k, carry, out=out, lane=lane):
            out[k] = pool[jnp.maximum(table_ref[row, lane + k], 0)]
            return carry

        lax.fori_loop(0, out.shape[0], step, 0)
        lane += out.shape[0]


def leave_kernel(part, table_ref, own_ref, partner_ref, *refs):
    outs, (pool, sem) = refs[:-2], refs[-2:]
    pairs = own_ref.shape[0]
    half = own_ref.shape[2] // 2
    copies = [
        pltpu.make_async_copy(
            ref.at[:, :, pl.ds(part * half, half), :],
            pool.at[pl.ds(b * pairs, pairs)],
            sem.at[b],
        )
        for b, ref in enumerate((own_ref, partner_ref))
    ]
    for copy in copies:
        copy.start()
    for copy in copies:
        copy.wait()
    deal(table_ref, part, pool, outs)


def leave(part, table, own, partner, sizes):
    pairs, two, length, width = own.shape
    vmem = pl.BlockSpec(memory_space=pltpu.VMEM)
    anywhere = pl.BlockSpec(memory_space=pl.ANY)
    return pl.pallas_call(
        functools.partial(leave_kernel, part),
        out_shape=tuple(
            jax.ShapeDtypeStruct((n, two, length // 2, width), own.dtype) for n in sizes
        ),
        in_specs=[pl.BlockSpec(memory_space=pltpu.SMEM), anywhere, anywhere],
        out_specs=(vmem,) * len(sizes),
        scratch_shapes=[
            pltpu.VMEM((2 * pairs, two, length // 2, width), own.dtype),
            pltpu.SemaphoreType.DMA((2,)),
        ],
        compiler_params=pltpu.CompilerParams(vmem_limit_bytes=40 << 20),
        name="leave",
        interpret=INTERPRET,
    )(table, own, partner)


def pooled(refs, pool, sem):
    copies = []
    start = 0
    for ref in refs:
        count = ref.shape[0]
        copies.append(
            pltpu.make_async_copy(ref, pool.at[pl.ds(start, count)], sem.at[len(copies)])
        )
        start += count
    return copies


def turn_kernel(row, count, table_ref, *refs):
    sources, outs, (pool, sem) = refs[:count], refs[count:-2], refs[-2:]
    copies = pooled(sources, pool, sem)
    for copy in copies:
        copy.start()
    for copy in copies:
        copy.wait()
    deal(table_ref, row, pool, outs)


def turn_over(table, row, sources, sizes):
    vmem = pl.BlockSpec(memory_space=pltpu.VMEM)
    anywhere = pl.BlockSpec(memory_space=pl.ANY)
    payload = sources[0].shape[1:]
    return pl.pallas_call(
        functools.partial(turn_kernel, row, len(sources)),
        out_shape=tuple(jax.ShapeDtypeStruct((n,) + payload, sources[0].dtype) for n in sizes),
        in_specs=[pl.BlockSpec(memory_space=pltpu.SMEM)] + [anywhere] * len(sources),
        out_specs=(vmem,) * len(sizes),
        scratch_shapes=[
            pltpu.VMEM((sum(s.shape[0] for s in sources),) + payload, sources[0].dtype),
            pltpu.SemaphoreType.DMA((len(sources),)),
        ],
        compiler_params=pltpu.CompilerParams(vmem_limit_bytes=40 << 20),
        name="turn_over",
        interpret=INTERPRET,
    )(table, *sources)


def land_kernel(count_a, count_b, table_ref, *refs):
    sources_a, sources_b = refs[:count_a], refs[count_a : count_a + count_b]
    outs = refs[count_a + count_b : count_a + count_b + PARTS]
    live_ref, pool_a, pool_b, done, sem_a, sem_b, out_sem = refs[count_a + count_b + PARTS :]
    row_count, length, _ = done.shape
    half = length // 2
    copies = pooled(sources_a, pool_a, sem_a) + pooled(sources_b, pool_b, sem_b)
    for copy in copies:
        copy.start()
    for copy in copies:
        copy.wait()

    def step(m, carry):
        live = table_ref[4, m] >= 0
        live_ref[m] = jnp.where(live, 1, 0)
        for part, pool in ((0, pool_a), (1, pool_b)):
            code = jnp.maximum(table_ref[4 + part, m], 0)
            value = pool[code >> 1, code & 1]
            done[m, pl.ds(part * half, half), :] = jnp.where(live, value, jnp.zeros_like(value))
        return carry

    rows = row_count // PARTS
    leaving = [
        pltpu.make_async_copy(done.at[pl.ds(k * rows, rows)], out, out_sem.at[k])
        for k, out in enumerate(outs)
    ]
    for k in range(PARTS):
        lax.fori_loop(k * rows, (k + 1) * rows, step, 0)
        leaving[k].start()
    for copy in leaving:
        copy.wait()


def land(table, sources_a, sources_b, row_count, length):
    anywhere = pl.BlockSpec(memory_space=pl.ANY)
    smem = pl.BlockSpec(memory_space=pltpu.SMEM)
    two, half, width = sources_a[0].shape[1:]
    dtype = sources_a[0].dtype
    return pl.pallas_call(
        functools.partial(land_kernel, len(sources_a), len(sources_b)),
        out_shape=(jax.ShapeDtypeStruct((row_count // PARTS, length, width), dtype),) * PARTS
        + (jax.ShapeDtypeStruct((row_count,), jnp.int32),),
        in_specs=[smem] + [anywhere] * (len(sources_a) + len(sources_b)),
        out_specs=(pl.BlockSpec(memory_space=pltpu.HBM),) * PARTS + (smem,),
        scratch_shapes=[
            pltpu.VMEM((sum(s.shape[0] for s in sources_a), two, half, width), dtype),
            pltpu.VMEM((sum(s.shape[0] for s in sources_b), two, half, width), dtype),
            pltpu.VMEM((row_count, length, width), dtype),
            pltpu.SemaphoreType.DMA((len(sources_a),)),
            pltpu.SemaphoreType.DMA((len(sources_b),)),
            pltpu.SemaphoreType.DMA((PARTS,)),
        ],
        compiler_params=pltpu.CompilerParams(vmem_limit_bytes=40 << 20),
        name="land",
        interpret=INTERPRET,
    )(table, *sources_a, *sources_b)


def chain(forward, backward, caps, step, ring):
    def moved(i, by):
        return (i // (step * ring)) * step * ring + (i + by * step) % (step * ring)

    devices = range(lax.axis_size("depth"))
    onward, returning = [], []
    for cap in caps:
        forward = lax.ppermute(forward[:cap], "depth", [(i, moved(i, 1)) for i in devices])
        backward = lax.ppermute(backward[:cap], "depth", [(i, moved(i, -1)) for i in devices])
        onward.append(forward)
        returning.append(backward)
    return onward + returning


def routed(route, table, own, partner):
    z_caps, x_caps, x_stay = route
    z_sizes = (z_caps[0], z_caps[0], Z_STAY)
    x_sizes = (x_caps[0], x_caps[0], x_stay)
    z_plus, z_minus, z_still = leave(0, table, own, partner, z_sizes)
    x_plus, x_minus, x_still = leave(1, table, own, partner, x_sizes)
    along_x = chain(x_plus, x_minus, x_caps, 2 * RING_Z, RING_X)
    along_z = chain(z_plus, z_minus, z_caps, 2, RING_Z)
    later = turn_over(table, 3, along_x + [x_still], z_sizes)
    last_b = chain(later[0], later[1], z_caps, 2, RING_Z)
    turned = turn_over(table, 2, along_z + [z_still], x_sizes)
    last_a = chain(turned[0], turned[1], x_caps, 2 * RING_Z, RING_X)
    return land(
        table,
        last_a + [turned[2]],
        last_b + [later[2]],
        own.shape[0] * own.shape[1],
        own.shape[2],
    )


def dense(targets, everywhere, own):
    row_count = targets.shape[0]
    _, _, length, width = own.shape
    peers = lax.axis_size("depth")
    position = lax.axis_index("depth")
    capacity = max(2, (row_count + peers - 1) // peers)
    slots = jnp.where(
        targets >= 0,
        targets // row_count * capacity + jnp.arange(row_count) % capacity,
        -1,
    )
    outgoing = spread(own.reshape(row_count, length, width), slots, peers * capacity)
    got = lax.all_to_all(
        outgoing.reshape((peers, capacity, length, width)),
        "depth",
        split_axis=0,
        concat_axis=0,
        tiled=True,
    ).reshape(peers * capacity, length, width)
    local = everywhere - position * row_count
    mine = jnp.logical_and(local >= 0, local < row_count)
    code = (
        lax.broadcasted_iota(jnp.int32, (peers, row_count), 0) * capacity
        + lax.broadcasted_iota(jnp.int32, (peers, row_count), 1) % capacity
    )
    wanted = jnp.where(mine, local, -1).reshape(1, -1)
    hit = jnp.arange(row_count)[:, None] == wanted
    source = jnp.max(jnp.where(hit, code.reshape(1, -1), -1), axis=1)
    return (*settle(source, got), (source >= 0).astype(jnp.int32))


def layer(
    alignment_input,
    target_slot,
    device_alignment,
    layer_norm_gain,
    layer_norm_bias,
    query_key_value_weight,
    output_weight,
):
    targets = target_slot[0]
    row_count, length, width = alignment_input.shape[1:]
    peers = lax.axis_size("depth")
    position = lax.axis_index("depth")
    own = alignment_input.reshape(row_count // 2, 2, length, width)
    everywhere = lax.all_to_all(
        jnp.broadcast_to(targets[None, None], (peers, 1, row_count)),
        "depth",
        split_axis=0,
        concat_axis=0,
        tiled=True,
    ).reshape(peers, row_count)
    partner = lax.ppermute(own, "depth", [(i, i ^ 1) for i in range(peers)])
    bundled = bundle(query_key_value_weight[0], output_weight[0], layer_norm_gain, layer_norm_bias)
    bundled = shifted(bundled, "section", 1, True)
    table, meta, pick = plan(position, device_alignment, everywhere, partner)
    *settled, live = lax.switch(
        pick[0],
        [
            lambda t, o, p, a, b: dense(a, b, o),
            lambda t, o, p, a, b: routed(ROUTE, t, o, p),
        ],
        table,
        own,
        partner,
        targets,
        everywhere,
    )
    balanced = [part.reshape(-1, width) for part in settled]
    earlier = [shifted(part, "section", 1, True) for part in balanced]
    tied, tied_low = front(
        live, balanced, layer_norm_gain, layer_norm_bias, query_key_value_weight[0]
    )
    tied, up, down = join(
        meta, tied, shifted(tied_low, "depth", 1, False), shifted(tied_low, "depth", -1, False)
    )
    neighbours = [shifted(up, "depth", 2, False), shifted(down, "depth", -2, False)]
    attention = middle(live, meta, tied, neighbours)
    attention = shifted(attention, "section", 1, True)
    values = []
    for rows in earlier:
        values.append(values_of(rows, bundled, row_count))
    handed = finish(attention, bundled, earlier, values)
    return handed.reshape(1, row_count, length, width)


def solution(mesh):
    placed = (
        P("section", "depth", None, None),
        P("section", "depth"),
        P("section", None),
        P("section", None),
        P("section", None),
        P("section", None, None),
        P("section", None, None),
    )
    return jax.shard_map(
        layer,
        mesh=mesh,
        in_specs=placed,
        out_specs=P("section", "depth", None, None),
        check_vma=False,
    )
```
